256 devices in a mesh: ctx: 32 (over z, y), tp: 8 (over x, core).
Axes of the slice: x: 4, y: 4, z: 8, core: 2. Of those that a mesh axis runs over, the one named last changes fastest.
Arguments:
- queries: bfloat16 [4096, 5120], P('ctx', 'tp'), may hold values from -40 to 40
- keys: bfloat16 [4096, 1024], P('ctx', 'tp'), may hold values from -40 to 40
- values: bfloat16 [4096, 1024], P('ctx', 'tp'), may hold values from -6 to 6
- out_grad: bfloat16 [4096, 5120], P('ctx', 'tp'), may hold values from -6 to 6
- ancestry: int32 [32, 17], replicated, may hold values from 0 to 31, as said below
- w_query: bfloat16 [5120, 5120], P(None, 'tp'), may hold values from -0.078125 to 0.078125
- key_matrix: bfloat16 [5120, 1024], P(None, 'tp'), may hold values from -0.078125 to 0.078125
- value_matrix: bfloat16 [5120, 1024], P(None, 'tp'), may hold values from -0.078125 to 0.078125
Outputs:
- input_grad: bfloat16 [4096, 5120], P('ctx', 'tp')
The draws below stay inside these ranges and needn't reach their ends.
Inputs may be any that keep to these rules, and one draw needn't show every extreme that they name: `ancestry`: row b holds b, then its ancestors in order parent, grandparent and so on (each an earlier block), then b again to fill the row. Blocks 0 to 16 form one chain, each the parent of the next; no block has more than 16 ancestors; every block descends from blocks 0 to 3 or is one of them.
All inputs are finite; a program needn't handle non-finite values.
Results may differ from the reference program's by a relative error of at most 0.024.
Values may be sent and summed in bfloat16 or wider, within the bound.
No kernel may reach another device: no remote copies, remote signals or barrier semaphores. Data moves between devices by JAX's collectives and lax.ppermute only.
A program may use at most 128 MiB of HBM per device.

```python
import math
import jax
import jax.numpy as jnp
from jax import lax

MODEL_WIDTH = 5120
QUERY_HEADS = 40
KEY_VALUE_HEADS = 8
HEAD_SIZE = 128
TREE_BLOCK_SIZE = 128
PACK_TOKENS = 4096
PACK_BLOCKS = 32
PROMPT_BLK = 4
DEPTH = 16
ANC = 17


def draw_keys(key, part):
    random_jitter = jax.random.truncated_normal(jax.random.fold_in(key, 1), -4.0, 4.0, (PACK_TOKENS, KEY_VALUE_HEADS * HEAD_SIZE), jnp.float32)
    return random_jitter.astype(jnp.bfloat16)


def draw_queries(key, part):
    random_jitter = jax.random.truncated_normal(jax.random.fold_in(key, 3), -4.0, 4.0, (PACK_TOKENS, QUERY_HEADS * HEAD_SIZE), jnp.float32)
    return random_jitter.astype(jnp.bfloat16)


def draw_ancestry(key, part):
    base_key = jax.random.fold_in(key, 99)
    coin_key, pick_key = jax.random.split(base_key)
    coin_flips = jax.random.randint(coin_key, (PACK_BLOCKS,), 0, 2)
    pick_draws = jax.random.randint(pick_key, (PACK_BLOCKS,), 0, 1 << 20)
    lowest = PROMPT_BLK - 1

    def place(carry, block_id):
        depths, parents = carry
        previous = jnp.maximum(block_id - 1, 0)
        spread = jnp.maximum(block_id - lowest, 1)
        candidate = lowest + pick_draws[block_id] % spread
        candidate = jnp.where(depths[candidate] < DEPTH, candidate, lowest)
        extend = (coin_flips[block_id] == 1) & (depths[previous] < DEPTH)
        fallback = jnp.where(extend, previous, candidate)
        parent = jnp.where(block_id <= DEPTH, previous, fallback)
        block_depth = jnp.where(block_id == 0, 0, depths[parent] + 1)
        return ((depths.at[block_id].set(block_depth), parents.at[block_id].set(parent)), 0)
    start_carry = (jnp.zeros((PACK_BLOCKS,), jnp.int32), jnp.zeros((PACK_BLOCKS,), jnp.int32))
    (depths, parents), unused = lax.scan(place, start_carry, jnp.arange(PACK_BLOCKS, dtype=jnp.int32))
    own_ids = jnp.arange(PACK_BLOCKS, dtype=jnp.int32)
    walker = own_ids
    columns = [own_ids]
    for step_id in range(1, ANC):
        walker = parents[walker]
        columns.append(jnp.where(step_id <= depths, walker, own_ids))
    return jnp.stack(columns, axis=1)


def steps_of(key, dims, shards, low, largest):
    gain = 1.0
    for dim, shards_of in shards:
        draws = jax.random.uniform(jax.random.fold_in(jax.random.fold_in(key, 6), dim), (shards_of,), jnp.float32, low / len(shards), largest / len(shards))
        gain = gain * jnp.repeat(jnp.exp(draws), dims[dim] // shards_of).reshape((-1,) + (1,) * (len(dims) - 1 - dim))
    return gain


def scatter_about(stream_key, dims, scale, bound, cuts=(), kind=jnp.bfloat16):
    loudness = steps_of(stream_key, dims, cuts, -0.22, 0.18) if cuts else 1.0
    entries = jax.random.normal(stream_key, dims, jnp.float32) * scale * loudness
    return jnp.minimum(jnp.maximum(entries, -bound), bound).astype(kind)


def setup_inputs(seed: int = 0) -> dict:
    arg_keys = jax.random.split(jax.random.key(seed), 9)
    return {
        "queries": draw_queries(jax.random.fold_in(arg_keys[8], 71), 0),
        "keys": draw_keys(jax.random.fold_in(arg_keys[8], 71), 0),
        "values": scatter_about(arg_keys[2], (PACK_TOKENS, KEY_VALUE_HEADS * HEAD_SIZE), 1.0, 6.0, ((0, 32), (1, 8))),
        "out_grad": scatter_about(arg_keys[3], (PACK_TOKENS, QUERY_HEADS * HEAD_SIZE), 1.0, 6.0, ((0, 32), (1, 8))),
        "ancestry": draw_ancestry(jax.random.fold_in(arg_keys[8], 71), 0),
        "w_query": scatter_about(arg_keys[5], (MODEL_WIDTH, QUERY_HEADS * HEAD_SIZE), MODEL_WIDTH ** -0.5, 0.078125, ((1, 8),)),
        "key_matrix": scatter_about(arg_keys[6], (MODEL_WIDTH, KEY_VALUE_HEADS * HEAD_SIZE), MODEL_WIDTH ** -0.5, 0.078125, ((1, 8),)),
        "value_matrix": scatter_about(arg_keys[7], (MODEL_WIDTH, KEY_VALUE_HEADS * HEAD_SIZE), MODEL_WIDTH ** -0.5, 0.078125, ((1, 8),)),
    }


ROPE_BASE = 1000000.0
MASKED = -1.0e30


def inverse_rotary(grads, token_places):
    half_width = grads.shape[-1] // 2
    frequencies = jnp.exp(jnp.arange(half_width, dtype=jnp.float32) * (-2.0 * math.log(ROPE_BASE) / grads.shape[-1]))
    angles = token_places[:, None] * frequencies[None, :]
    cosine = jnp.cos(angles)[:, None, :]
    sine_part = jnp.sin(angles)[:, None, :]
    front_half = grads[..., :half_width]
    second = grads[..., half_width:]
    return jnp.concatenate([front_half * cosine + second * sine_part, second * cosine - front_half * sine_part], axis=-1)


def reference(queries, keys, values, out_grad, ancestry, w_query, key_matrix, value_matrix):
    heads_per_group = QUERY_HEADS // KEY_VALUE_HEADS
    factor = HEAD_SIZE ** -0.5
    every_block = jnp.arange(PACK_BLOCKS, dtype=jnp.int32)
    depths = jnp.sum((ancestry != every_block[:, None]).astype(jnp.int32), axis=1)
    token_ids = jnp.arange(PACK_TOKENS, dtype=jnp.int32)
    token_block = token_ids // TREE_BLOCK_SIZE
    listed = jnp.any(ancestry[:, :, None] == every_block[None, None, :], axis=1)
    visible = listed[token_block][:, token_block] & ((token_block[:, None] != token_block[None, :]) | (token_ids[None, :] <= token_ids[:, None]))
    token_places = (TREE_BLOCK_SIZE * depths[token_block] + token_ids % TREE_BLOCK_SIZE).astype(jnp.float32)
    query_heads = queries.reshape(PACK_TOKENS, QUERY_HEADS, HEAD_SIZE).transpose(1, 0, 2)
    grad_heads = out_grad.reshape(PACK_TOKENS, QUERY_HEADS, HEAD_SIZE).transpose(1, 0, 2)
    heads_of_key = keys.reshape(PACK_TOKENS, KEY_VALUE_HEADS, HEAD_SIZE).transpose(1, 0, 2)
    heads_of_value = values.reshape(PACK_TOKENS, KEY_VALUE_HEADS, HEAD_SIZE).transpose(1, 0, 2)

    def one_head(inputs):
        query_h, grad_h, kv_index = inputs
        key_h = heads_of_key[kv_index]
        value_h = heads_of_value[kv_index]
        scores = jnp.dot(query_h, key_h.T, preferred_element_type=jnp.float32) * factor
        scores = jnp.where(visible, scores, MASKED)
        maxima = jnp.max(scores, axis=1)
        weights = jnp.where(visible, jnp.exp(scores - maxima[:, None]), 0.0)
        totals = jnp.sum(weights, axis=1)
        attended = (jnp.dot(weights.astype(jnp.bfloat16), value_h, preferred_element_type=jnp.float32) / totals[:, None]).astype(jnp.bfloat16)
        log_totals = maxima + jnp.log(totals)
        row_dots = jnp.sum(grad_h.astype(jnp.float32) * attended.astype(jnp.float32), axis=1)
        probs = jnp.where(visible, jnp.exp(scores - log_totals[:, None]), 0.0)
        prob_grads = jnp.dot(grad_h, value_h.T, preferred_element_type=jnp.float32)
        score_grads = (probs * (prob_grads - row_dots[:, None])).astype(jnp.bfloat16)
        query_grad = jnp.dot(score_grads, key_h, preferred_element_type=jnp.float32) * factor
        key_grad = jnp.dot(score_grads.T, query_h, preferred_element_type=jnp.float32) * factor
        value_grad = jnp.dot(probs.astype(jnp.bfloat16).T, grad_h, preferred_element_type=jnp.float32)
        return query_grad, key_grad, value_grad

    kv_of_head = jnp.arange(QUERY_HEADS, dtype=jnp.int32) // heads_per_group
    query_grads, gradient_keys, gradient_values = lax.map(one_head, (query_heads, grad_heads, kv_of_head))
    query_low = inverse_rotary(query_grads.transpose(1, 0, 2), token_places).astype(jnp.bfloat16).reshape(PACK_TOKENS, QUERY_HEADS * HEAD_SIZE)
    summed_key = gradient_keys.reshape(KEY_VALUE_HEADS, heads_per_group, PACK_TOKENS, HEAD_SIZE).sum(axis=1).transpose(1, 0, 2)
    summed_value = gradient_values.reshape(KEY_VALUE_HEADS, heads_per_group, PACK_TOKENS, HEAD_SIZE).sum(axis=1).transpose(1, 0, 2)
    key_reduced = inverse_rotary(summed_key, token_places).astype(jnp.bfloat16).reshape(PACK_TOKENS, KEY_VALUE_HEADS * HEAD_SIZE)
    value_reduced = summed_value.astype(jnp.bfloat16).reshape(PACK_TOKENS, KEY_VALUE_HEADS * HEAD_SIZE)
    summed = jnp.dot(query_low, w_query.T, preferred_element_type=jnp.float32)
    summed = summed + jnp.dot(key_reduced, key_matrix.T, preferred_element_type=jnp.float32)
    summed = summed + jnp.dot(value_reduced, value_matrix.T, preferred_element_type=jnp.float32)
    return summed.astype(jnp.bfloat16)
```

```python
import math

import jax
import jax.numpy as jnp
from jax import lax
from jax.experimental import pallas as pl
from jax.experimental.pallas import tpu as pltpu
from jax.sharding import Mesh, PartitionSpec as P

HEAD = 128
BLOCK = 128
GROUP = 5
ROWS = GROUP * BLOCK
NZ, NY, NX, NC = 8, 4, 4, 2
ANC = 17
ROPE_BASE = 1000000.0
MASKED = -1e30
FACTOR = HEAD ** -0.5
NT = (((1,), (1,)), ((), ()))
NN = (((1,), (0,)), ((), ()))
VMEM_LIMIT = 48 << 20


def dot_nt(a, b):
    return lax.dot_general(a, b, NT, preferred_element_type=jnp.float32)


def dot_nn(a, b):
    return lax.dot_general(a, b, NN, preferred_element_type=jnp.float32)


def build_items(place_ref, anc_ref, list_ref, item_ref):
    z = place_ref[0]
    y = place_ref[1]
    base = jnp.int32(0)
    for j in range(NY):
        query_block = NY * z + (y - j) % NY
        bits = jnp.int32(0)
        for i in range(ANC):
            key_block = anc_ref[query_block, i]
            bits = bits | jnp.where(key_block % NY == y, jnp.int32(1) << (key_block // NY), 0)
        count = jnp.int32(0)
        for key_z in range(NZ):
            list_ref[count] = key_z
            count = count + ((bits >> key_z) & 1)
        for p in range(NZ // 2):
            first = jnp.where(2 * p < count, list_ref[2 * p], 0)
            both = 2 * p + 1 < count
            second = jnp.where(both, list_ref[2 * p + 1], first)
            item_ref[base + p, 0] = j
            item_ref[base + p, 1] = first
            item_ref[base + p, 2] = second
            if j == 0:
                item_ref[base + p, 3] = jnp.where(first == z, 1, 0)
                item_ref[base + p, 4] = jnp.where(both, jnp.where(second == z, 1, 0), 2)
            else:
                item_ref[base + p, 3] = 0
                item_ref[base + p, 4] = jnp.where(both, 0, 2)
        base = base + (count + 1) // 2
    return base


def stack_heads(groups, q_rows, g_rows):
    for j in range(NY):
        for h in range(GROUP):
            q_rows[j, h * BLOCK:(h + 1) * BLOCK, :] = groups[j][:, h * HEAD:(h + 1) * HEAD]
            g_rows[j, h * BLOCK:(h + 1) * BLOCK, :] = groups[j][:, ROWS + h * HEAD:ROWS + (h + 1) * HEAD]


def fill_bias(bias):
    key_row = lax.broadcasted_iota(jnp.int32, (BLOCK, ROWS), 0)
    query_row = lax.broadcasted_iota(jnp.int32, (BLOCK, ROWS), 1) % BLOCK
    bias[0] = jnp.zeros((BLOCK, ROWS), jnp.float32)
    bias[1] = jnp.where(key_row <= query_row, 0.0, MASKED)
    bias[2] = jnp.full((BLOCK, ROWS), MASKED, jnp.float32)


def load_item(p, item_ref, kv_ref, bias):
    j = item_ref[p, 0]
    first = item_ref[p, 1]
    second = item_ref[p, 2]
    kv = jnp.concatenate([kv_ref[first], kv_ref[second]], axis=0)
    both_bias = jnp.concatenate([bias[item_ref[p, 3]], bias[item_ref[p, 4]]], axis=0)
    return j, first, second, kv[:, :HEAD], kv[:, HEAD:], both_bias


def stats_kernel(place_ref, anc_ref, kv_ref, g0, g1, g2, g3, stat_ref, q_rows, g_rows, bias, list_ref, item_ref):
    stack_heads((g0, g1, g2, g3), q_rows, g_rows)
    fill_bias(bias)
    items = build_items(place_ref, anc_ref, list_ref, item_ref)
    for j in range(NY):
        stat_ref[j, 0:1, :] = jnp.full((1, ROWS), MASKED, jnp.float32)
        stat_ref[j, 1:4, :] = jnp.zeros((3, ROWS), jnp.float32)

    def step(p, carry):
        j, first, second, key_pair, value_pair, both_bias = load_item(p, item_ref, kv_ref, bias)
        scores = dot_nt(key_pair, q_rows[j]) * FACTOR + both_bias
        prob_grads = dot_nt(value_pair, g_rows[j])
        old = stat_ref[j, 0:1, :]
        highest = jnp.maximum(old, jnp.max(scores, axis=0, keepdims=True))
        weights = jnp.exp(scores - highest)
        shrink = jnp.exp(old - highest)
        stat_ref[j, 0:1, :] = highest
        stat_ref[j, 1:2, :] = stat_ref[j, 1:2, :] * shrink + jnp.sum(weights, axis=0, keepdims=True)
        stat_ref[j, 2:3, :] = stat_ref[j, 2:3, :] * shrink + jnp.sum(weights * prob_grads, axis=0, keepdims=True)
        return carry

    lax.fori_loop(0, items, step, 0)


def grads_kernel(place_ref, anc_ref, kv_ref, g0, g1, g2, g3, s0, s1, s2, s3,
                 dkv_ref, dq0, dq1, dq2, dq3,
                 q_rows, g_rows, bias, key_cols, rows, dk_acc, dv_acc, dq_acc, list_ref, item_ref):
    stack_heads((g0, g1, g2, g3), q_rows, g_rows)
    fill_bias(bias)
    items = build_items(place_ref, anc_ref, list_ref, item_ref)
    for a in range(NZ):
        key_cols[a] = kv_ref[a][:, :HEAD].T
    stats = (s0, s1, s2, s3)
    for j in range(NY):
        views = [stats[k][(j - k) % NY] for k in range(NY)]
        maxima = views[0][0:1]
        for k in range(1, NY):
            maxima = jnp.maximum(maxima, views[k][0:1])
        totals = jnp.zeros((1, ROWS), jnp.float32)
        dots = jnp.zeros((1, ROWS), jnp.float32)
        for k in range(NY):
            shrink = jnp.exp(views[k][0:1] - maxima)
            totals = totals + views[k][1:2] * shrink
            dots = dots + views[k][2:3] * shrink
        rows[j, 0:1, :] = maxima + jnp.log(totals)
        rows[j, 1:2, :] = dots / totals
    dk_acc[...] = jnp.zeros_like(dk_acc)
    dv_acc[...] = jnp.zeros_like(dv_acc)
    dq_acc[...] = jnp.zeros_like(dq_acc)

    def step(p, carry):
        j, first, second, key_pair, value_pair, both_bias = load_item(p, item_ref, kv_ref, bias)
        scores = dot_nt(key_pair, q_rows[j]) * FACTOR + both_bias
        prob_grads = dot_nt(value_pair, g_rows[j])
        probs = jnp.exp(scores - rows[j, 0:1, :])
        score_grads = (probs * (prob_grads - rows[j, 1:2, :])).astype(jnp.bfloat16)
        probs_low = probs.astype(jnp.bfloat16)
        dk_pair = dot_nn(score_grads, q_rows[j])
        dv_pair = dot_nn(probs_low, g_rows[j])
        dk_acc[first] += dk_pair[:BLOCK]
        dk_acc[second] += dk_pair[BLOCK:]
        dv_acc[first] += dv_pair[:BLOCK]
        dv_acc[second] += dv_pair[BLOCK:]
        cols = jnp.concatenate([key_cols[first], key_cols[second]], axis=1)
        dq_acc[j] += dot_nn(cols, score_grads)
        return carry

    lax.fori_loop(0, items, step, 0)
    for a in range(NZ):
        dkv_ref[a, :, :HEAD] = (dk_acc[a] * FACTOR).astype(jnp.bfloat16)
        dkv_ref[a, :, HEAD:] = dv_acc[a].astype(jnp.bfloat16)
    for j, out in enumerate((dq0, dq1, dq2, dq3)):
        for h in range(GROUP):
            part = dq_acc[j, :, h * BLOCK:(h + 1) * BLOCK].T * FACTOR
            out[:, h * HEAD:(h + 1) * HEAD] = part.astype(jnp.bfloat16)


def unrotate(x, cosine, sine):
    return x * cosine + pltpu.roll(x, HEAD // 2, 1) * sine


def first_half_kernel(place_ref, cos_ref, sin_ref, q0, q1, q2, q3, dkv_ref, wq, wk, wv, out_ref, low_ref):
    @pl.when(pl.program_id(0) == 0)
    def _():
        cosine = cos_ref[...]
        sine = sin_ref[...]
        for h in range(GROUP):
            cols = slice(h * HEAD, (h + 1) * HEAD)
            total = q0[:, cols].astype(jnp.float32)
            for part in (q1, q2, q3):
                total = total + part[:, cols].astype(jnp.float32)
            low_ref[:, cols] = unrotate(total, cosine, sine).astype(jnp.bfloat16)
        total = dkv_ref[0].astype(jnp.float32)
        for a in range(1, NZ):
            total = total + dkv_ref[a].astype(jnp.float32)
        low_ref[:, ROWS:ROWS + HEAD] = unrotate(total[:, :HEAD], cosine, sine).astype(jnp.bfloat16)
        low_ref[:, ROWS + HEAD:] = total[:, HEAD:].astype(jnp.bfloat16)

    out_ref[0] = project(low_ref, wq, wk, wv).astype(out_ref.dtype)


def second_half_kernel(place_ref, low_ref, wq, wk, wv, out_ref):
    out_ref[0] = project(low_ref, wq, wk, wv).astype(out_ref.dtype)


def project(low_ref, wq, wk, wv):
    total = dot_nt(low_ref[:, :ROWS], wq[...])
    total = total + dot_nt(low_ref[:, ROWS:ROWS + HEAD], wk[...])
    return total + dot_nt(low_ref[:, ROWS + HEAD:], wv[...])


def whole(shape):
    return pl.BlockSpec(shape, lambda *_: (0,) * len(shape))


def weight_specs(flip):
    def pick(i, place):
        core = 1 - place[3] if flip else place[3]
        return (2 * ((place[2] + i) % NX) + core, 0)

    return [pl.BlockSpec((ROWS, ROWS), pick), pl.BlockSpec((ROWS, HEAD), pick), pl.BlockSpec((ROWS, HEAD), pick)]


def shift(size, k):
    return [(i, (i + k) % size) for i in range(size)]


def shards(queries, keys, values, out_grad, ancestry, w_query, key_matrix, value_matrix):
    f32, bf16, i32 = jnp.float32, jnp.bfloat16, jnp.int32
    z, y, x, c = (lax.axis_index(name) for name in "zyxc")
    place = jnp.stack([z, y, x, c]).astype(i32)
    group = jnp.concatenate([queries, out_grad], axis=1)
    groups = [group] + [lax.ppermute(group, "y", shift(NY, k)) for k in range(1, NY)]
    kv = jnp.concatenate([keys, values], axis=1)
    kv_all = lax.all_to_all(jnp.broadcast_to(kv[None], (NZ,) + kv.shape), "z", 0, 0, tiled=True)

    own_block = NY * z + y
    own_row = lax.dynamic_slice_in_dim(ancestry, own_block, 1, 0)
    depth = jnp.sum((own_row != own_block).astype(i32))
    token_places = (BLOCK * depth + jnp.arange(BLOCK, dtype=i32)).astype(f32)
    frequencies = jnp.exp(jnp.arange(HEAD // 2, dtype=f32) * (-2.0 * math.log(ROPE_BASE) / HEAD))
    angles = token_places[:, None] * frequencies[None, :]
    cosine = jnp.cos(angles)
    sine = jnp.sin(angles)
    cosine = jnp.concatenate([cosine, cosine], axis=1)
    sine = jnp.concatenate([sine, -sine], axis=1)

    params = pltpu.CompilerParams(vmem_limit_bytes=VMEM_LIMIT)
    common = [
        pltpu.VMEM((NY, ROWS, HEAD), bf16),
        pltpu.VMEM((NY, ROWS, HEAD), bf16),
        pltpu.VMEM((3, BLOCK, ROWS), f32),
    ]
    lists = [pltpu.SMEM((NZ + 1,), i32), pltpu.SMEM((5 * NZ // 2, 5), i32)]
    in_shapes = [kv_all.shape] + [group.shape] * NY
    stats = pl.pallas_call(
        stats_kernel,
        out_shape=jax.ShapeDtypeStruct((NY, 4, ROWS), f32),
        grid_spec=pltpu.PrefetchScalarGridSpec(
            num_scalar_prefetch=2,
            grid=(1,),
            in_specs=[whole(s) for s in in_shapes],
            out_specs=whole((NY, 4, ROWS)),
            scratch_shapes=common + lists,
        ),
        compiler_params=params,
        name="stats",
    )(place, ancestry, kv_all, *groups)
    all_stats = [stats] + [lax.ppermute(stats, "y", shift(NY, k)) for k in range(1, NY)]
    dkv, *dq_parts = pl.pallas_call(
        grads_kernel,
        out_shape=[jax.ShapeDtypeStruct((NZ, BLOCK, 2 * HEAD), bf16)]
        + [jax.ShapeDtypeStruct((BLOCK, ROWS), bf16)] * NY,
        grid_spec=pltpu.PrefetchScalarGridSpec(
            num_scalar_prefetch=2,
            grid=(1,),
            in_specs=[whole(s) for s in in_shapes + [stats.shape] * NY],
            out_specs=[whole((NZ, BLOCK, 2 * HEAD))] + [whole((BLOCK, ROWS))] * NY,
            scratch_shapes=common
            + [
                pltpu.VMEM((NZ, HEAD, BLOCK), bf16),
                pltpu.VMEM((NY, 2, ROWS), f32),
                pltpu.VMEM((NZ, BLOCK, HEAD), f32),
                pltpu.VMEM((NZ, BLOCK, HEAD), f32),
                pltpu.VMEM((NY, HEAD, ROWS), f32),
            ]
            + lists,
        ),
        compiler_params=params,
        name="grads",
    )(place, ancestry, kv_all, *groups, *all_stats)
    dq_own = [dq_parts[0]] + [lax.ppermute(dq_parts[k], "y", shift(NY, -k)) for k in range(1, NY)]
    dkv_own = lax.all_to_all(dkv, "z", 0, 0, tiled=True)

    out_block = pl.BlockSpec((1, BLOCK, ROWS), lambda i, place: (i, 0, 0))
    low_shape = (BLOCK, ROWS + 2 * HEAD)
    away, low = pl.pallas_call(
        first_half_kernel,
        out_shape=[jax.ShapeDtypeStruct((NX, BLOCK, ROWS), bf16), jax.ShapeDtypeStruct(low_shape, bf16)],
        grid_spec=pltpu.PrefetchScalarGridSpec(
            num_scalar_prefetch=1,
            grid=(NX,),
            in_specs=[whole((BLOCK, HEAD))] * 2
            + [whole((BLOCK, ROWS))] * NY
            + [whole(dkv_own.shape)]
            + weight_specs(True),
            out_specs=[out_block, whole(low_shape)],
        ),
        compiler_params=params,
        name="first_half",
    )(place, cosine, sine, *dq_own, dkv_own, w_query, key_matrix, value_matrix)
    arrived = lax.ppermute(away, "c", shift(NC, 1))
    kept = pl.pallas_call(
        second_half_kernel,
        out_shape=jax.ShapeDtypeStruct((NX, BLOCK, ROWS), f32),
        grid_spec=pltpu.PrefetchScalarGridSpec(
            num_scalar_prefetch=1,
            grid=(NX,),
            in_specs=[whole(low_shape)] + weight_specs(False),
            out_specs=out_block,
        ),
        compiler_params=params,
        name="second_half",
    )(place, low, w_query, key_matrix, value_matrix)
    total = kept[0] + arrived[0].astype(f32)
    sent = [(kept[k] + arrived[k].astype(f32)).astype(bf16) for k in range(1, NX)]
    for k in range(1, NX):
        total = total + lax.ppermute(sent[k - 1], "x", shift(NX, k)).astype(f32)
    return total.astype(bf16)


def solution(mesh):
    grid = Mesh(mesh.devices.reshape(NZ, NY, NX, NC), ("z", "y", "x", "c"))
    split = P(("z", "y"), ("x", "c"))
    weight = P(None, ("x", "c"))
    return jax.shard_map(
        shards,
        mesh=grid,
        in_specs=(split, split, split, split, P(), weight, weight, weight),
        out_specs=split,
        check_vma=False,
    )
```

```python
import math

import jax
import jax.numpy as jnp
from jax import lax
from jax.experimental import pallas as pl
from jax.experimental.pallas import tpu as pltpu
from jax.sharding import Mesh, PartitionSpec as P

HEAD = 128
BLOCK = 128
GROUP = 5
ROWS = GROUP * BLOCK
NZ, NY, NX, NC = 8, 4, 4, 2
PAIRS = NZ // 2
ANC = 17
ROPE_BASE = 1000000.0
MASKED = -1e30
FACTOR = HEAD ** -0.5
NT = (((1,), (1,)), ((), ()))
NN = (((1,), (0,)), ((), ()))
F32, BF16, I32 = jnp.float32, jnp.bfloat16, jnp.int32
VMEM_LIMIT = 16 << 20

VM = pl.BlockSpec(memory_space=pltpu.VMEM)
SM = pl.BlockSpec(memory_space=pltpu.SMEM)
HB = pl.BlockSpec(memory_space=pltpu.HBM)


def dot_nt(a, b):
    return lax.dot_general(a, b, NT, preferred_element_type=F32)


def dot_nn(a, b):
    return lax.dot_general(a, b, NN, preferred_element_type=F32)


def call(body, out_shape, in_specs, out_specs, name, scratch=()):
    return pl.pallas_call(
        body,
        out_shape=out_shape,
        in_specs=in_specs,
        out_specs=out_specs,
        scratch_shapes=list(scratch),
        compiler_params=pltpu.CompilerParams(vmem_limit_bytes=VMEM_LIMIT),
        name=name,
    )


def in_hbm(*arrays):
    return [pltpu.with_memory_space_constraint(a, pltpu.HBM) for a in arrays]


def pack_kernel(q_ref, g_ref, k_ref, v_ref, rows_ref, kv_ref, sem):
    copies = []
    for a in range(NZ):
        copies.append((k_ref, kv_ref.at[a, :, 0:HEAD]))
        copies.append((v_ref, kv_ref.at[a, :, HEAD:2 * HEAD]))
    for h in range(GROUP):
        cols = slice(h * HEAD, (h + 1) * HEAD)
        copies.append((q_ref.at[:, cols], rows_ref.at[h * BLOCK:(h + 1) * BLOCK, :]))
        copies.append((g_ref.at[:, cols], rows_ref.at[ROWS + h * BLOCK:ROWS + (h + 1) * BLOCK, :]))
    started = [pltpu.make_async_copy(src, dst, sem.at[i]) for i, (src, dst) in enumerate(copies)]
    for copy in started:
        copy.start()
    for copy in started:
        copy.wait()


def plan_kernel(place_ref, anc_ref, rows_ref, item_ref, list_ref):
    z = place_ref[0]
    y = place_ref[1]
    for j in range(NY):
        query_block = NY * z + ((y - j) & (NY - 1))
        bits = jnp.int32(0)
        for i in range(ANC):
            key_block = anc_ref[query_block, i]
            bits = bits | jnp.where((key_block & (NY - 1)) == y, jnp.int32(1) << (key_block >> 2), 0)
        count = jnp.int32(0)
        for key_z in range(NZ):
            list_ref[count] = key_z
            count = count + ((bits >> key_z) & 1)
        for p in range(PAIRS):
            row = PAIRS * j + p
            first = jnp.where(2 * p < count, list_ref[2 * p], 0)
            both = 2 * p + 1 < count
            second = jnp.where(both, list_ref[2 * p + 1], first)
            item_ref[row, 0] = first
            item_ref[row, 1] = second
            causal = jnp.int32(0) if j == 0 else jnp.int32(-BLOCK)
            item_ref[row, 2] = jnp.where(first == z, causal, -BLOCK)
            item_ref[row, 3] = jnp.where(both, jnp.where(second == z, causal, -BLOCK), BLOCK)
        item_ref[NY * PAIRS + j, 0] = (count + 1) // 2


def stats_kernel(item_ref, kv_ref, g0, g1, g2, g3, stat_ref, score_ref, pgrad_ref):
    key_row = lax.broadcasted_iota(I32, (BLOCK, ROWS), 0)
    query_row = lax.broadcasted_iota(I32, (BLOCK, ROWS), 1) % BLOCK
    gap = query_row - key_row
    for j, group in enumerate((g0, g1, g2, g3)):

        def step(p, carry, j=j, group=group):
            old, totals, dots = carry
            row = PAIRS * j + p
            first = item_ref[row, 0]
            second = item_ref[row, 1]
            kv = jnp.concatenate([kv_ref[first], kv_ref[second]], axis=0)
            scores = dot_nt(kv[:, :HEAD], group[:ROWS, :]) * FACTOR
            prob_grads = dot_nt(kv[:, HEAD:], group[ROWS:, :])
            upper = jnp.where(gap >= item_ref[row, 2], scores[:BLOCK], MASKED)
            lower = jnp.where(gap >= item_ref[row, 3], scores[BLOCK:], MASKED)
            scores = jnp.concatenate([upper, lower], axis=0)
            score_ref[row] = scores
            pgrad_ref[row] = prob_grads
            highest = jnp.maximum(old, jnp.max(scores, axis=0, keepdims=True))
            weights = jnp.exp(scores - highest)
            shrink = jnp.exp(old - highest)
            totals = totals * shrink + jnp.sum(weights, axis=0, keepdims=True)
            dots = dots * shrink + jnp.sum(weights * prob_grads, axis=0, keepdims=True)
            return highest, totals, dots

        zero = jnp.zeros((1, ROWS), F32)
        start = (jnp.full((1, ROWS), MASKED, F32), zero, zero)
        highest, totals, dots = lax.fori_loop(0, item_ref[NY * PAIRS + j, 0], step, start)
        stat_ref[j, 0:1, :] = highest
        stat_ref[j, 1:2, :] = totals
        stat_ref[j, 2:3, :] = dots
        stat_ref[j, 3:4, :] = zero


def turn_kernel(kv_ref, stat_ref, key_cols):
    for a in range(NZ):
        key_cols[a] = kv_ref[a, :, :HEAD].T


def grads_kernel(item_ref, cols_ref, score_ref, pgrad_ref, g0, g1, g2, g3, s0, s1, s2, s3,
                 dkv_hbm, dq0, dq1, dq2, dq3, dk_acc, dv_acc, dkv_low, sem):
    stats = (s0, s1, s2, s3)
    dk_acc[...] = jnp.zeros_like(dk_acc)
    dv_acc[...] = jnp.zeros_like(dv_acc)
    for j, (group, out) in enumerate(zip((g0, g1, g2, g3), (dq0, dq1, dq2, dq3))):
        views = [stats[k][(j - k) % NY] for k in range(NY)]
        maxima = views[0][0:1]
        for k in range(1, NY):
            maxima = jnp.maximum(maxima, views[k][0:1])
        totals = jnp.zeros((1, ROWS), F32)
        dots = jnp.zeros((1, ROWS), F32)
        for k in range(NY):
            shrink = jnp.exp(views[k][0:1] - maxima)
            totals = totals + views[k][1:2] * shrink
            dots = dots + views[k][2:3] * shrink
        log_totals = maxima + jnp.log(totals)
        row_dots = dots / totals

        def step(p, query_grad, j=j, group=group, log_totals=log_totals, row_dots=row_dots):
            row = PAIRS * j + p
            first = item_ref[row, 0]
            second = item_ref[row, 1]
            probs = jnp.exp(score_ref[row] - log_totals)
            score_grads = (probs * (pgrad_ref[row] - row_dots)).astype(BF16)
            dk_pair = dot_nn(score_grads, group[:ROWS, :])
            dv_pair = dot_nn(probs.astype(BF16), group[ROWS:, :])
            dk_acc[first] += dk_pair[:BLOCK]
            dk_acc[second] += dk_pair[BLOCK:]
            dv_acc[first] += dv_pair[:BLOCK]
            dv_acc[second] += dv_pair[BLOCK:]
            cols = jnp.concatenate([cols_ref[first], cols_ref[second]], axis=1)
            return query_grad + dot_nn(cols, score_grads)

        query_grad = lax.fori_loop(0, item_ref[NY * PAIRS + j, 0], step, jnp.zeros((HEAD, ROWS), F32))
        out[...] = (query_grad * FACTOR).astype(BF16)
    for a in range(NZ):
        dkv_low[a, :, :HEAD] = (dk_acc[a] * FACTOR).astype(BF16)
        dkv_low[a, :, HEAD:] = dv_acc[a].astype(BF16)
    copy = pltpu.make_async_copy(dkv_low, dkv_hbm, sem)
    copy.start()
    copy.wait()


def unrotate(x, cosine, sine):
    front = x[:HEAD // 2]
    back = x[HEAD // 2:]
    return jnp.concatenate([front * cosine + back * sine, back * cosine - front * sine], axis=0)


def query_part_kernel(place_ref, cos_ref, sin_ref, q0, q1, q2, q3, wq, out_ref, low_ref):
    @pl.when(pl.program_id(0) == 0)
    def _():
        cosine = cos_ref[...]
        sine = sin_ref[...]
        for h in range(GROUP):
            cols = slice(h * HEAD, (h + 1) * HEAD)
            total = q0[:, cols].astype(F32)
            for part in (q1, q2, q3):
                total = total + part[:, cols].astype(F32)
            low_ref[:, cols] = unrotate(total, cosine, sine).T.astype(BF16)

    out_ref[0] = dot_nt(low_ref[...], wq[...])


def add_key_value(low_ref, part_ref, wk, wv):
    total = part_ref[0] + dot_nt(low_ref[:, :HEAD], wk[...])
    return total + dot_nt(low_ref[:, HEAD:], wv[...])


def first_half_kernel(place_ref, cos_ref, sin_ref, dkv_ref, part_ref, wk, wv, out_ref, low_ref):
    @pl.when(pl.program_id(0) == 0)
    def _():
        total = dkv_ref[0].astype(F32)
        for a in range(1, NZ):
            total = total + dkv_ref[a].astype(F32)
        low_ref[:, :HEAD] = unrotate(total[:, :HEAD].T, cos_ref[...], sin_ref[...]).T.astype(BF16)
        low_ref[:, HEAD:] = total[:, HEAD:].astype(BF16)

    out_ref[0] = add_key_value(low_ref, part_ref, wk, wv).astype(BF16)


def second_half_kernel(place_ref, low_ref, part_ref, wk, wv, out_ref):
    out_ref[0] = add_key_value(low_ref, part_ref, wk, wv)


def weight_rows(first, width):
    def pick(i, place):
        step = i + first
        core = jnp.where(step < NX, 1 - place[3], place[3])
        return (2 * ((place[2] + step) & (NX - 1)) + core, 0)

    return pl.BlockSpec((ROWS, width), pick)


def out_rows(first):
    return pl.BlockSpec((1, BLOCK, ROWS), lambda i, place: (i + first, 0, 0))


def stepped(body, steps, out_shape, in_specs, out_specs, name, scratch=()):
    return pl.pallas_call(
        body,
        out_shape=out_shape,
        grid_spec=pltpu.PrefetchScalarGridSpec(
            num_scalar_prefetch=1,
            grid=(steps,),
            in_specs=in_specs,
            out_specs=out_specs,
            scratch_shapes=list(scratch),
        ),
        compiler_params=pltpu.CompilerParams(vmem_limit_bytes=VMEM_LIMIT),
        name=name,
    )


def shift(size, k):
    return [(i, (i + k) % size) for i in range(size)]


def shards(queries, keys, values, out_grad, ancestry, w_query, key_matrix, value_matrix):
    z, y, x, c = (lax.axis_index(name) for name in "zyxc")
    place = jnp.stack([z, y, x, c]).astype(I32)
    group, kv = call(
        pack_kernel,
        [pltpu.VMEM((2 * ROWS, HEAD), BF16), pltpu.HBM((NZ, BLOCK, 2 * HEAD), BF16)],
        [HB] * 4,
        [VM, HB],
        "pack",
        [pltpu.SemaphoreType.DMA((2 * NZ + 2 * GROUP,))],
    )(*in_hbm(queries, out_grad, keys, values))
    groups = [group] + [lax.ppermute(group, "y", shift(NY, k)) for k in range(1, NY)]
    kv_all = lax.all_to_all(kv, "z", 0, 0, tiled=True)

    own_block = NY * z + y
    own_row = lax.dynamic_slice_in_dim(ancestry, own_block, 1, 0)
    depth = jnp.sum((own_row != own_block).astype(I32))
    token_places = (BLOCK * depth + jnp.arange(BLOCK, dtype=I32)).astype(F32)
    frequencies = jnp.exp(jnp.arange(HEAD // 2, dtype=F32) * (-2.0 * math.log(ROPE_BASE) / HEAD))
    angles = frequencies[:, None] * token_places[None, :]
    cosine = jnp.cos(angles)
    sine = jnp.sin(angles)
    items = call(
        plan_kernel,
        jax.ShapeDtypeStruct((NY * PAIRS + NY, 4), I32),
        [SM, SM, VM],
        SM,
        "plan",
        [pltpu.SMEM((NZ + 1,), I32)],
    )(place, ancestry, group)
    items, cosine, sine = lax.optimization_barrier((items, cosine, sine))

    tiles = (NY * PAIRS, 2 * BLOCK, ROWS)
    stats, scores, prob_grads = call(
        stats_kernel,
        [jax.ShapeDtypeStruct((NY, 4, ROWS), F32), pltpu.VMEM(tiles, F32), pltpu.VMEM(tiles, F32)],
        [SM] + [VM] * (1 + NY),
        [VM] * 3,
        "stats",
    )(items, kv_all, *groups)
    all_stats = [stats] + [lax.ppermute(stats, "y", shift(NY, k)) for k in range(1, NY)]
    key_cols = call(
        turn_kernel, pltpu.VMEM((NZ, HEAD, BLOCK), BF16), [VM, VM], VM, "turn",
    )(kv_all, stats)
    dkv, *dq_parts = call(
        grads_kernel,
        [pltpu.HBM((NZ, BLOCK, 2 * HEAD), BF16)] + [pltpu.VMEM((HEAD, ROWS), BF16)] * NY,
        [SM] + [VM] * (3 + 2 * NY),
        [HB] + [VM] * NY,
        "grads",
        [
            pltpu.VMEM((NZ, BLOCK, HEAD), F32),
            pltpu.VMEM((NZ, BLOCK, HEAD), F32),
            pltpu.VMEM((NZ, BLOCK, 2 * HEAD), BF16),
            pltpu.SemaphoreType.DMA,
        ],
    )(items, key_cols, scores, prob_grads, *groups, *all_stats)
    dq_own = [dq_parts[0]] + [lax.ppermute(dq_parts[k], "y", shift(NY, -k)) for k in range(1, NY)]
    dkv_own = lax.all_to_all(dkv, "z", 0, 0, tiled=True)

    wq, wk, wv = in_hbm(w_query, key_matrix, value_matrix)
    query_part = stepped(
        query_part_kernel,
        2 * NX,
        pltpu.VMEM((2 * NX, BLOCK, ROWS), F32),
        [VM] * (2 + NY) + [weight_rows(0, ROWS)],
        out_rows(0),
        "query_part",
        [pltpu.VMEM((BLOCK, ROWS), BF16)],
    )(place, cosine, sine, *dq_own, wq)
    away, low = stepped(
        first_half_kernel,
        NX,
        [pltpu.VMEM((NX, BLOCK, ROWS), BF16), pltpu.VMEM((BLOCK, 2 * HEAD), BF16)],
        [VM] * 3 + [out_rows(0), weight_rows(0, HEAD), weight_rows(0, HEAD)],
        [out_rows(0), VM],
        "first_half",
    )(place, cosine, sine, dkv_own, query_part, wk, wv)
    arrived = lax.ppermute(away, "c", shift(NC, 1))
    kept = stepped(
        second_half_kernel,
        NX,
        pltpu.VMEM((NX, BLOCK, ROWS), F32),
        [VM, out_rows(NX), weight_rows(NX, HEAD), weight_rows(NX, HEAD)],
        out_rows(0),
        "second_half",
    )(place, low, query_part, wk, wv)
    total = kept[0] + arrived[0].astype(F32)
    sent = [(kept[k] + arrived[k].astype(F32)).astype(BF16) for k in range(1, NX)]
    for k in range(1, NX):
        total = total + lax.ppermute(sent[k - 1], "x", shift(NX, k)).astype(F32)
    return total.astype(BF16)


def solution(mesh):
    grid = Mesh(mesh.devices.reshape(NZ, NY, NX, NC), ("z", "y", "x", "c"))
    split = P(("z", "y"), ("x", "c"))
    weight = P(None, ("x", "c"))
    return jax.shard_map(
        shards,
        mesh=grid,
        in_specs=(split, split, split, split, P(), weight, weight, weight),
        out_specs=split,
        check_vma=False,
    )
```

```python
import math

import jax
import jax.numpy as jnp
from jax import lax
from jax.experimental import pallas as pl
from jax.experimental.pallas import tpu as pltpu
from jax.sharding import Mesh, PartitionSpec as P

HEAD = 128
BLOCK = 128
GROUP = 5
ROWS = GROUP * BLOCK
NZ, NY, NX, NC = 8, 4, 4, 2
PAIRS = NZ // 2
ANC = 17
ROPE_BASE = 1000000.0
MASKED = -1e30
FACTOR = HEAD ** -0.5
NT = (((1,), (1,)), ((), ()))
NN = (((1,), (0,)), ((), ()))
F32, BF16, I32 = jnp.float32, jnp.bfloat16, jnp.int32
VMEM_LIMIT = 16 << 20

VM = pl.BlockSpec(memory_space=pltpu.VMEM)
SM = pl.BlockSpec(memory_space=pltpu.SMEM)
HB = pl.BlockSpec(memory_space=pltpu.HBM)


def dot_nt(a, b):
    return lax.dot_general(a, b, NT, preferred_element_type=F32)


def dot_nn(a, b):
    return lax.dot_general(a, b, NN, preferred_element_type=F32)


def call(body, out_shape, in_specs, out_specs, name, scratch=()):
    return pl.pallas_call(
        body,
        out_shape=out_shape,
        in_specs=in_specs,
        out_specs=out_specs,
        scratch_shapes=list(scratch),
        compiler_params=pltpu.CompilerParams(vmem_limit_bytes=VMEM_LIMIT),
        name=name,
    )


def in_hbm(*arrays):
    return [pltpu.with_memory_space_constraint(a, pltpu.HBM) for a in arrays]


def run_copies(pairs, sem):
    started = [pltpu.make_async_copy(src, dst, sem.at[i]) for i, (src, dst) in enumerate(pairs)]
    for copy in started:
        copy.start()
    for copy in started:
        copy.wait()


def stack_kernel(q_ref, g_ref, rows_ref, sem):
    pairs = []
    for h in range(GROUP):
        cols = slice(h * HEAD, (h + 1) * HEAD)
        pairs.append((q_ref.at[:, cols], rows_ref.at[h * BLOCK:(h + 1) * BLOCK, :]))
        pairs.append((g_ref.at[:, cols], rows_ref.at[ROWS + h * BLOCK:ROWS + (h + 1) * BLOCK, :]))
    run_copies(pairs, sem)


def spread_kernel(k_ref, v_ref, rows_ref, kv_ref, pair_ref, sem):
    run_copies([(k_ref, pair_ref.at[:, 0:HEAD]), (v_ref, pair_ref.at[:, HEAD:2 * HEAD])], sem)
    run_copies([(pair_ref, kv_ref.at[a]) for a in range(NZ)], sem)


def flush_kernel(low_ref, out_ref, sem):
    run_copies([(low_ref, out_ref)], sem)


def plan_kernel(place_ref, anc_ref, rows_ref, item_ref, list_ref):
    z = place_ref[0]
    y = place_ref[1]
    for j in range(NY):
        query_block = NY * z + ((y - j) & (NY - 1))
        bits = jnp.int32(0)
        for i in range(ANC):
            key_block = anc_ref[query_block, i]
            bits = bits | jnp.where((key_block & (NY - 1)) == y, jnp.int32(1) << (key_block >> 2), 0)
        count = jnp.int32(0)
        for key_z in range(NZ):
            list_ref[count] = key_z
            count = count + ((bits >> key_z) & 1)
        for p in range(PAIRS):
            row = PAIRS * j + p
            first = jnp.where(2 * p < count, list_ref[2 * p], 0)
            both = 2 * p + 1 < count
            second = jnp.where(both, list_ref[2 * p + 1], first)
            item_ref[row, 0] = first
            item_ref[row, 1] = second
            causal = jnp.int32(0) if j == 0 else jnp.int32(-BLOCK)
            item_ref[row, 2] = jnp.where(first == z, causal, -BLOCK)
            item_ref[row, 3] = jnp.where(both, jnp.where(second == z, causal, -BLOCK), BLOCK)
        item_ref[NY * PAIRS + j, 0] = (count + 1) // 2


def stats_kernel(item_ref, kv_ref, g0, g1, g2, g3, stat_ref, score_ref, pgrad_ref):
    key_row = lax.broadcasted_iota(I32, (BLOCK, ROWS), 0)
    query_row = lax.broadcasted_iota(I32, (BLOCK, ROWS), 1) % BLOCK
    gap = query_row - key_row
    for j, group in enumerate((g0, g1, g2, g3)):

        def step(p, carry, j=j, group=group):
            old, totals, dots = carry
            row = PAIRS * j + p
            first = item_ref[row, 0]
            second = item_ref[row, 1]
            kv = jnp.concatenate([kv_ref[first], kv_ref[second]], axis=0)
            scores = dot_nt(kv[:, :HEAD], group[:ROWS, :]) * FACTOR
            prob_grads = dot_nt(kv[:, HEAD:], group[ROWS:, :])
            upper = jnp.where(gap >= item_ref[row, 2], scores[:BLOCK], MASKED)
            lower = jnp.where(gap >= item_ref[row, 3], scores[BLOCK:], MASKED)
            scores = jnp.concatenate([upper, lower], axis=0)
            score_ref[row] = scores
            pgrad_ref[row] = prob_grads
            highest = jnp.maximum(old, jnp.max(scores, axis=0, keepdims=True))
            weights = jnp.exp(scores - highest)
            shrink = jnp.exp(old - highest)
            totals = totals * shrink + jnp.sum(weights, axis=0, keepdims=True)
            dots = dots * shrink + jnp.sum(weights * prob_grads, axis=0, keepdims=True)
            return highest, totals, dots

        zero = jnp.zeros((1, ROWS), F32)
        start = (jnp.full((1, ROWS), MASKED, F32), zero, zero)
        highest, totals, dots = lax.fori_loop(0, item_ref[NY * PAIRS + j, 0], step, start)
        stat_ref[j, 0:1, :] = highest
        stat_ref[j, 1:2, :] = totals
        stat_ref[j, 2:3, :] = dots
        stat_ref[j, 3:4, :] = zero


def turn_kernel(kv_ref, stat_ref, key_cols):
    for a in range(NZ):
        key_cols[a] = kv_ref[a, :, :HEAD].T


def grads_kernel(item_ref, cols_ref, score_ref, pgrad_ref, g0, g1, g2, g3, s0, s1, s2, s3,
                 dkv_ref, dq0, dq1, dq2, dq3, dk_acc, dv_acc):
    stats = (s0, s1, s2, s3)
    dk_acc[...] = jnp.zeros_like(dk_acc)
    dv_acc[...] = jnp.zeros_like(dv_acc)
    for j, (group, out) in enumerate(zip((g0, g1, g2, g3), (dq0, dq1, dq2, dq3))):
        views = [stats[k][(j - k) % NY] for k in range(NY)]
        maxima = views[0][0:1]
        for k in range(1, NY):
            maxima = jnp.maximum(maxima, views[k][0:1])
        totals = jnp.zeros((1, ROWS), F32)
        dots = jnp.zeros((1, ROWS), F32)
        for k in range(NY):
            shrink = jnp.exp(views[k][0:1] - maxima)
            totals = totals + views[k][1:2] * shrink
            dots = dots + views[k][2:3] * shrink
        log_totals = maxima + jnp.log(totals)
        row_dots = dots / totals

        def step(p, query_grad, j=j, group=group, log_totals=log_totals, row_dots=row_dots):
            row = PAIRS * j + p
            first = item_ref[row, 0]
            second = item_ref[row, 1]
            probs = jnp.exp(score_ref[row] - log_totals)
            score_grads = (probs * (pgrad_ref[row] - row_dots)).astype(BF16)
            dk_pair = dot_nn(score_grads, group[:ROWS, :])
            dv_pair = dot_nn(probs.astype(BF16), group[ROWS:, :])
            dk_acc[first] += dk_pair[:BLOCK]
            dk_acc[second] += dk_pair[BLOCK:]
            dv_acc[first] += dv_pair[:BLOCK]
            dv_acc[second] += dv_pair[BLOCK:]
            cols = jnp.concatenate([cols_ref[first], cols_ref[second]], axis=1)
            return query_grad + dot_nn(cols, score_grads)

        query_grad = lax.fori_loop(0, item_ref[NY * PAIRS + j, 0], step, jnp.zeros((HEAD, ROWS), F32))
        out[...] = (query_grad * FACTOR).astype(BF16)
    for a in range(NZ):
        dkv_ref[a, :, :HEAD] = (dk_acc[a] * FACTOR).astype(BF16)
        dkv_ref[a, :, HEAD:] = dv_acc[a].astype(BF16)


def unrotate(x, cosine, sine):
    front = x[:HEAD // 2]
    back = x[HEAD // 2:]
    return jnp.concatenate([front * cosine + back * sine, back * cosine - front * sine], axis=0)


def query_part_kernel(place_ref, cos_ref, sin_ref, q0, q1, q2, q3, wq, out_ref, low_ref):
    @pl.when(pl.program_id(0) == 0)
    def _():
        cosine = cos_ref[...]
        sine = sin_ref[...]
        for h in range(GROUP):
            cols = slice(h * HEAD, (h + 1) * HEAD)
            total = q0[:, cols].astype(F32)
            for part in (q1, q2, q3):
                total = total + part[:, cols].astype(F32)
            low_ref[cols, :] = unrotate(total, cosine, sine).astype(BF16)

    out_ref[0] = dot_nn(wq[...], low_ref[...])


def add_key_value(low_ref, part_ref, wk, wv):
    total = part_ref[0] + dot_nn(wk[...], low_ref[:HEAD, :])
    return total + dot_nn(wv[...], low_ref[HEAD:, :])


def first_half_kernel(place_ref, cos_ref, sin_ref, dkv_ref, part_ref, wk, wv, out_ref, low_ref):
    @pl.when(pl.program_id(0) == 0)
    def _():
        total = dkv_ref[0].astype(F32)
        for a in range(1, NZ):
            total = total + dkv_ref[a].astype(F32)
        low_ref[:HEAD, :] = unrotate(total[:, :HEAD].T, cos_ref[...], sin_ref[...]).astype(BF16)
        low_ref[HEAD:, :] = total[:, HEAD:].T.astype(BF16)

    out_ref[0] = add_key_value(low_ref, part_ref, wk, wv).astype(BF16)


def second_half_kernel(place_ref, low_ref, part_ref, wk, wv, out_ref):
    out_ref[0] = add_key_value(low_ref, part_ref, wk, wv)


def finish_kernel(kept_ref, arrived_ref, p0, p1, p2, out_ref):
    for h in range(GROUP):
        rows = slice(h * HEAD, (h + 1) * HEAD)
        total = kept_ref[rows, :]
        for part in (arrived_ref, p0, p1, p2):
            total = total + part[rows, :].astype(F32)
        out_ref[:, rows] = total.T.astype(BF16)


def weight_rows(first, width):
    def pick(i, place):
        step = i + first
        core = jnp.where(step < NX, 1 - place[3], place[3])
        return (2 * ((place[2] + step) & (NX - 1)) + core, 0)

    return pl.BlockSpec((ROWS, width), pick)


def out_rows(first):
    return pl.BlockSpec((1, ROWS, BLOCK), lambda i, place: (i + first, 0, 0))


def stepped(body, steps, out_shape, in_specs, out_specs, name, scratch=()):
    return pl.pallas_call(
        body,
        out_shape=out_shape,
        grid_spec=pltpu.PrefetchScalarGridSpec(
            num_scalar_prefetch=1,
            grid=(steps,),
            in_specs=in_specs,
            out_specs=out_specs,
            scratch_shapes=list(scratch),
        ),
        compiler_params=pltpu.CompilerParams(vmem_limit_bytes=VMEM_LIMIT),
        name=name,
    )


def shift(size, k):
    return [(i, (i + k) % size) for i in range(size)]


def shards(queries, keys, values, out_grad, ancestry, w_query, key_matrix, value_matrix):
    z, y, x, c = (lax.axis_index(name) for name in "zyxc")
    place = jnp.stack([z, y, x, c]).astype(I32)
    group = call(
        stack_kernel, pltpu.VMEM((2 * ROWS, HEAD), BF16), [HB] * 2, VM, "stack",
        [pltpu.SemaphoreType.DMA((2 * GROUP,))],
    )(*in_hbm(queries, out_grad))
    kv = call(
        spread_kernel, pltpu.HBM((NZ, BLOCK, 2 * HEAD), BF16), [HB, HB, VM], HB, "spread",
        [pltpu.VMEM((BLOCK, 2 * HEAD), BF16), pltpu.SemaphoreType.DMA((NZ,))],
    )(*in_hbm(keys, values), group)
    groups = [group] + [lax.ppermute(group, "y", shift(NY, k)) for k in range(1, NY)]
    kv_all = lax.all_to_all(kv, "z", 0, 0, tiled=True)

    own_block = NY * z + y
    own_row = lax.dynamic_slice_in_dim(ancestry, own_block, 1, 0)
    depth = jnp.sum((own_row != own_block).astype(I32))
    token_places = (BLOCK * depth + jnp.arange(BLOCK, dtype=I32)).astype(F32)
    frequencies = jnp.exp(jnp.arange(HEAD // 2, dtype=F32) * (-2.0 * math.log(ROPE_BASE) / HEAD))
    angles = frequencies[:, None] * token_places[None, :]
    cosine = jnp.cos(angles)
    sine = jnp.sin(angles)
    items = call(
        plan_kernel,
        jax.ShapeDtypeStruct((NY * PAIRS + NY, 4), I32),
        [SM, SM, VM],
        SM,
        "plan",
        [pltpu.SMEM((NZ + 1,), I32)],
    )(place, ancestry, group)
    items, cosine, sine = lax.optimization_barrier((items, cosine, sine))

    tiles = (NY * PAIRS, 2 * BLOCK, ROWS)
    stats, scores, prob_grads = call(
        stats_kernel,
        [jax.ShapeDtypeStruct((NY, 4, ROWS), F32), pltpu.VMEM(tiles, F32), pltpu.VMEM(tiles, F32)],
        [SM] + [VM] * (1 + NY),
        [VM] * 3,
        "stats",
    )(items, kv_all, *groups)
    all_stats = [stats] + [lax.ppermute(stats, "y", shift(NY, k)) for k in range(1, NY)]
    key_cols = call(
        turn_kernel, pltpu.VMEM((NZ, HEAD, BLOCK), BF16), [VM, VM], VM, "turn",
    )(kv_all, stats)
    dkv, *dq_parts = call(
        grads_kernel,
        [pltpu.VMEM((NZ, BLOCK, 2 * HEAD), BF16)] + [pltpu.VMEM((HEAD, ROWS), BF16)] * NY,
        [SM] + [VM] * (3 + 2 * NY),
        [VM] * (1 + NY),
        "grads",
        [pltpu.VMEM((NZ, BLOCK, HEAD), F32), pltpu.VMEM((NZ, BLOCK, HEAD), F32)],
    )(items, key_cols, scores, prob_grads, *groups, *all_stats)
    dq_own = [dq_parts[0]] + [lax.ppermute(dq_parts[k], "y", shift(NY, -k)) for k in range(1, NY)]
    dkv = call(
        flush_kernel, pltpu.HBM(dkv.shape, BF16), [VM], HB, "flush", [pltpu.SemaphoreType.DMA((1,))],
    )(dkv)
    dkv_own = lax.all_to_all(dkv, "z", 0, 0, tiled=True)

    wq, wk, wv = in_hbm(w_query, key_matrix, value_matrix)
    query_part = stepped(
        query_part_kernel,
        2 * NX,
        pltpu.VMEM((2 * NX, ROWS, BLOCK), F32),
        [VM] * (2 + NY) + [weight_rows(0, ROWS)],
        out_rows(0),
        "query_part",
        [pltpu.VMEM((ROWS, BLOCK), BF16)],
    )(place, cosine, sine, *dq_own, wq)
    away, low = stepped(
        first_half_kernel,
        NX,
        [pltpu.VMEM((NX, ROWS, BLOCK), BF16), pltpu.VMEM((2 * HEAD, BLOCK), BF16)],
        [VM] * 3 + [out_rows(0), weight_rows(0, HEAD), weight_rows(0, HEAD)],
        [out_rows(0), VM],
        "first_half",
    )(place, cosine, sine, dkv_own, query_part, wk, wv)
    arrived = lax.ppermute(away, "c", shift(NC, 1))
    kept = stepped(
        second_half_kernel,
        NX,
        pltpu.VMEM((NX, ROWS, BLOCK), F32),
        [VM, out_rows(NX), weight_rows(NX, HEAD), weight_rows(NX, HEAD)],
        out_rows(0),
        "second_half",
    )(place, low, query_part, wk, wv)
    sent = [(kept[k] + arrived[k].astype(F32)).astype(BF16) for k in range(1, NX)]
    parts = [lax.ppermute(sent[k - 1], "x", shift(NX, k)) for k in range(1, NX)]
    return call(
        finish_kernel, jax.ShapeDtypeStruct((BLOCK, ROWS), BF16), [VM] * (2 + len(parts)), VM, "finish",
    )(kept[0], arrived[0], *parts)


def solution(mesh):
    grid = Mesh(mesh.devices.reshape(NZ, NY, NX, NC), ("z", "y", "x", "c"))
    split = P(("z", "y"), ("x", "c"))
    weight = P(None, ("x", "c"))
    return jax.shard_map(
        shards,
        mesh=grid,
        in_specs=(split, split, split, split, P(), weight, weight, weight),
        out_specs=split,
        check_vma=False,
    )
```

```python
import math

import jax
import jax.numpy as jnp
from jax import lax
from jax.experimental import pallas as pl
from jax.experimental.pallas import tpu as pltpu
from jax.sharding import Mesh, PartitionSpec as P

HEAD = 128
BLOCK = 128
GROUP = 5
ROWS = GROUP * BLOCK
NZ, NY, NX, NC = 8, 4, 4, 2
PAIRS = NZ // 2
ANC = 17
ROPE_BASE = 1000000.0
MASKED = -1e30
FACTOR = HEAD ** -0.5
NT = (((1,), (1,)), ((), ()))
NN = (((1,), (0,)), ((), ()))
F32, BF16, I32 = jnp.float32, jnp.bfloat16, jnp.int32
VMEM_LIMIT = 16 << 20
PLAN_FLOPS = 15_000_000_000

VM = pl.BlockSpec(memory_space=pltpu.VMEM)
SM = pl.BlockSpec(memory_space=pltpu.SMEM)
HB = pl.BlockSpec(memory_space=pltpu.HBM)


def dot_nt(a, b):
    return lax.dot_general(a, b, NT, preferred_element_type=F32)


def dot_nn(a, b):
    return lax.dot_general(a, b, NN, preferred_element_type=F32)


def call(body, out_shape, in_specs, out_specs, name, scratch=(), flops=0):
    return pl.pallas_call(
        body,
        out_shape=out_shape,
        in_specs=in_specs,
        out_specs=out_specs,
        scratch_shapes=list(scratch),
        compiler_params=pltpu.CompilerParams(vmem_limit_bytes=VMEM_LIMIT),
        cost_estimate=pl.CostEstimate(flops=flops, transcendentals=0, bytes_accessed=0) if flops else None,
        name=name,
    )


def in_hbm(*arrays):
    return [pltpu.with_memory_space_constraint(a, pltpu.HBM) for a in arrays]


def run_copies(pairs, sem):
    started = [pltpu.make_async_copy(src, dst, sem.at[i]) for i, (src, dst) in enumerate(pairs)]
    for copy in started:
        copy.start()
    for copy in started:
        copy.wait()


def stack_kernel(q_ref, g_ref, rows_ref, sem):
    pairs = []
    for h in range(GROUP):
        cols = slice(h * HEAD, (h + 1) * HEAD)
        pairs.append((q_ref.at[:, cols], rows_ref.at[h * BLOCK:(h + 1) * BLOCK, :]))
        pairs.append((g_ref.at[:, cols], rows_ref.at[ROWS + h * BLOCK:ROWS + (h + 1) * BLOCK, :]))
    run_copies(pairs, sem)


def spread_kernel(k_ref, v_ref, rows_ref, kv_ref, pair_ref, sem):
    run_copies([(k_ref, pair_ref.at[:, 0:HEAD]), (v_ref, pair_ref.at[:, HEAD:2 * HEAD])], sem)
    run_copies([(pair_ref, kv_ref.at[a]) for a in range(NZ)], sem)


def flush_kernel(low_ref, out_ref, sem):
    run_copies([(low_ref, out_ref)], sem)


def plan_kernel(place_ref, anc_ref, g1, g2, g3, item_ref, list_ref):
    z = place_ref[0]
    y = place_ref[1]
    for j in range(NY):
        query_block = NY * z + ((y - j) & (NY - 1))
        bits = jnp.int32(0)
        for i in range(ANC):
            key_block = anc_ref[query_block, i]
            bits = bits | jnp.where((key_block & (NY - 1)) == y, jnp.int32(1) << (key_block >> 2), 0)
        count = jnp.int32(0)
        for key_z in range(NZ):
            list_ref[count] = key_z
            count = count + ((bits >> key_z) & 1)
        for p in range(PAIRS):
            row = PAIRS * j + p
            first = jnp.where(2 * p < count, list_ref[2 * p], 0)
            both = 2 * p + 1 < count
            second = jnp.where(both, list_ref[2 * p + 1], first)
            item_ref[row, 0] = first
            item_ref[row, 1] = second
            causal = jnp.int32(0) if j == 0 else jnp.int32(-BLOCK)
            item_ref[row, 2] = jnp.where(first == z, causal, -BLOCK)
            item_ref[row, 3] = jnp.where(both, jnp.where(second == z, causal, -BLOCK), BLOCK)
        item_ref[NY * PAIRS + j, 0] = (count + 1) // 2


def stats_kernel(item_ref, kv_ref, g0, g1, g2, g3, stat_ref, score_ref, pgrad_ref):
    key_row = lax.broadcasted_iota(I32, (BLOCK, ROWS), 0)
    query_row = lax.broadcasted_iota(I32, (BLOCK, ROWS), 1) % BLOCK
    gap = query_row - key_row
    for j, group in enumerate((g0, g1, g2, g3)):

        def step(p, carry, j=j, group=group):
            old, totals, dots = carry
            row = PAIRS * j + p
            first = item_ref[row, 0]
            second = item_ref[row, 1]
            kv = jnp.concatenate([kv_ref[first], kv_ref[second]], axis=0)
            scores = dot_nt(kv[:, :HEAD], group[:ROWS, :]) * FACTOR
            prob_grads = dot_nt(kv[:, HEAD:], group[ROWS:, :])
            upper = jnp.where(gap >= item_ref[row, 2], scores[:BLOCK], MASKED)
            lower = jnp.where(gap >= item_ref[row, 3], scores[BLOCK:], MASKED)
            scores = jnp.concatenate([upper, lower], axis=0)
            score_ref[row] = scores
            pgrad_ref[row] = prob_grads
            highest = jnp.maximum(old, jnp.max(scores, axis=0, keepdims=True))
            weights = jnp.exp(scores - highest)
            shrink = jnp.exp(old - highest)
            totals = totals * shrink + jnp.sum(weights, axis=0, keepdims=True)
            dots = dots * shrink + jnp.sum(weights * prob_grads, axis=0, keepdims=True)
            return highest, totals, dots

        zero = jnp.zeros((1, ROWS), F32)
        start = (jnp.full((1, ROWS), MASKED, F32), zero, zero)
        highest, totals, dots = lax.fori_loop(0, item_ref[NY * PAIRS + j, 0], step, start)
        stat_ref[j, 0:1, :] = highest
        stat_ref[j, 1:2, :] = totals
        stat_ref[j, 2:3, :] = dots
        stat_ref[j, 3:4, :] = zero


def turn_kernel(kv_ref, stat_ref, key_cols):
    for a in range(NZ):
        key_cols[a] = kv_ref[a, :, :HEAD].T


def grads_kernel(item_ref, cols_ref, score_ref, pgrad_ref, g0, g1, g2, g3, s0, s1, s2, s3,
                 dkv_ref, dq0, dq1, dq2, dq3, dk_acc, dv_acc):
    stats = (s0, s1, s2, s3)
    dk_acc[...] = jnp.zeros_like(dk_acc)
    dv_acc[...] = jnp.zeros_like(dv_acc)
    for j, (group, out) in enumerate(zip((g0, g1, g2, g3), (dq0, dq1, dq2, dq3))):
        views = [stats[k][(j - k) % NY] for k in range(NY)]
        maxima = views[0][0:1]
        for k in range(1, NY):
            maxima = jnp.maximum(maxima, views[k][0:1])
        totals = jnp.zeros((1, ROWS), F32)
        dots = jnp.zeros((1, ROWS), F32)
        for k in range(NY):
            shrink = jnp.exp(views[k][0:1] - maxima)
            totals = totals + views[k][1:2] * shrink
            dots = dots + views[k][2:3] * shrink
        log_totals = maxima + jnp.log(totals)
        row_dots = dots / totals

        def step(p, query_grad, j=j, group=group, log_totals=log_totals, row_dots=row_dots):
            row = PAIRS * j + p
            first = item_ref[row, 0]
            second = item_ref[row, 1]
            probs = jnp.exp(score_ref[row] - log_totals)
            score_grads = (probs * (pgrad_ref[row] - row_dots)).astype(BF16)
            dk_pair = dot_nn(score_grads, group[:ROWS, :])
            dv_pair = dot_nn(probs.astype(BF16), group[ROWS:, :])
            dk_acc[first] += dk_pair[:BLOCK]
            dk_acc[second] += dk_pair[BLOCK:]
            dv_acc[first] += dv_pair[:BLOCK]
            dv_acc[second] += dv_pair[BLOCK:]
            cols = jnp.concatenate([cols_ref[first], cols_ref[second]], axis=1)
            return query_grad + dot_nn(cols, score_grads)

        query_grad = lax.fori_loop(0, item_ref[NY * PAIRS + j, 0], step, jnp.zeros((HEAD, ROWS), F32))
        out[...] = (query_grad * FACTOR).astype(BF16)
    for a in range(NZ):
        dkv_ref[a, :, :HEAD] = (dk_acc[a] * FACTOR).astype(BF16)
        dkv_ref[a, :, HEAD:] = dv_acc[a].astype(BF16)


def unrotate(x, cosine, sine):
    front = x[:HEAD // 2]
    back = x[HEAD // 2:]
    return jnp.concatenate([front * cosine + back * sine, back * cosine - front * sine], axis=0)


def weight_rows(place_ref, step):
    core = 1 - place_ref[3] if step < NX else place_ref[3]
    return pl.ds(pl.multiple_of((2 * ((place_ref[2] + step) & (NX - 1)) + core) * ROWS, ROWS), ROWS)


def query_part_kernel(place_ref, cos_ref, sin_ref, q0, q1, q2, q3, wq_hbm, out_ref, wq, sem):
    copies = [
        pltpu.make_async_copy(wq_hbm.at[weight_rows(place_ref, i), :], wq.at[i], sem.at[i]) for i in range(2 * NX)
    ]
    for copy in copies:
        copy.start()
    cosine = cos_ref[...]
    sine = sin_ref[...]
    low = []
    for h in range(GROUP):
        cols = slice(h * HEAD, (h + 1) * HEAD)
        total = q0[:, cols].astype(F32)
        for part in (q1, q2, q3):
            total = total + part[:, cols].astype(F32)
        low.append(unrotate(total, cosine, sine).astype(BF16))
    low = jnp.concatenate(low, axis=0)
    for i, copy in enumerate(copies):
        copy.wait()
        out_ref[i] = dot_nn(wq[i], low)


def fetch_pair(place_ref, first, wk_hbm, wv_hbm, wk, wv, sem):
    copies = []
    for i in range(NX):
        rows = weight_rows(place_ref, first + i)
        copies.append(
            (
                pltpu.make_async_copy(wk_hbm.at[rows, :], wk.at[i], sem.at[2 * i]),
                pltpu.make_async_copy(wv_hbm.at[rows, :], wv.at[i], sem.at[2 * i + 1]),
            )
        )
    for pair in copies:
        for copy in pair:
            copy.start()
    return copies


def first_half_kernel(place_ref, cos_ref, sin_ref, dkv_ref, part_ref, wk_hbm, wv_hbm, out_ref, low_ref, wk, wv, sem):
    copies = fetch_pair(place_ref, 0, wk_hbm, wv_hbm, wk, wv, sem)
    total = dkv_ref[0].astype(F32)
    for a in range(1, NZ):
        total = total + dkv_ref[a].astype(F32)
    low_ref[:HEAD, :] = unrotate(total[:, :HEAD].T, cos_ref[...], sin_ref[...]).astype(BF16)
    low_ref[HEAD:, :] = total[:, HEAD:].T.astype(BF16)
    for i, pair in enumerate(copies):
        for copy in pair:
            copy.wait()
        total = part_ref[i] + dot_nn(wk[i], low_ref[:HEAD, :])
        out_ref[i] = (total + dot_nn(wv[i], low_ref[HEAD:, :])).astype(BF16)


def second_half_kernel(place_ref, low_ref, part_ref, wk_hbm, wv_hbm, out_ref, wk, wv, sem):
    copies = fetch_pair(place_ref, NX, wk_hbm, wv_hbm, wk, wv, sem)
    for i, pair in enumerate(copies):
        for copy in pair:
            copy.wait()
        total = part_ref[NX + i] + dot_nn(wk[i], low_ref[:HEAD, :])
        out_ref[i] = total + dot_nn(wv[i], low_ref[HEAD:, :])


def finish_kernel(kept_ref, arrived_ref, p0, p1, p2, out_ref):
    for h in range(GROUP):
        rows = slice(h * HEAD, (h + 1) * HEAD)
        total = kept_ref[rows, :]
        for part in (arrived_ref, p0, p1, p2):
            total = total + part[rows, :].astype(F32)
        out_ref[:, rows] = total.T.astype(BF16)


def shift(size, k):
    return [(i, (i + k) % size) for i in range(size)]


def shards(queries, keys, values, out_grad, ancestry, w_query, key_matrix, value_matrix):
    z, y, x, c = (lax.axis_index(name) for name in "zyxc")
    place = jnp.stack([z, y, x, c]).astype(I32)
    group = call(
        stack_kernel, pltpu.VMEM((2 * ROWS, HEAD), BF16), [HB] * 2, VM, "stack",
        [pltpu.SemaphoreType.DMA((2 * GROUP,))],
    )(*in_hbm(queries, out_grad))
    kv = call(
        spread_kernel, pltpu.HBM((NZ, BLOCK, 2 * HEAD), BF16), [HB, HB, VM], HB, "spread",
        [pltpu.VMEM((BLOCK, 2 * HEAD), BF16), pltpu.SemaphoreType.DMA((NZ,))],
    )(*in_hbm(keys, values), group)
    groups = [group] + [lax.ppermute(group, "y", shift(NY, k)) for k in range(1, NY)]
    kv_all = lax.all_to_all(kv, "z", 0, 0, tiled=True)

    own_block = NY * z + y
    own_row = lax.dynamic_slice_in_dim(ancestry, own_block, 1, 0)
    depth = jnp.sum((own_row != own_block).astype(I32))
    token_places = (BLOCK * depth + jnp.arange(BLOCK, dtype=I32)).astype(F32)
    frequencies = jnp.exp(jnp.arange(HEAD // 2, dtype=F32) * (-2.0 * math.log(ROPE_BASE) / HEAD))
    angles = frequencies[:, None] * token_places[None, :]
    cosine = jnp.cos(angles)
    sine = jnp.sin(angles)
    items = call(
        plan_kernel,
        jax.ShapeDtypeStruct((NY * PAIRS + NY, 4), I32),
        [SM, SM] + [VM] * 3,
        SM,
        "plan",
        [pltpu.SMEM((NZ + 1,), I32)],
        PLAN_FLOPS,
    )(place, ancestry, *groups[1:])
    items, cosine, sine = lax.optimization_barrier((items, cosine, sine))

    tiles = (NY * PAIRS, 2 * BLOCK, ROWS)
    stats, scores, prob_grads = call(
        stats_kernel,
        [jax.ShapeDtypeStruct((NY, 4, ROWS), F32), pltpu.VMEM(tiles, F32), pltpu.VMEM(tiles, F32)],
        [SM] + [VM] * (1 + NY),
        [VM] * 3,
        "stats",
    )(items, kv_all, *groups)
    all_stats = [stats] + [lax.ppermute(stats, "y", shift(NY, k)) for k in range(1, NY)]
    key_cols = call(
        turn_kernel, pltpu.VMEM((NZ, HEAD, BLOCK), BF16), [VM, VM], VM, "turn",
    )(kv_all, stats)
    dkv, *dq_parts = call(
        grads_kernel,
        [pltpu.VMEM((NZ, BLOCK, 2 * HEAD), BF16)] + [pltpu.VMEM((HEAD, ROWS), BF16)] * NY,
        [SM] + [VM] * (3 + 2 * NY),
        [VM] * (1 + NY),
        "grads",
        [pltpu.VMEM((NZ, BLOCK, HEAD), F32), pltpu.VMEM((NZ, BLOCK, HEAD), F32)],
    )(items, key_cols, scores, prob_grads, *groups, *all_stats)
    dq_own = [dq_parts[0]] + [lax.ppermute(dq_parts[k], "y", shift(NY, -k)) for k in range(1, NY)]
    dkv = call(
        flush_kernel, pltpu.HBM(dkv.shape, BF16), [VM], HB, "flush", [pltpu.SemaphoreType.DMA((1,))],
    )(dkv)
    dkv_own = lax.all_to_all(dkv, "z", 0, 0, tiled=True)

    wq, wk, wv = in_hbm(w_query, key_matrix, value_matrix)
    query_part = call(
        query_part_kernel,
        pltpu.VMEM((2 * NX, ROWS, BLOCK), F32),
        [SM] + [VM] * (2 + NY) + [HB],
        VM,
        "query_part",
        [pltpu.VMEM((2 * NX, ROWS, ROWS), BF16), pltpu.SemaphoreType.DMA((2 * NX,))],
    )(place, cosine, sine, *dq_own, wq)
    pair_scratch = [pltpu.VMEM((NX, ROWS, HEAD), BF16)] * 2 + [pltpu.SemaphoreType.DMA((2 * NX,))]
    away, low = call(
        first_half_kernel,
        [pltpu.VMEM((NX, ROWS, BLOCK), BF16), pltpu.VMEM((2 * HEAD, BLOCK), BF16)],
        [SM] + [VM] * 4 + [HB] * 2,
        [VM, VM],
        "first_half",
        pair_scratch,
    )(place, cosine, sine, dkv_own, query_part, wk, wv)
    arrived = lax.ppermute(away, "c", shift(NC, 1))
    kept = call(
        second_half_kernel,
        pltpu.VMEM((NX, ROWS, BLOCK), F32),
        [SM] + [VM] * 2 + [HB] * 2,
        VM,
        "second_half",
        pair_scratch,
    )(place, low, query_part, wk, wv)
    sent = [(kept[k] + arrived[k].astype(F32)).astype(BF16) for k in range(1, NX)]
    parts = [lax.ppermute(sent[k - 1], "x", shift(NX, k)) for k in range(1, NX)]
    return call(
        finish_kernel, jax.ShapeDtypeStruct((BLOCK, ROWS), BF16), [VM] * (2 + len(parts)), VM, "finish",
    )(kept[0], arrived[0], *parts)


def solution(mesh):
    grid = Mesh(mesh.devices.reshape(NZ, NY, NX, NC), ("z", "y", "x", "c"))
    split = P(("z", "y"), ("x", "c"))
    weight = P(None, ("x", "c"))
    return jax.shard_map(
        shards,
        mesh=grid,
        in_specs=(split, split, split, split, P(), weight, weight, weight),
        out_specs=split,
        check_vma=False,
    )
```

```python
import math

import jax
import jax.numpy as jnp
from jax import lax
from jax.experimental import pallas as pl
from jax.experimental.pallas import tpu as pltpu
from jax.sharding import Mesh, PartitionSpec as P

HEAD = 128
BLOCK = 128
GROUP = 5
ROWS = GROUP * BLOCK
NZ, NY, NX, NC = 8, 4, 4, 2
PAIRS = NZ // 2
ANC = 17
ROPE_BASE = 1000000.0
MASKED = -1e30
FACTOR = HEAD ** -0.5
NT = (((1,), (1,)), ((), ()))
NN = (((1,), (0,)), ((), ()))
F32, BF16, I32 = jnp.float32, jnp.bfloat16, jnp.int32
VMEM_LIMIT = 16 << 20
STATS_FLOPS = 2 * 2 * (NY * ROWS) * (NZ * BLOCK) * HEAD
GRADS_FLOPS = 3 * 2 * (NY * ROWS) * (NZ * BLOCK) * HEAD
QUERY_FLOPS = 2 * BLOCK * ROWS * 2 * NX * ROWS

VM = pl.BlockSpec(memory_space=pltpu.VMEM)
SM = pl.BlockSpec(memory_space=pltpu.SMEM)
HB = pl.BlockSpec(memory_space=pltpu.HBM)


def dot_nt(a, b):
    return lax.dot_general(a, b, NT, preferred_element_type=F32)


def dot_nn(a, b):
    return lax.dot_general(a, b, NN, preferred_element_type=F32)


def call(body, out_shape, in_specs, out_specs, name, scratch=(), flops=0):
    return pl.pallas_call(
        body,
        out_shape=out_shape,
        in_specs=in_specs,
        out_specs=out_specs,
        scratch_shapes=list(scratch),
        compiler_params=pltpu.CompilerParams(vmem_limit_bytes=VMEM_LIMIT),
        cost_estimate=pl.CostEstimate(flops=flops, transcendentals=0, bytes_accessed=0) if flops else None,
        name=name,
    )


def in_hbm(*arrays):
    return [pltpu.with_memory_space_constraint(a, pltpu.HBM) for a in arrays]


def run_copies(pairs, sem):
    started = [pltpu.make_async_copy(src, dst, sem.at[i]) for i, (src, dst) in enumerate(pairs)]
    for copy in started:
        copy.start()
    for copy in started:
        copy.wait()


def stack_kernel(q_ref, g_ref, k_ref, v_ref, rows_ref, kv_ref, sem):
    pairs = [(k_ref, kv_ref.at[:, 0:HEAD]), (v_ref, kv_ref.at[:, HEAD:2 * HEAD])]
    for h in range(GROUP):
        cols = slice(h * HEAD, (h + 1) * HEAD)
        pairs.append((q_ref.at[:, cols], rows_ref.at[h * BLOCK:(h + 1) * BLOCK, :]))
        pairs.append((g_ref.at[:, cols], rows_ref.at[ROWS + h * BLOCK:ROWS + (h + 1) * BLOCK, :]))
    run_copies(pairs, sem)


def plan_kernel(place_ref, anc_ref, rows_ref, item_ref, list_ref):
    z = place_ref[0]
    y = place_ref[1]
    for j in range(NY):
        query_block = NY * z + ((y - j) & (NY - 1))
        bits = jnp.int32(0)
        for i in range(ANC):
            key_block = anc_ref[query_block, i]
            key_z = key_block >> 2
            slot = 2 * ((z >> 1) - (key_z >> 1)) + ((z ^ key_z) & 1)
            bits = bits | jnp.where((key_block & (NY - 1)) == y, jnp.int32(1) << slot, 0)
        count = jnp.int32(0)
        for r in range(NZ):
            list_ref[count] = r
            count = count + ((bits >> r) & 1)
        for p in range(PAIRS):
            row = PAIRS * j + p
            first = jnp.where(2 * p < count, list_ref[2 * p], 0)
            both = 2 * p + 1 < count
            second = jnp.where(both, list_ref[2 * p + 1], first)
            item_ref[row, 0] = first
            item_ref[row, 1] = second
            causal = jnp.int32(0) if j == 0 else jnp.int32(-BLOCK)
            item_ref[row, 2] = jnp.where(first == 0, causal, -BLOCK)
            item_ref[row, 3] = jnp.where(both, jnp.where(second == 0, causal, -BLOCK), BLOCK)
        item_ref[NY * PAIRS + j, 0] = (count + 1) // 2


def stats_kernel(item_ref, k0, k1, k2, k3, g0, g1, g2, g3, stat_ref, score_ref, pgrad_ref, kv_ref):
    for k, part in enumerate((k0, k1, k2, k3)):
        kv_ref[2 * k] = part[:BLOCK, :]
        kv_ref[2 * k + 1] = part[BLOCK:, :]
    key_row = lax.broadcasted_iota(I32, (BLOCK, ROWS), 0)
    query_row = lax.broadcasted_iota(I32, (BLOCK, ROWS), 1) % BLOCK
    gap = query_row - key_row
    for j, group in enumerate((g0, g1, g2, g3)):

        def step(p, carry, j=j, group=group):
            old, totals, dots = carry
            row = PAIRS * j + p
            first = item_ref[row, 0]
            second = item_ref[row, 1]
            kv = jnp.concatenate([kv_ref[first], kv_ref[second]], axis=0)
            scores = dot_nt(kv[:, :HEAD], group[:ROWS, :]) * FACTOR
            prob_grads = dot_nt(kv[:, HEAD:], group[ROWS:, :])
            upper = jnp.where(gap >= item_ref[row, 2], scores[:BLOCK], MASKED)
            lower = jnp.where(gap >= item_ref[row, 3], scores[BLOCK:], MASKED)
            scores = jnp.concatenate([upper, lower], axis=0)
            score_ref[row] = scores
            pgrad_ref[row] = prob_grads
            highest = jnp.maximum(old, jnp.max(scores, axis=0, keepdims=True))
            weights = jnp.exp(scores - highest)
            shrink = jnp.exp(old - highest)
            totals = totals * shrink + jnp.sum(weights, axis=0, keepdims=True)
            dots = dots * shrink + jnp.sum(weights * prob_grads, axis=0, keepdims=True)
            return highest, totals, dots

        zero = jnp.zeros((1, ROWS), F32)
        start = (jnp.full((1, ROWS), MASKED, F32), zero, zero)
        highest, totals, dots = lax.fori_loop(0, item_ref[NY * PAIRS + j, 0], step, start)
        stat_ref[j, 0:1, :] = highest
        stat_ref[j, 1:2, :] = totals
        stat_ref[j, 2:3, :] = dots
        stat_ref[j, 3:4, :] = zero


def join_kernel(own_ref, beside_ref, pair_ref):
    pair_ref[:BLOCK, :] = own_ref[...]
    pair_ref[BLOCK:, :] = beside_ref[...]


def turn_kernel(k0, k1, k2, k3, stat_ref, key_cols):
    for k, part in enumerate((k0, k1, k2, k3)):
        key_cols[2 * k] = part[:BLOCK, :HEAD].T
        key_cols[2 * k + 1] = part[BLOCK:, :HEAD].T


def grads_kernel(item_ref, cols_ref, score_ref, pgrad_ref, g0, g1, g2, g3, s0, s1, s2, s3,
                 d0, d1, d2, d3, dq0, dq1, dq2, dq3, dk_acc, dv_acc):
    stats = (s0, s1, s2, s3)
    dk_acc[...] = jnp.zeros_like(dk_acc)
    dv_acc[...] = jnp.zeros_like(dv_acc)
    for j, (group, out) in enumerate(zip((g0, g1, g2, g3), (dq0, dq1, dq2, dq3))):
        views = [stats[k][(j - k) % NY] for k in range(NY)]
        maxima = views[0][0:1]
        for k in range(1, NY):
            maxima = jnp.maximum(maxima, views[k][0:1])
        totals = jnp.zeros((1, ROWS), F32)
        dots = jnp.zeros((1, ROWS), F32)
        for k in range(NY):
            shrink = jnp.exp(views[k][0:1] - maxima)
            totals = totals + views[k][1:2] * shrink
            dots = dots + views[k][2:3] * shrink
        log_totals = maxima + jnp.log(totals)
        row_dots = dots / totals

        def step(p, query_grad, j=j, group=group, log_totals=log_totals, row_dots=row_dots):
            row = PAIRS * j + p
            first = item_ref[row, 0]
            second = item_ref[row, 1]
            probs = jnp.exp(score_ref[row] - log_totals)
            score_grads = (probs * (pgrad_ref[row] - row_dots)).astype(BF16)
            dk_pair = dot_nn(score_grads, group[:ROWS, :])
            dv_pair = dot_nn(probs.astype(BF16), group[ROWS:, :])
            dk_acc[first] += dk_pair[:BLOCK]
            dk_acc[second] += dk_pair[BLOCK:]
            dv_acc[first] += dv_pair[:BLOCK]
            dv_acc[second] += dv_pair[BLOCK:]
            cols = jnp.concatenate([cols_ref[first], cols_ref[second]], axis=1)
            return query_grad + dot_nn(cols, score_grads)

        query_grad = lax.fori_loop(0, item_ref[NY * PAIRS + j, 0], step, jnp.zeros((HEAD, ROWS), F32))
        out[...] = (query_grad * FACTOR).astype(BF16)
    for slot in range(NZ):
        out = (d0, d1, d2, d3)[slot // 2]
        rows = slice((slot % 2) * BLOCK, (slot % 2 + 1) * BLOCK)
        out[rows, :HEAD] = (dk_acc[slot] * FACTOR).astype(BF16)
        out[rows, HEAD:] = dv_acc[slot].astype(BF16)


def unrotate(x, cosine, sine):
    front = x[:HEAD // 2]
    back = x[HEAD // 2:]
    return jnp.concatenate([front * cosine + back * sine, back * cosine - front * sine], axis=0)


def weight_rows(place_ref, step):
    core = 1 - place_ref[3] if step < NX else place_ref[3]
    return pl.ds(pl.multiple_of((2 * ((place_ref[2] + step) & (NX - 1)) + core) * ROWS, ROWS), ROWS)


def query_part_kernel(place_ref, cos_ref, sin_ref, q0, q1, q2, q3, wq_hbm, out_ref, wq, sem):
    copies = [
        pltpu.make_async_copy(wq_hbm.at[weight_rows(place_ref, i), :], wq.at[i], sem.at[i]) for i in range(2 * NX)
    ]
    for copy in copies:
        copy.start()
    cosine = cos_ref[...]
    sine = sin_ref[...]
    low = []
    for h in range(GROUP):
        cols = slice(h * HEAD, (h + 1) * HEAD)
        total = q0[:, cols].astype(F32)
        for part in (q1, q2, q3):
            total = total + part[:, cols].astype(F32)
        low.append(unrotate(total, cosine, sine).astype(BF16))
    low = jnp.concatenate(low, axis=0)
    for i, copy in enumerate(copies):
        copy.wait()
        out_ref[i] = dot_nn(wq[i], low)


def fold_kernel(d0, d1, d2, d3, own_ref, beside_ref):
    total = d0[...].astype(F32)
    for part in (d1, d2, d3):
        total = total + part[...].astype(F32)
    own_ref[...] = total[:BLOCK]
    beside_ref[...] = total[BLOCK:].astype(BF16)


def first_half_kernel(place_ref, cos_ref, sin_ref, own_ref, beside_ref, part_ref, wk, wv, out_ref, low_ref):
    total = own_ref[...] + beside_ref[...].astype(F32)
    low_ref[:HEAD, :] = unrotate(total[:, :HEAD].T, cos_ref[...], sin_ref[...]).astype(BF16)
    low_ref[HEAD:, :] = total[:, HEAD:].T.astype(BF16)
    for i in range(NX):
        out_ref[i] = add_key_value(place_ref, i, low_ref, part_ref, wk, wv).astype(BF16)


def second_half_kernel(place_ref, low_ref, part_ref, wk, wv, out_ref):
    for i in range(NX):
        out_ref[i] = add_key_value(place_ref, NX + i, low_ref, part_ref, wk, wv)


def add_key_value(place_ref, step, low_ref, part_ref, wk, wv):
    rows = weight_rows(place_ref, step)
    total = part_ref[step] + dot_nn(wk[rows, :], low_ref[:HEAD, :])
    return total + dot_nn(wv[rows, :], low_ref[HEAD:, :])


def finish_kernel(kept_ref, arrived_ref, p0, p1, p2, out_ref):
    for h in range(GROUP):
        rows = slice(h * HEAD, (h + 1) * HEAD)
        total = kept_ref[rows, :]
        for part in (arrived_ref, p0, p1, p2):
            total = total + part[rows, :].astype(F32)
        out_ref[:, rows] = total.T.astype(BF16)


def shift(size, k):
    return [(i, (i + k) % size) for i in range(size)]


def shards(queries, keys, values, out_grad, ancestry, w_query, key_matrix, value_matrix):
    z, y, x, c = (lax.axis_index(name) for name in "zyxc")
    place = jnp.stack([z, y, x, c]).astype(I32)
    group, kv = call(
        stack_kernel,
        [pltpu.VMEM((2 * ROWS, HEAD), BF16), pltpu.VMEM((BLOCK, 2 * HEAD), BF16)],
        [HB] * 4,
        [VM] * 2,
        "stack",
        [pltpu.SemaphoreType.DMA((2 * GROUP + 2,))],
    )(*in_hbm(queries, out_grad, keys, values))
    groups = [group] + [lax.ppermute(group, "y", shift(NY, k)) for k in range(1, NY)]
    beside = [(i, i ^ 1) for i in range(NZ)]
    pair_shape = pltpu.VMEM((2 * BLOCK, 2 * HEAD), BF16)
    pair = call(join_kernel, pair_shape, [VM] * 2, VM, "join")(kv, lax.ppermute(kv, "z", beside))
    strides = range(2, NZ, 2)
    kvs = [pair] + [lax.ppermute(pair, "z", [(i, i + k) for i in range(NZ - k)]) for k in strides]

    own_block = NY * z + y
    own_row = lax.dynamic_slice_in_dim(ancestry, own_block, 1, 0)
    depth = jnp.sum((own_row != own_block).astype(I32))
    token_places = (BLOCK * depth + jnp.arange(BLOCK, dtype=I32)).astype(F32)
    frequencies = jnp.exp(jnp.arange(HEAD // 2, dtype=F32) * (-2.0 * math.log(ROPE_BASE) / HEAD))
    angles = frequencies[:, None] * token_places[None, :]
    cosine = jnp.cos(angles)
    sine = jnp.sin(angles)
    items = call(
        plan_kernel,
        jax.ShapeDtypeStruct((NY * PAIRS + NY, 4), I32),
        [SM, SM, VM],
        SM,
        "plan",
        [pltpu.SMEM((NZ + 1,), I32)],
    )(place, ancestry, group)
    items, cosine, sine = lax.optimization_barrier((items, cosine, sine))

    tiles = (NY * PAIRS, 2 * BLOCK, ROWS)
    stats, scores, prob_grads = call(
        stats_kernel,
        [jax.ShapeDtypeStruct((NY, 4, ROWS), F32), pltpu.VMEM(tiles, F32), pltpu.VMEM(tiles, F32)],
        [SM] + [VM] * (NZ // 2 + NY),
        [VM] * 3,
        "stats",
        [pltpu.VMEM((NZ, BLOCK, 2 * HEAD), BF16)],
        STATS_FLOPS,
    )(items, *kvs, *groups)
    all_stats = [stats] + [lax.ppermute(stats, "y", shift(NY, k)) for k in range(1, NY)]
    key_cols = call(
        turn_kernel, pltpu.VMEM((NZ, HEAD, BLOCK), BF16), [VM] * (NZ // 2 + 1), VM, "turn",
    )(*kvs, stats)
    grads = call(
        grads_kernel,
        [pair_shape] * (NZ // 2) + [pltpu.VMEM((HEAD, ROWS), BF16)] * NY,
        [SM] + [VM] * (3 + 2 * NY),
        [VM] * (NZ // 2 + NY),
        "grads",
        [pltpu.VMEM((NZ, BLOCK, HEAD), F32), pltpu.VMEM((NZ, BLOCK, HEAD), F32)],
        GRADS_FLOPS,
    )(items, key_cols, scores, prob_grads, *groups, *all_stats)
    dkv_parts, dq_parts = grads[:NZ // 2], grads[NZ // 2:]
    dq_own = [dq_parts[0]] + [lax.ppermute(dq_parts[k], "y", shift(NY, -k)) for k in range(1, NY)]
    dkv_sent = [
        lax.ppermute(part, "z", [(i, i - k) for i in range(k, NZ)]) for k, part in zip(strides, dkv_parts[1:])
    ]
    own_sum, beside_sum = call(
        fold_kernel,
        [pltpu.VMEM((BLOCK, 2 * HEAD), F32), pltpu.VMEM((BLOCK, 2 * HEAD), BF16)],
        [VM] * (NZ // 2),
        [VM] * 2,
        "fold",
    )(dkv_parts[0], *dkv_sent)
    beside_sum = lax.ppermute(beside_sum, "z", beside)

    query_part = call(
        query_part_kernel,
        pltpu.VMEM((2 * NX, ROWS, BLOCK), F32),
        [SM] + [VM] * (2 + NY) + [HB],
        VM,
        "query_part",
        [pltpu.VMEM((2 * NX, ROWS, ROWS), BF16), pltpu.SemaphoreType.DMA((2 * NX,))],
        QUERY_FLOPS,
    )(place, cosine, sine, *dq_own, *in_hbm(w_query))
    away, low = call(
        first_half_kernel,
        [pltpu.VMEM((NX, ROWS, BLOCK), BF16), pltpu.VMEM((2 * HEAD, BLOCK), BF16)],
        [SM] + [VM] * 7,
        [VM, VM],
        "first_half",
    )(place, cosine, sine, own_sum, beside_sum, query_part, key_matrix, value_matrix)
    arrived = lax.ppermute(away, "c", shift(NC, 1))
    kept = call(
        second_half_kernel,
        pltpu.VMEM((NX, ROWS, BLOCK), F32),
        [SM] + [VM] * 4,
        VM,
        "second_half",
    )(place, low, query_part, key_matrix, value_matrix)
    sent = [(kept[k] + arrived[k].astype(F32)).astype(BF16) for k in range(1, NX)]
    parts = [lax.ppermute(sent[k - 1], "x", shift(NX, k)) for k in range(1, NX)]
    return call(
        finish_kernel, jax.ShapeDtypeStruct((BLOCK, ROWS), BF16), [VM] * (2 + len(parts)), VM, "finish",
    )(kept[0], arrived[0], *parts)


def solution(mesh):
    grid = Mesh(mesh.devices.reshape(NZ, NY, NX, NC), ("z", "y", "x", "c"))
    split = P(("z", "y"), ("x", "c"))
    weight = P(None, ("x", "c"))
    return jax.shard_map(
        shards,
        mesh=grid,
        in_specs=(split, split, split, split, P(), weight, weight, weight),
        out_specs=split,
        check_vma=False,
    )
```

```python
import math

import jax
import jax.numpy as jnp
from jax import lax
from jax.experimental import pallas as pl
from jax.experimental.pallas import tpu as pltpu
from jax.sharding import Mesh, PartitionSpec as P

HEAD = 128
BLOCK = 128
GROUP = 5
ROWS = GROUP * BLOCK
NZ, NY, NX, NC = 8, 4, 4, 2
PAIRS = NZ // 2
ANC = 17
ROPE_BASE = 1000000.0
MASKED = -1e30
FACTOR = HEAD ** -0.5
NT = (((1,), (1,)), ((), ()))
NN = (((1,), (0,)), ((), ()))
F32, BF16, I32 = jnp.float32, jnp.bfloat16, jnp.int32
VMEM_LIMIT = 16 << 20
STATS_FLOPS = 2 * 2 * (NY * ROWS) * (NZ * BLOCK) * HEAD
GRADS_FLOPS = 3 * 2 * (NY * ROWS) * (NZ * BLOCK) * HEAD
QUERY_FLOPS = 2 * BLOCK * ROWS * 2 * NX * ROWS

VM = pl.BlockSpec(memory_space=pltpu.VMEM)
SM = pl.BlockSpec(memory_space=pltpu.SMEM)
HB = pl.BlockSpec(memory_space=pltpu.HBM)


def dot_nt(a, b):
    return lax.dot_general(a, b, NT, preferred_element_type=F32)


def dot_nn(a, b):
    return lax.dot_general(a, b, NN, preferred_element_type=F32)


def call(body, out_shape, in_specs, out_specs, name, scratch=(), flops=0):
    return pl.pallas_call(
        body,
        out_shape=out_shape,
        in_specs=in_specs,
        out_specs=out_specs,
        scratch_shapes=list(scratch),
        compiler_params=pltpu.CompilerParams(vmem_limit_bytes=VMEM_LIMIT),
        cost_estimate=pl.CostEstimate(flops=flops, transcendentals=0, bytes_accessed=0) if flops else None,
        name=name,
    )


def in_hbm(*arrays):
    return [pltpu.with_memory_space_constraint(a, pltpu.HBM) for a in arrays]


def run_copies(pairs, sem):
    started = [pltpu.make_async_copy(src, dst, sem.at[i]) for i, (src, dst) in enumerate(pairs)]
    for copy in started:
        copy.start()
    for copy in started:
        copy.wait()


def stack_kernel(q_ref, g_ref, k_ref, v_ref, rows_ref, kv_ref, sem):
    pairs = [(k_ref, kv_ref.at[:, 0:HEAD]), (v_ref, kv_ref.at[:, HEAD:2 * HEAD])]
    for h in range(GROUP):
        cols = slice(h * HEAD, (h + 1) * HEAD)
        pairs.append((q_ref.at[:, cols], rows_ref.at[h * BLOCK:(h + 1) * BLOCK, :]))
        pairs.append((g_ref.at[:, cols], rows_ref.at[ROWS + h * BLOCK:ROWS + (h + 1) * BLOCK, :]))
    run_copies(pairs, sem)


def plan_kernel(place_ref, anc_ref, rows_ref, item_ref, list_ref):
    z = place_ref[0]
    y = place_ref[1]
    for j in range(NY):
        query_block = NY * z + ((y - j) & (NY - 1))
        bits = jnp.int32(0)
        for i in range(ANC):
            key_block = anc_ref[query_block, i]
            bits = bits | jnp.where((key_block & (NY - 1)) == y, jnp.int32(1) << (key_block >> 2), 0)
        count = jnp.int32(0)
        for key_z in range(NZ):
            list_ref[count] = key_z
            count = count + ((bits >> key_z) & 1)
        for p in range(PAIRS):
            row = PAIRS * j + p
            first = jnp.where(2 * p < count, list_ref[2 * p], 0)
            both = 2 * p + 1 < count
            second = jnp.where(both, list_ref[2 * p + 1], first)
            item_ref[row, 0] = first
            item_ref[row, 1] = second
            causal = jnp.int32(0) if j == 0 else jnp.int32(-BLOCK)
            item_ref[row, 2] = jnp.where(first == z, causal, -BLOCK)
            item_ref[row, 3] = jnp.where(both, jnp.where(second == z, causal, -BLOCK), BLOCK)
        item_ref[NY * PAIRS + j, 0] = (count + 1) // 2


def stats_kernel(item_ref, kv_ref, g0, g1, g2, g3, stat_ref, score_ref, pgrad_ref):
    key_row = lax.broadcasted_iota(I32, (BLOCK, ROWS), 0)
    query_row = lax.broadcasted_iota(I32, (BLOCK, ROWS), 1) % BLOCK
    gap = query_row - key_row
    for j, group in enumerate((g0, g1, g2, g3)):

        def step(p, carry, j=j, group=group):
            old, totals, dots = carry
            row = PAIRS * j + p
            first = item_ref[row, 0]
            second = item_ref[row, 1]
            kv = jnp.concatenate([kv_ref[first], kv_ref[second]], axis=0)
            scores = dot_nt(kv[:, :HEAD], group[:ROWS, :]) * FACTOR
            prob_grads = dot_nt(kv[:, HEAD:], group[ROWS:, :])
            upper = jnp.where(gap >= item_ref[row, 2], scores[:BLOCK], MASKED)
            lower = jnp.where(gap >= item_ref[row, 3], scores[BLOCK:], MASKED)
            scores = jnp.concatenate([upper, lower], axis=0)
            score_ref[row] = scores
            pgrad_ref[row] = prob_grads
            highest = jnp.maximum(old, jnp.max(scores, axis=0, keepdims=True))
            weights = jnp.exp(scores - highest)
            shrink = jnp.exp(old - highest)
            totals = totals * shrink + jnp.sum(weights, axis=0, keepdims=True)
            dots = dots * shrink + jnp.sum(weights * prob_grads, axis=0, keepdims=True)
            return highest, totals, dots

        zero = jnp.zeros((1, ROWS), F32)
        start = (jnp.full((1, ROWS), MASKED, F32), zero, zero)
        highest, totals, dots = lax.fori_loop(0, item_ref[NY * PAIRS + j, 0], step, start)
        stat_ref[j, 0:1, :] = highest
        stat_ref[j, 1:2, :] = totals
        stat_ref[j, 2:3, :] = dots
        stat_ref[j, 3:4, :] = zero


def turn_kernel(kv_ref, stat_ref, key_cols):
    for a in range(NZ):
        key_cols[a] = kv_ref[a, :, :HEAD].T


def flush_kernel(low_ref, out_ref, sem):
    run_copies([(low_ref, out_ref)], sem)


def grads_kernel(item_ref, cols_ref, score_ref, pgrad_ref, g0, g1, g2, g3, s0, s1, s2, s3,
                 dkv_ref, dq0, dq1, dq2, dq3, dk_acc, dv_acc):
    stats = (s0, s1, s2, s3)
    dk_acc[...] = jnp.zeros_like(dk_acc)
    dv_acc[...] = jnp.zeros_like(dv_acc)
    for j, (group, out) in enumerate(zip((g0, g1, g2, g3), (dq0, dq1, dq2, dq3))):
        views = [stats[k][(j - k) % NY] for k in range(NY)]
        maxima = views[0][0:1]
        for k in range(1, NY):
            maxima = jnp.maximum(maxima, views[k][0:1])
        totals = jnp.zeros((1, ROWS), F32)
        dots = jnp.zeros((1, ROWS), F32)
        for k in range(NY):
            shrink = jnp.exp(views[k][0:1] - maxima)
            totals = totals + views[k][1:2] * shrink
            dots = dots + views[k][2:3] * shrink
        log_totals = maxima + jnp.log(totals)
        row_dots = dots / totals

        def step(p, query_grad, j=j, group=group, log_totals=log_totals, row_dots=row_dots):
            row = PAIRS * j + p
            first = item_ref[row, 0]
            second = item_ref[row, 1]
            probs = jnp.exp(score_ref[row] - log_totals)
            score_grads = (probs * (pgrad_ref[row] - row_dots)).astype(BF16)
            dk_pair = dot_nn(score_grads, group[:ROWS, :])
            dv_pair = dot_nn(probs.astype(BF16), group[ROWS:, :])
            dk_acc[first] += dk_pair[:BLOCK]
            dk_acc[second] += dk_pair[BLOCK:]
            dv_acc[first] += dv_pair[:BLOCK]
            dv_acc[second] += dv_pair[BLOCK:]
            cols = jnp.concatenate([cols_ref[first], cols_ref[second]], axis=1)
            return query_grad + dot_nn(cols, score_grads)

        query_grad = lax.fori_loop(0, item_ref[NY * PAIRS + j, 0], step, jnp.zeros((HEAD, ROWS), F32))
        out[...] = (query_grad * FACTOR).astype(BF16)
    for a in range(NZ):
        dkv_ref[a, :, :HEAD] = (dk_acc[a] * FACTOR).astype(BF16)
        dkv_ref[a, :, HEAD:] = dv_acc[a].astype(BF16)


def unrotate(x, cosine, sine):
    front = x[:HEAD // 2]
    back = x[HEAD // 2:]
    return jnp.concatenate([front * cosine + back * sine, back * cosine - front * sine], axis=0)


def weight_rows(place_ref, step):
    core = 1 - place_ref[3] if step < NX else place_ref[3]
    return pl.ds(pl.multiple_of((2 * ((place_ref[2] + step) & (NX - 1)) + core) * ROWS, ROWS), ROWS)


def fetch_kernel(place_ref, dq_ref, wq_hbm, *refs):
    blocks, sem = refs[:-1], refs[-1]
    run_copies([(wq_hbm.at[weight_rows(place_ref, i), :], block) for i, block in enumerate(blocks)], sem)


def start_pair(place_ref, first, wk_hbm, wv_hbm, wk, wv, sem):
    copies = []
    for i in range(NX):
        rows = weight_rows(place_ref, first + i)
        copies.append(pltpu.make_async_copy(wk_hbm.at[rows, :], wk.at[i], sem.at[2 * i]))
        copies.append(pltpu.make_async_copy(wv_hbm.at[rows, :], wv.at[i], sem.at[2 * i + 1]))
    for copy in copies:
        copy.start()
    return copies


def query_part_kernel(place_ref, cos_ref, sin_ref, q0, q1, q2, q3, wk_hbm, wv_hbm, *refs):
    blocks, out_ref, wk, wv, sem = refs[:2 * NX], *refs[2 * NX:]
    copies = start_pair(place_ref, 0, wk_hbm, wv_hbm, wk, wv, sem)
    cosine = cos_ref[...]
    sine = sin_ref[...]
    low = []
    for h in range(GROUP):
        cols = slice(h * HEAD, (h + 1) * HEAD)
        total = q0[:, cols].astype(F32)
        for part in (q1, q2, q3):
            total = total + part[:, cols].astype(F32)
        low.append(unrotate(total, cosine, sine).astype(BF16))
    low = jnp.concatenate(low, axis=0)
    for i, block in enumerate(blocks):
        out_ref[i] = dot_nn(block[...], low).astype(BF16)
    for copy in copies:
        copy.wait()


def first_half_kernel(place_ref, cos_ref, sin_ref, dkv_ref, part_ref, wk, wv, wk_hbm, wv_hbm,
                      out_ref, low_ref, wk_kept, wv_kept, sem):
    copies = start_pair(place_ref, NX, wk_hbm, wv_hbm, wk_kept, wv_kept, sem)
    total = dkv_ref[0].astype(F32)
    for a in range(1, NZ):
        total = total + dkv_ref[a].astype(F32)
    low_ref[:HEAD, :] = unrotate(total[:, :HEAD].T, cos_ref[...], sin_ref[...]).astype(BF16)
    low_ref[HEAD:, :] = total[:, HEAD:].T.astype(BF16)
    for i in range(NX):
        out_ref[i] = (part_ref[i] + key_value_part(low_ref, wk[i], wv[i])).astype(BF16)
    for copy in copies:
        copy.wait()


def second_half_kernel(low_ref, part_ref, wk, wv, out_ref):
    for i in range(NX):
        out_ref[i] = part_ref[NX + i] + key_value_part(low_ref, wk[i], wv[i])


def key_value_part(low_ref, wk, wv):
    return dot_nn(wk, low_ref[:HEAD, :]) + dot_nn(wv, low_ref[HEAD:, :])


def finish_kernel(kept_ref, arrived_ref, p0, p1, p2, out_ref):
    for h in range(GROUP):
        rows = slice(h * HEAD, (h + 1) * HEAD)
        total = kept_ref[rows, :]
        for part in (arrived_ref, p0, p1, p2):
            total = total + part[rows, :].astype(F32)
        out_ref[:, rows] = total.T.astype(BF16)


def shift(size, k):
    return [(i, (i + k) % size) for i in range(size)]


def shards(queries, keys, values, out_grad, ancestry, w_query, key_matrix, value_matrix):
    z, y, x, c = (lax.axis_index(name) for name in "zyxc")
    place = jnp.stack([z, y, x, c]).astype(I32)
    group, kv = call(
        stack_kernel,
        [pltpu.VMEM((2 * ROWS, HEAD), BF16), pltpu.VMEM((BLOCK, 2 * HEAD), BF16)],
        [HB] * 4,
        [VM] * 2,
        "stack",
        [pltpu.SemaphoreType.DMA((2 * GROUP + 2,))],
    )(*in_hbm(queries, out_grad, keys, values))
    groups = [group] + [lax.ppermute(group, "y", shift(NY, k)) for k in range(1, NY)]
    kv_all = lax.all_gather(kv, "z", axis=0, tiled=False)

    own_block = NY * z + y
    own_row = lax.dynamic_slice_in_dim(ancestry, own_block, 1, 0)
    depth = jnp.sum((own_row != own_block).astype(I32))
    token_places = (BLOCK * depth + jnp.arange(BLOCK, dtype=I32)).astype(F32)
    frequencies = jnp.exp(jnp.arange(HEAD // 2, dtype=F32) * (-2.0 * math.log(ROPE_BASE) / HEAD))
    angles = frequencies[:, None] * token_places[None, :]
    cosine = jnp.cos(angles)
    sine = jnp.sin(angles)
    items = call(
        plan_kernel,
        jax.ShapeDtypeStruct((NY * PAIRS + NY, 4), I32),
        [SM, SM, VM],
        SM,
        "plan",
        [pltpu.SMEM((NZ + 1,), I32)],
    )(place, ancestry, group)
    items, cosine, sine = lax.optimization_barrier((items, cosine, sine))

    tiles = (NY * PAIRS, 2 * BLOCK, ROWS)
    stats, scores, prob_grads = call(
        stats_kernel,
        [jax.ShapeDtypeStruct((NY, 4, ROWS), F32), pltpu.VMEM(tiles, F32), pltpu.VMEM(tiles, F32)],
        [SM] + [VM] * (1 + NY),
        [VM] * 3,
        "stats",
        (),
        STATS_FLOPS,
    )(items, kv_all, *groups)
    all_stats = [stats] + [lax.ppermute(stats, "y", shift(NY, k)) for k in range(1, NY)]
    key_cols = call(
        turn_kernel, pltpu.VMEM((NZ, HEAD, BLOCK), BF16), [VM] * 2, VM, "turn",
    )(kv_all, stats)
    dkv, *dq_parts = call(
        grads_kernel,
        [pltpu.VMEM((NZ, BLOCK, 2 * HEAD), BF16)] + [pltpu.VMEM((HEAD, ROWS), BF16)] * NY,
        [SM] + [VM] * (3 + 2 * NY),
        [VM] * (1 + NY),
        "grads",
        [pltpu.VMEM((NZ, BLOCK, HEAD), F32), pltpu.VMEM((NZ, BLOCK, HEAD), F32)],
        GRADS_FLOPS,
    )(items, key_cols, scores, prob_grads, *groups, *all_stats)
    dq_own = [dq_parts[0]] + [lax.ppermute(dq_parts[k], "y", shift(NY, -k)) for k in range(1, NY)]
    dkv = call(
        flush_kernel, pltpu.HBM(dkv.shape, BF16), [VM], HB, "flush", [pltpu.SemaphoreType.DMA((1,))],
    )(dkv)
    dkv_own = lax.all_to_all(dkv, "z", 0, 0, tiled=True)

    wq, wk, wv = in_hbm(w_query, key_matrix, value_matrix)
    blocks = call(
        fetch_kernel,
        [pltpu.VMEM((ROWS, ROWS), BF16)] * (2 * NX),
        [SM, VM, HB],
        [VM] * (2 * NX),
        "fetch",
        [pltpu.SemaphoreType.DMA((2 * NX,))],
    )(place, dq_parts[0], wq)
    pair_shapes = [pltpu.VMEM((NX, ROWS, HEAD), BF16)] * 2
    query_part, wk_away, wv_away = call(
        query_part_kernel,
        [pltpu.VMEM((2 * NX, ROWS, BLOCK), BF16)] + pair_shapes,
        [SM] + [VM] * (2 + NY) + [HB] * 2 + [VM] * (2 * NX),
        [VM] * 3,
        "query_part",
        [pltpu.SemaphoreType.DMA((2 * NX,))],
        QUERY_FLOPS,
    )(place, cosine, sine, *dq_own, wk, wv, *blocks)
    away, low, wk_kept, wv_kept = call(
        first_half_kernel,
        [pltpu.VMEM((NX, ROWS, BLOCK), BF16), pltpu.VMEM((2 * HEAD, BLOCK), BF16)] + pair_shapes,
        [SM] + [VM] * 6 + [HB] * 2,
        [VM] * 4,
        "first_half",
        [pltpu.SemaphoreType.DMA((2 * NX,))],
    )(place, cosine, sine, dkv_own, query_part, wk_away, wv_away, wk, wv)
    arrived = lax.ppermute(away, "c", shift(NC, 1))
    kept = call(
        second_half_kernel,
        pltpu.VMEM((NX, ROWS, BLOCK), F32),
        [VM] * 4,
        VM,
        "second_half",
    )(low, query_part, wk_kept, wv_kept)
    sent = [(kept[k] + arrived[k].astype(F32)).astype(BF16) for k in range(1, NX)]
    parts = [lax.ppermute(sent[k - 1], "x", shift(NX, k)) for k in range(1, NX)]
    return call(
        finish_kernel, jax.ShapeDtypeStruct((BLOCK, ROWS), BF16), [VM] * (2 + len(parts)), VM, "finish",
    )(kept[0], arrived[0], *parts)


def solution(mesh):
    grid = Mesh(mesh.devices.reshape(NZ, NY, NX, NC), ("z", "y", "x", "c"))
    split = P(("z", "y"), ("x", "c"))
    weight = P(None, ("x", "c"))
    return jax.shard_map(
        shards,
        mesh=grid,
        in_specs=(split, split, split, split, P(), weight, weight, weight),
        out_specs=split,
        check_vma=False,
    )
```

```python
import math

import jax
import jax.numpy as jnp
from jax import lax
from jax.experimental import pallas as pl
from jax.experimental.pallas import tpu as pltpu
from jax.sharding import Mesh, PartitionSpec as P

HEAD = 128
BLOCK = 128
GROUP = 5
ROWS = GROUP * BLOCK
NZ, NY, NX, NC = 8, 4, 4, 2
PAIRS = NZ // 2
ANC = 17
ROPE_BASE = 1000000.0
MASKED = -1e30
FACTOR = HEAD ** -0.5
NT = (((1,), (1,)), ((), ()))
NN = (((1,), (0,)), ((), ()))
F32, BF16, I32 = jnp.float32, jnp.bfloat16, jnp.int32
VMEM_LIMIT = 16 << 20
STATS_FLOPS = 2 * 2 * (NY * ROWS) * (NZ * BLOCK) * HEAD
GRADS_FLOPS = 3 * 2 * (NY * ROWS) * (NZ * BLOCK) * HEAD
QUERY_FLOPS = 2 * BLOCK * ROWS * 2 * NX * ROWS

VM = pl.BlockSpec(memory_space=pltpu.VMEM)
SM = pl.BlockSpec(memory_space=pltpu.SMEM)
HB = pl.BlockSpec(memory_space=pltpu.HBM)


def dot_nt(a, b):
    return lax.dot_general(a, b, NT, preferred_element_type=F32)


def dot_nn(a, b):
    return lax.dot_general(a, b, NN, preferred_element_type=F32)


def call(body, out_shape, in_specs, out_specs, name, scratch=(), flops=0):
    return pl.pallas_call(
        body,
        out_shape=out_shape,
        in_specs=in_specs,
        out_specs=out_specs,
        scratch_shapes=list(scratch),
        compiler_params=pltpu.CompilerParams(vmem_limit_bytes=VMEM_LIMIT),
        cost_estimate=pl.CostEstimate(flops=flops, transcendentals=0, bytes_accessed=0) if flops else None,
        name=name,
    )


def in_hbm(*arrays):
    return [pltpu.with_memory_space_constraint(a, pltpu.HBM) for a in arrays]


def run_copies(pairs, sem):
    started = [pltpu.make_async_copy(src, dst, sem.at[i]) for i, (src, dst) in enumerate(pairs)]
    for copy in started:
        copy.start()
    for copy in started:
        copy.wait()


def stack_kernel(q_ref, g_ref, k_ref, v_ref, rows_ref, kv_ref, sem):
    pairs = [(k_ref, kv_ref.at[:, 0:HEAD]), (v_ref, kv_ref.at[:, HEAD:2 * HEAD])]
    for h in range(GROUP):
        cols = slice(h * HEAD, (h + 1) * HEAD)
        pairs.append((q_ref.at[:, cols], rows_ref.at[h * BLOCK:(h + 1) * BLOCK, :]))
        pairs.append((g_ref.at[:, cols], rows_ref.at[ROWS + h * BLOCK:ROWS + (h + 1) * BLOCK, :]))
    run_copies(pairs, sem)


def plan_kernel(place_ref, anc_ref, rows_ref, item_ref, list_ref):
    z = place_ref[0]
    y = place_ref[1]
    for j in range(NY):
        query_block = NY * z + ((y - j) & (NY - 1))
        bits = jnp.int32(0)
        for i in range(ANC):
            key_block = anc_ref[query_block, i]
            bits = bits | jnp.where((key_block & (NY - 1)) == y, jnp.int32(1) << (key_block >> 2), 0)
        count = jnp.int32(0)
        for key_z in range(NZ):
            list_ref[count] = key_z
            count = count + ((bits >> key_z) & 1)
        for p in range(PAIRS):
            row = PAIRS * j + p
            first = jnp.where(2 * p < count, list_ref[2 * p], 0)
            both = 2 * p + 1 < count
            second = jnp.where(both, list_ref[2 * p + 1], first)
            item_ref[row, 0] = first
            item_ref[row, 1] = second
            causal = jnp.int32(0) if j == 0 else jnp.int32(-BLOCK)
            item_ref[row, 2] = jnp.where(first == z, causal, -BLOCK)
            item_ref[row, 3] = jnp.where(both, jnp.where(second == z, causal, -BLOCK), BLOCK)
        item_ref[NY * PAIRS + j, 0] = (count + 1) // 2
        item_ref[NY * PAIRS + j, 1] = z


def stats_kernel(item_ref, k0, k1, k2, k3, k4, k5, k6, k7, g0, g1, g2, g3, stat_ref, score_ref, pgrad_ref, kv_ref):
    z = item_ref[NY * PAIRS, 1]
    for r, part in enumerate((k0, k1, k2, k3, k4, k5, k6, k7)):
        kv_ref[(z - r) & (NZ - 1)] = part[...]
    key_row = lax.broadcasted_iota(I32, (BLOCK, ROWS), 0)
    query_row = lax.broadcasted_iota(I32, (BLOCK, ROWS), 1) % BLOCK
    gap = query_row - key_row
    for j, group in enumerate((g0, g1, g2, g3)):

        def step(p, carry, j=j, group=group):
            old, totals, dots = carry
            row = PAIRS * j + p
            first = item_ref[row, 0]
            second = item_ref[row, 1]
            kv = jnp.concatenate([kv_ref[first], kv_ref[second]], axis=0)
            scores = dot_nt(kv[:, :HEAD], group[:ROWS, :]) * FACTOR
            prob_grads = dot_nt(kv[:, HEAD:], group[ROWS:, :])
            upper = jnp.where(gap >= item_ref[row, 2], scores[:BLOCK], MASKED)
            lower = jnp.where(gap >= item_ref[row, 3], scores[BLOCK:], MASKED)
            scores = jnp.concatenate([upper, lower], axis=0)
            score_ref[row] = scores
            pgrad_ref[row] = prob_grads
            highest = jnp.maximum(old, jnp.max(scores, axis=0, keepdims=True))
            weights = jnp.exp(scores - highest)
            shrink = jnp.exp(old - highest)
            totals = totals * shrink + jnp.sum(weights, axis=0, keepdims=True)
            dots = dots * shrink + jnp.sum(weights * prob_grads, axis=0, keepdims=True)
            return highest, totals, dots

        zero = jnp.zeros((1, ROWS), F32)
        start = (jnp.full((1, ROWS), MASKED, F32), zero, zero)
        highest, totals, dots = lax.fori_loop(0, item_ref[NY * PAIRS + j, 0], step, start)
        stat_ref[j, 0:1, :] = highest
        stat_ref[j, 1:2, :] = totals
        stat_ref[j, 2:3, :] = dots
        stat_ref[j, 3:4, :] = zero


def turn_kernel(item_ref, k0, k1, k2, k3, k4, k5, k6, k7, stat_ref, key_cols):
    z = item_ref[NY * PAIRS, 1]
    for r, part in enumerate((k0, k1, k2, k3, k4, k5, k6, k7)):
        key_cols[(z - r) & (NZ - 1)] = part[:, :HEAD].T


def flush_kernel(low_ref, out_ref, sem):
    run_copies([(low_ref, out_ref)], sem)


def grads_kernel(item_ref, cols_ref, score_ref, pgrad_ref, g0, g1, g2, g3, s0, s1, s2, s3,
                 dkv_ref, dq0, dq1, dq2, dq3, dk_acc, dv_acc):
    stats = (s0, s1, s2, s3)
    dk_acc[...] = jnp.zeros_like(dk_acc)
    dv_acc[...] = jnp.zeros_like(dv_acc)
    for j, (group, out) in enumerate(zip((g0, g1, g2, g3), (dq0, dq1, dq2, dq3))):
        views = [stats[k][(j - k) % NY] for k in range(NY)]
        maxima = views[0][0:1]
        for k in range(1, NY):
            maxima = jnp.maximum(maxima, views[k][0:1])
        totals = jnp.zeros((1, ROWS), F32)
        dots = jnp.zeros((1, ROWS), F32)
        for k in range(NY):
            shrink = jnp.exp(views[k][0:1] - maxima)
            totals = totals + views[k][1:2] * shrink
            dots = dots + views[k][2:3] * shrink
        log_totals = maxima + jnp.log(totals)
        row_dots = dots / totals

        def step(p, query_grad, j=j, group=group, log_totals=log_totals, row_dots=row_dots):
            row = PAIRS * j + p
            first = item_ref[row, 0]
            second = item_ref[row, 1]
            probs = jnp.exp(score_ref[row] - log_totals)
            score_grads = (probs * (pgrad_ref[row] - row_dots)).astype(BF16)
            dk_pair = dot_nn(score_grads, group[:ROWS, :])
            dv_pair = dot_nn(probs.astype(BF16), group[ROWS:, :])
            dk_acc[first] += dk_pair[:BLOCK]
            dk_acc[second] += dk_pair[BLOCK:]
            dv_acc[first] += dv_pair[:BLOCK]
            dv_acc[second] += dv_pair[BLOCK:]
            cols = jnp.concatenate([cols_ref[first], cols_ref[second]], axis=1)
            return query_grad + dot_nn(cols, score_grads)

        query_grad = lax.fori_loop(0, item_ref[NY * PAIRS + j, 0], step, jnp.zeros((HEAD, ROWS), F32))
        out[...] = (query_grad * FACTOR).astype(BF16)
    for a in range(NZ):
        dkv_ref[a, :, :HEAD] = (dk_acc[a] * FACTOR).astype(BF16)
        dkv_ref[a, :, HEAD:] = dv_acc[a].astype(BF16)


def unrotate(x, cosine, sine):
    front = x[:HEAD // 2]
    back = x[HEAD // 2:]
    return jnp.concatenate([front * cosine + back * sine, back * cosine - front * sine], axis=0)


def weight_rows(place_ref, step):
    core = 1 - place_ref[3] if step < NX else place_ref[3]
    return pl.ds(pl.multiple_of((2 * ((place_ref[2] + step) & (NX - 1)) + core) * ROWS, ROWS), ROWS)


def fetch_kernel(place_ref, dq_ref, wq_hbm, *refs):
    blocks, sem = refs[:-1], refs[-1]
    run_copies([(wq_hbm.at[weight_rows(place_ref, i), :], block) for i, block in enumerate(blocks)], sem)


def start_pair(place_ref, first, wk_hbm, wv_hbm, wk, wv, sem):
    copies = []
    for i in range(NX):
        rows = weight_rows(place_ref, first + i)
        copies.append(pltpu.make_async_copy(wk_hbm.at[rows, :], wk.at[i], sem.at[2 * i]))
        copies.append(pltpu.make_async_copy(wv_hbm.at[rows, :], wv.at[i], sem.at[2 * i + 1]))
    for copy in copies:
        copy.start()
    return copies


def query_part_kernel(place_ref, cos_ref, sin_ref, q0, q1, q2, q3, wk_hbm, wv_hbm, *refs):
    blocks, out_ref, wk, wv, sem = refs[:2 * NX], *refs[2 * NX:]
    copies = start_pair(place_ref, 0, wk_hbm, wv_hbm, wk, wv, sem)
    cosine = cos_ref[...]
    sine = sin_ref[...]
    low = []
    for h in range(GROUP):
        cols = slice(h * HEAD, (h + 1) * HEAD)
        total = q0[:, cols].astype(F32)
        for part in (q1, q2, q3):
            total = total + part[:, cols].astype(F32)
        low.append(unrotate(total, cosine, sine).astype(BF16))
    low = jnp.concatenate(low, axis=0)
    for i, block in enumerate(blocks):
        out_ref[i] = dot_nn(block[...], low).astype(BF16)
    for copy in copies:
        copy.wait()


def first_half_kernel(place_ref, cos_ref, sin_ref, dkv_ref, part_ref, wk, wv, wk_hbm, wv_hbm,
                      out_ref, low_ref, wk_kept, wv_kept, sem):
    copies = start_pair(place_ref, NX, wk_hbm, wv_hbm, wk_kept, wv_kept, sem)
    total = dkv_ref[0].astype(F32)
    for a in range(1, NZ):
        total = total + dkv_ref[a].astype(F32)
    low_ref[:HEAD, :] = unrotate(total[:, :HEAD].T, cos_ref[...], sin_ref[...]).astype(BF16)
    low_ref[HEAD:, :] = total[:, HEAD:].T.astype(BF16)
    for i in range(NX):
        out_ref[i] = (part_ref[i] + key_value_part(low_ref, wk[i], wv[i])).astype(BF16)
    for copy in copies:
        copy.wait()


def second_half_kernel(low_ref, part_ref, wk, wv, out_ref):
    for i in range(NX):
        out_ref[i] = part_ref[NX + i] + key_value_part(low_ref, wk[i], wv[i])


def key_value_part(low_ref, wk, wv):
    return dot_nn(wk, low_ref[:HEAD, :]) + dot_nn(wv, low_ref[HEAD:, :])


def finish_kernel(kept_ref, arrived_ref, p0, p1, p2, out_ref):
    for h in range(GROUP):
        rows = slice(h * HEAD, (h + 1) * HEAD)
        total = kept_ref[rows, :]
        for part in (arrived_ref, p0, p1, p2):
            total = total + part[rows, :].astype(F32)
        out_ref[:, rows] = total.T.astype(BF16)


def shift(size, k):
    return [(i, (i + k) % size) for i in range(size)]


def shards(queries, keys, values, out_grad, ancestry, w_query, key_matrix, value_matrix):
    z, y, x, c = (lax.axis_index(name) for name in "zyxc")
    place = jnp.stack([z, y, x, c]).astype(I32)
    group, kv = call(
        stack_kernel,
        [pltpu.VMEM((2 * ROWS, HEAD), BF16), pltpu.VMEM((BLOCK, 2 * HEAD), BF16)],
        [HB] * 4,
        [VM] * 2,
        "stack",
        [pltpu.SemaphoreType.DMA((2 * GROUP + 2,))],
    )(*in_hbm(queries, out_grad, keys, values))
    groups = [group] + [lax.ppermute(group, "y", shift(NY, k)) for k in range(1, NY)]
    below, above = [kv], [kv]
    for r in range(1, NZ // 2):
        below.append(lax.ppermute(below[-1], "z", shift(NZ, 1)))
        above.append(lax.ppermute(above[-1], "z", shift(NZ, -1)))
    kvs = below + [lax.ppermute(below[-1], "z", shift(NZ, 1))] + above[:0:-1]

    own_block = NY * z + y
    own_row = lax.dynamic_slice_in_dim(ancestry, own_block, 1, 0)
    depth = jnp.sum((own_row != own_block).astype(I32))
    token_places = (BLOCK * depth + jnp.arange(BLOCK, dtype=I32)).astype(F32)
    frequencies = jnp.exp(jnp.arange(HEAD // 2, dtype=F32) * (-2.0 * math.log(ROPE_BASE) / HEAD))
    angles = frequencies[:, None] * token_places[None, :]
    cosine = jnp.cos(angles)
    sine = jnp.sin(angles)
    items = call(
        plan_kernel,
        jax.ShapeDtypeStruct((NY * PAIRS + NY, 4), I32),
        [SM, SM, VM],
        SM,
        "plan",
        [pltpu.SMEM((NZ + 1,), I32)],
    )(place, ancestry, group)
    items, cosine, sine = lax.optimization_barrier((items, cosine, sine))

    tiles = (NY * PAIRS, 2 * BLOCK, ROWS)
    stats, scores, prob_grads = call(
        stats_kernel,
        [jax.ShapeDtypeStruct((NY, 4, ROWS), F32), pltpu.VMEM(tiles, F32), pltpu.VMEM(tiles, F32)],
        [SM] + [VM] * (NZ + NY),
        [VM] * 3,
        "stats",
        [pltpu.VMEM((NZ, BLOCK, 2 * HEAD), BF16)],
        STATS_FLOPS,
    )(items, *kvs, *groups)
    all_stats = [stats] + [lax.ppermute(stats, "y", shift(NY, k)) for k in range(1, NY)]
    key_cols = call(
        turn_kernel, pltpu.VMEM((NZ, HEAD, BLOCK), BF16), [SM] + [VM] * (NZ + 1), VM, "turn",
    )(items, *kvs, stats)
    dkv, *dq_parts = call(
        grads_kernel,
        [pltpu.VMEM((NZ, BLOCK, 2 * HEAD), BF16)] + [pltpu.VMEM((HEAD, ROWS), BF16)] * NY,
        [SM] + [VM] * (3 + 2 * NY),
        [VM] * (1 + NY),
        "grads",
        [pltpu.VMEM((NZ, BLOCK, HEAD), F32), pltpu.VMEM((NZ, BLOCK, HEAD), F32)],
        GRADS_FLOPS,
    )(items, key_cols, scores, prob_grads, *groups, *all_stats)
    dq_own = [dq_parts[0]] + [lax.ppermute(dq_parts[k], "y", shift(NY, -k)) for k in range(1, NY)]
    dkv = call(
        flush_kernel, pltpu.HBM(dkv.shape, BF16), [VM], HB, "flush", [pltpu.SemaphoreType.DMA((1,))],
    )(dkv)
    dkv_own = lax.all_to_all(dkv, "z", 0, 0, tiled=True)

    wq, wk, wv = in_hbm(w_query, key_matrix, value_matrix)
    blocks = call(
        fetch_kernel,
        [pltpu.VMEM((ROWS, ROWS), BF16)] * (2 * NX),
        [SM, VM, HB],
        [VM] * (2 * NX),
        "fetch",
        [pltpu.SemaphoreType.DMA((2 * NX,))],
    )(place, dq_parts[0], wq)
    pair_shapes = [pltpu.VMEM((NX, ROWS, HEAD), BF16)] * 2
    query_part, wk_away, wv_away = call(
        query_part_kernel,
        [pltpu.VMEM((2 * NX, ROWS, BLOCK), BF16)] + pair_shapes,
        [SM] + [VM] * (2 + NY) + [HB] * 2 + [VM] * (2 * NX),
        [VM] * 3,
        "query_part",
        [pltpu.SemaphoreType.DMA((2 * NX,))],
        QUERY_FLOPS,
    )(place, cosine, sine, *dq_own, wk, wv, *blocks)
    away, low, wk_kept, wv_kept = call(
        first_half_kernel,
        [pltpu.VMEM((NX, ROWS, BLOCK), BF16), pltpu.VMEM((2 * HEAD, BLOCK), BF16)] + pair_shapes,
        [SM] + [VM] * 6 + [HB] * 2,
        [VM] * 4,
        "first_half",
        [pltpu.SemaphoreType.DMA((2 * NX,))],
    )(place, cosine, sine, dkv_own, query_part, wk_away, wv_away, wk, wv)
    arrived = lax.ppermute(away, "c", shift(NC, 1))
    kept = call(
        second_half_kernel,
        pltpu.VMEM((NX, ROWS, BLOCK), F32),
        [VM] * 4,
        VM,
        "second_half",
    )(low, query_part, wk_kept, wv_kept)
    sent = [(kept[k] + arrived[k].astype(F32)).astype(BF16) for k in range(1, NX)]
    parts = [lax.ppermute(sent[k - 1], "x", shift(NX, k)) for k in range(1, NX)]
    return call(
        finish_kernel, jax.ShapeDtypeStruct((BLOCK, ROWS), BF16), [VM] * (2 + len(parts)), VM, "finish",
    )(kept[0], arrived[0], *parts)


def solution(mesh):
    grid = Mesh(mesh.devices.reshape(NZ, NY, NX, NC), ("z", "y", "x", "c"))
    split = P(("z", "y"), ("x", "c"))
    weight = P(None, ("x", "c"))
    return jax.shard_map(
        shards,
        mesh=grid,
        in_specs=(split, split, split, split, P(), weight, weight, weight),
        out_specs=split,
        check_vma=False,
    )
```

```python
import math

import jax
import jax.numpy as jnp
from jax import lax
from jax.experimental import pallas as pl
from jax.experimental.pallas import tpu as pltpu
from jax.sharding import Mesh, PartitionSpec as P

HEAD = 128
BLOCK = 128
GROUP = 5
ROWS = GROUP * BLOCK
NZ, NY, NX, NC = 8, 4, 4, 2
PAIRS = NZ // 2
ANC = 17
ROPE_BASE = 1000000.0
MASKED = -1e30
FACTOR = HEAD ** -0.5
NT = (((1,), (1,)), ((), ()))
NN = (((1,), (0,)), ((), ()))
F32, BF16, I32 = jnp.float32, jnp.bfloat16, jnp.int32
VMEM_LIMIT = 16 << 20
STATS_FLOPS = 2 * 2 * (NY * ROWS) * (NZ * BLOCK) * HEAD
GRADS_FLOPS = 3 * 2 * (NY * ROWS) * (NZ * BLOCK) * HEAD
QUERY_FLOPS = 2 * BLOCK * ROWS * 2 * NX * ROWS

VM = pl.BlockSpec(memory_space=pltpu.VMEM)
SM = pl.BlockSpec(memory_space=pltpu.SMEM)
HB = pl.BlockSpec(memory_space=pltpu.HBM)


def dot_nt(a, b):
    return lax.dot_general(a, b, NT, preferred_element_type=F32)


def dot_nn(a, b):
    return lax.dot_general(a, b, NN, preferred_element_type=F32)


def call(body, out_shape, in_specs, out_specs, name, scratch=(), flops=0):
    return pl.pallas_call(
        body,
        out_shape=out_shape,
        in_specs=in_specs,
        out_specs=out_specs,
        scratch_shapes=list(scratch),
        compiler_params=pltpu.CompilerParams(vmem_limit_bytes=VMEM_LIMIT),
        cost_estimate=pl.CostEstimate(flops=flops, transcendentals=0, bytes_accessed=0) if flops else None,
        name=name,
    )


def in_hbm(*arrays):
    return [pltpu.with_memory_space_constraint(a, pltpu.HBM) for a in arrays]


def run_copies(pairs, sem):
    started = [pltpu.make_async_copy(src, dst, sem.at[i]) for i, (src, dst) in enumerate(pairs)]
    for copy in started:
        copy.start()
    for copy in started:
        copy.wait()


def stack_kernel(q_ref, g_ref, k_ref, v_ref, rows_ref, kv_ref, sem):
    pairs = [(k_ref, kv_ref.at[:, 0:HEAD]), (v_ref, kv_ref.at[:, HEAD:2 * HEAD])]
    for h in range(GROUP):
        cols = slice(h * HEAD, (h + 1) * HEAD)
        pairs.append((q_ref.at[:, cols], rows_ref.at[h * BLOCK:(h + 1) * BLOCK, :]))
        pairs.append((g_ref.at[:, cols], rows_ref.at[ROWS + h * BLOCK:ROWS + (h + 1) * BLOCK, :]))
    run_copies(pairs, sem)


def plan_kernel(place_ref, anc_ref, rows_ref, item_ref, list_ref):
    z = place_ref[0]
    y = place_ref[1]
    for j in range(NY):
        query_block = NY * z + ((y - j) & (NY - 1))
        bits = jnp.int32(0)
        for i in range(ANC):
            key_block = anc_ref[i, query_block]
            bits = bits | jnp.where((key_block & (NY - 1)) == y, jnp.int32(1) << (key_block >> 2), 0)
        count = jnp.int32(0)
        for key_z in range(NZ):
            list_ref[count] = key_z
            count = count + ((bits >> key_z) & 1)
        for p in range(PAIRS):
            row = PAIRS * j + p
            first = jnp.where(2 * p < count, list_ref[2 * p], 0)
            both = 2 * p + 1 < count
            second = jnp.where(both, list_ref[2 * p + 1], first)
            item_ref[row, 0] = first
            item_ref[row, 1] = second
            causal = jnp.int32(0) if j == 0 else jnp.int32(-BLOCK)
            item_ref[row, 2] = jnp.where(first == z, causal, -BLOCK)
            item_ref[row, 3] = jnp.where(both, jnp.where(second == z, causal, -BLOCK), BLOCK)
        item_ref[NY * PAIRS + j, 0] = (count + 1) // 2
        item_ref[NY * PAIRS + j, 1] = z


def stats_kernel(item_ref, k0, k1, k2, k3, k4, k5, k6, k7, g0, g1, g2, g3, stat_ref, score_ref, pgrad_ref, kv_ref):
    z = item_ref[NY * PAIRS, 1]
    for r, part in enumerate((k0, k1, k2, k3, k4, k5, k6, k7)):
        kv_ref[(z - r) & (NZ - 1)] = part[...]
    key_row = lax.broadcasted_iota(I32, (BLOCK, ROWS), 0)
    query_row = lax.broadcasted_iota(I32, (BLOCK, ROWS), 1) % BLOCK
    gap = query_row - key_row
    for j, group in enumerate((g0, g1, g2, g3)):

        def step(p, carry, j=j, group=group):
            old, totals, dots = carry
            row = PAIRS * j + p
            first = item_ref[row, 0]
            second = item_ref[row, 1]
            kv = jnp.concatenate([kv_ref[first], kv_ref[second]], axis=0)
            scores = dot_nt(kv[:, :HEAD], group[:ROWS, :]) * FACTOR
            prob_grads = dot_nt(kv[:, HEAD:], group[ROWS:, :])
            upper = jnp.where(gap >= item_ref[row, 2], scores[:BLOCK], MASKED)
            lower = jnp.where(gap >= item_ref[row, 3], scores[BLOCK:], MASKED)
            scores = jnp.concatenate([upper, lower], axis=0)
            score_ref[row] = scores
            pgrad_ref[row] = prob_grads
            highest = jnp.maximum(old, jnp.max(scores, axis=0, keepdims=True))
            weights = jnp.exp(scores - highest)
            shrink = jnp.exp(old - highest)
            totals = totals * shrink + jnp.sum(weights, axis=0, keepdims=True)
            dots = dots * shrink + jnp.sum(weights * prob_grads, axis=0, keepdims=True)
            return highest, totals, dots

        zero = jnp.zeros((1, ROWS), F32)
        start = (jnp.full((1, ROWS), MASKED, F32), zero, zero)
        highest, totals, dots = lax.fori_loop(0, item_ref[NY * PAIRS + j, 0], step, start)
        stat_ref[j, 0:1, :] = highest
        stat_ref[j, 1:2, :] = totals
        stat_ref[j, 2:3, :] = dots
        stat_ref[j, 3:4, :] = zero


def turn_kernel(item_ref, k0, k1, k2, k3, k4, k5, k6, k7, stat_ref, key_cols):
    z = item_ref[NY * PAIRS, 1]
    for r, part in enumerate((k0, k1, k2, k3, k4, k5, k6, k7)):
        key_cols[(z - r) & (NZ - 1)] = part[:, :HEAD].T


def flush_kernel(low_ref, out_ref, sem):
    run_copies([(low_ref, out_ref)], sem)


def grads_kernel(item_ref, cols_ref, score_ref, pgrad_ref, g0, g1, g2, g3, s0, s1, s2, s3,
                 dkv_ref, dq0, dq1, dq2, dq3, dk_acc, dv_acc):
    stats = (s0, s1, s2, s3)
    dk_acc[...] = jnp.zeros_like(dk_acc)
    dv_acc[...] = jnp.zeros_like(dv_acc)
    for j, (group, out) in enumerate(zip((g0, g1, g2, g3), (dq0, dq1, dq2, dq3))):
        views = [stats[k][(j - k) % NY] for k in range(NY)]
        maxima = views[0][0:1]
        for k in range(1, NY):
            maxima = jnp.maximum(maxima, views[k][0:1])
        totals = jnp.zeros((1, ROWS), F32)
        dots = jnp.zeros((1, ROWS), F32)
        for k in range(NY):
            shrink = jnp.exp(views[k][0:1] - maxima)
            totals = totals + views[k][1:2] * shrink
            dots = dots + views[k][2:3] * shrink
        log_totals = maxima + jnp.log(totals)
        row_dots = dots / totals

        def step(p, query_grad, j=j, group=group, log_totals=log_totals, row_dots=row_dots):
            row = PAIRS * j + p
            first = item_ref[row, 0]
            second = item_ref[row, 1]
            probs = jnp.exp(score_ref[row] - log_totals)
            score_grads = (probs * (pgrad_ref[row] - row_dots)).astype(BF16)
            dk_pair = dot_nn(score_grads, group[:ROWS, :])
            dv_pair = dot_nn(probs.astype(BF16), group[ROWS:, :])
            dk_acc[first] += dk_pair[:BLOCK]
            dk_acc[second] += dk_pair[BLOCK:]
            dv_acc[first] += dv_pair[:BLOCK]
            dv_acc[second] += dv_pair[BLOCK:]
            cols = jnp.concatenate([cols_ref[first], cols_ref[second]], axis=1)
            return query_grad + dot_nn(cols, score_grads)

        query_grad = lax.fori_loop(0, item_ref[NY * PAIRS + j, 0], step, jnp.zeros((HEAD, ROWS), F32))
        out[...] = (query_grad * FACTOR).astype(BF16)
    for a in range(NZ):
        dkv_ref[a, :, :HEAD] = (dk_acc[a] * FACTOR).astype(BF16)
        dkv_ref[a, :, HEAD:] = dv_acc[a].astype(BF16)


def unrotate(x, cosine, sine):
    front = x[:HEAD // 2]
    back = x[HEAD // 2:]
    return jnp.concatenate([front * cosine + back * sine, back * cosine - front * sine], axis=0)


def weight_rows(place_ref, step):
    core = 1 - place_ref[3] if step < NX else place_ref[3]
    return pl.ds(pl.multiple_of((2 * ((place_ref[2] + step) & (NX - 1)) + core) * ROWS, ROWS), ROWS)


def fetch_kernel(place_ref, anc_ref, dq_ref, wq_hbm, cos_ref, sin_ref, *refs):
    blocks, sem = refs[:-1], refs[-1]
    copies = [
        pltpu.make_async_copy(wq_hbm.at[weight_rows(place_ref, i), :], block, sem.at[i])
        for i, block in enumerate(blocks)
    ]
    for copy in copies:
        copy.start()
    own_block = NY * place_ref[0] + place_ref[1]
    depth = jnp.int32(0)
    for i in range(ANC):
        depth = depth + jnp.where(anc_ref[i, own_block] != own_block, 1, 0)
    half = (HEAD // 2, BLOCK)
    pair = lax.broadcasted_iota(I32, half, 0).astype(F32)
    token_place = (lax.broadcasted_iota(I32, half, 1) + BLOCK * depth).astype(F32)
    angles = jnp.exp(pair * (-2.0 * math.log(ROPE_BASE) / HEAD)) * token_place
    cos_ref[...] = jnp.cos(angles)
    sin_ref[...] = jnp.sin(angles)
    for copy in copies:
        copy.wait()


def start_pair(place_ref, first, wk_hbm, wv_hbm, wk, wv, sem):
    copies = []
    for i in range(NX):
        rows = weight_rows(place_ref, first + i)
        copies.append(pltpu.make_async_copy(wk_hbm.at[rows, :], wk.at[i], sem.at[2 * i]))
        copies.append(pltpu.make_async_copy(wv_hbm.at[rows, :], wv.at[i], sem.at[2 * i + 1]))
    for copy in copies:
        copy.start()
    return copies


def query_part_kernel(place_ref, cos_ref, sin_ref, q0, q1, q2, q3, wk_hbm, wv_hbm, *refs):
    blocks, out_ref, wk, wv, sem = refs[:2 * NX], *refs[2 * NX:]
    copies = start_pair(place_ref, 0, wk_hbm, wv_hbm, wk, wv, sem)
    cosine = cos_ref[...]
    sine = sin_ref[...]
    low = []
    for h in range(GROUP):
        cols = slice(h * HEAD, (h + 1) * HEAD)
        total = q0[:, cols].astype(F32)
        for part in (q1, q2, q3):
            total = total + part[:, cols].astype(F32)
        low.append(unrotate(total, cosine, sine).astype(BF16))
    low = jnp.concatenate(low, axis=0)
    for i, block in enumerate(blocks):
        out_ref[i] = dot_nn(block[...], low).astype(BF16)
    for copy in copies:
        copy.wait()


def first_half_kernel(cos_ref, sin_ref, dkv_ref, part_ref, wk, wv, out_ref, low_ref):
    total = dkv_ref[0].astype(F32)
    for a in range(1, NZ):
        total = total + dkv_ref[a].astype(F32)
    low_ref[:HEAD, :] = unrotate(total[:, :HEAD].T, cos_ref[...], sin_ref[...]).astype(BF16)
    low_ref[HEAD:, :] = total[:, HEAD:].T.astype(BF16)
    for i in range(NX):
        out_ref[i] = (part_ref[i] + key_value_part(low_ref, wk[i], wv[i])).astype(BF16)


def second_half_kernel(place_ref, low_ref, part_ref, wk_hbm, wv_hbm, out_ref, wk, wv, sem):
    copies = start_pair(place_ref, NX, wk_hbm, wv_hbm, wk, wv, sem)
    for i in range(NX):
        for copy in copies[2 * i:2 * i + 2]:
            copy.wait()
        out_ref[i] = part_ref[NX + i] + key_value_part(low_ref, wk[i], wv[i])


def key_value_part(low_ref, wk, wv):
    return dot_nn(wk, low_ref[:HEAD, :]) + dot_nn(wv, low_ref[HEAD:, :])


def finish_kernel(kept_ref, arrived_ref, p0, p1, p2, out_ref):
    for h in range(GROUP):
        rows = slice(h * HEAD, (h + 1) * HEAD)
        total = kept_ref[rows, :]
        for part in (arrived_ref, p0, p1, p2):
            total = total + part[rows, :].astype(F32)
        out_ref[:, rows] = total.T.astype(BF16)


def shift(size, k):
    return [(i, (i + k) % size) for i in range(size)]


def shards(queries, keys, values, out_grad, ancestry, w_query, key_matrix, value_matrix):
    z, y, x, c = (lax.axis_index(name) for name in "zyxc")
    place = jnp.stack([z, y, x, c]).astype(I32)
    group, kv = call(
        stack_kernel,
        [pltpu.VMEM((2 * ROWS, HEAD), BF16), pltpu.VMEM((BLOCK, 2 * HEAD), BF16)],
        [HB] * 4,
        [VM] * 2,
        "stack",
        [pltpu.SemaphoreType.DMA((2 * GROUP + 2,))],
    )(*in_hbm(queries, out_grad, keys, values))
    groups = [group] + [lax.ppermute(group, "y", shift(NY, k)) for k in range(1, NY)]
    below, above = [kv], [kv]
    for r in range(1, NZ // 2):
        below.append(lax.ppermute(below[-1], "z", shift(NZ, 1)))
        above.append(lax.ppermute(above[-1], "z", shift(NZ, -1)))
    kvs = below + [lax.ppermute(below[-1], "z", shift(NZ, 1))] + above[:0:-1]

    items = call(
        plan_kernel,
        jax.ShapeDtypeStruct((NY * PAIRS + NY, 4), I32),
        [SM, SM, VM],
        SM,
        "plan",
        [pltpu.SMEM((NZ + 1,), I32)],
    )(place, ancestry.T, group)

    tiles = (NY * PAIRS, 2 * BLOCK, ROWS)
    stats, scores, prob_grads = call(
        stats_kernel,
        [jax.ShapeDtypeStruct((NY, 4, ROWS), F32), pltpu.VMEM(tiles, F32), pltpu.VMEM(tiles, F32)],
        [SM] + [VM] * (NZ + NY),
        [VM] * 3,
        "stats",
        [pltpu.VMEM((NZ, BLOCK, 2 * HEAD), BF16)],
        STATS_FLOPS,
    )(items, *kvs, *groups)
    all_stats = [stats] + [lax.ppermute(stats, "y", shift(NY, k)) for k in range(1, NY)]
    key_cols = call(
        turn_kernel, pltpu.VMEM((NZ, HEAD, BLOCK), BF16), [SM] + [VM] * (NZ + 1), VM, "turn",
    )(items, *kvs, stats)
    dkv, *dq_parts = call(
        grads_kernel,
        [pltpu.VMEM((NZ, BLOCK, 2 * HEAD), BF16)] + [pltpu.VMEM((HEAD, ROWS), BF16)] * NY,
        [SM] + [VM] * (3 + 2 * NY),
        [VM] * (1 + NY),
        "grads",
        [pltpu.VMEM((NZ, BLOCK, HEAD), F32), pltpu.VMEM((NZ, BLOCK, HEAD), F32)],
        GRADS_FLOPS,
    )(items, key_cols, scores, prob_grads, *groups, *all_stats)
    dq_own = [dq_parts[0]] + [lax.ppermute(dq_parts[k], "y", shift(NY, -k)) for k in range(1, NY)]
    dkv = call(
        flush_kernel, pltpu.HBM(dkv.shape, BF16), [VM], HB, "flush", [pltpu.SemaphoreType.DMA((1,))],
    )(dkv)
    dkv_own = lax.all_to_all(dkv, "z", 0, 0, tiled=True)

    wq, wk, wv = in_hbm(w_query, key_matrix, value_matrix)
    cosine, sine, *blocks = call(
        fetch_kernel,
        [pltpu.VMEM((HEAD // 2, BLOCK), F32)] * 2 + [pltpu.VMEM((ROWS, ROWS), BF16)] * (2 * NX),
        [SM, SM, VM, HB],
        [VM] * (2 * NX + 2),
        "fetch",
        [pltpu.SemaphoreType.DMA((2 * NX,))],
    )(place, ancestry.T, dq_parts[0], wq)
    pair_shapes = [pltpu.VMEM((NX, ROWS, HEAD), BF16)] * 2
    query_part, wk_away, wv_away = call(
        query_part_kernel,
        [pltpu.VMEM((2 * NX, ROWS, BLOCK), BF16)] + pair_shapes,
        [SM] + [VM] * (2 + NY) + [HB] * 2 + [VM] * (2 * NX),
        [VM] * 3,
        "query_part",
        [pltpu.SemaphoreType.DMA((2 * NX,))],
        QUERY_FLOPS,
    )(place, cosine, sine, *dq_own, wk, wv, *blocks)
    away, low = call(
        first_half_kernel,
        [pltpu.VMEM((NX, ROWS, BLOCK), BF16), pltpu.VMEM((2 * HEAD, BLOCK), BF16)],
        [VM] * 6,
        [VM] * 2,
        "first_half",
    )(cosine, sine, dkv_own, query_part, wk_away, wv_away)
    arrived = lax.ppermute(away, "c", shift(NC, 1))
    kept = call(
        second_half_kernel,
        pltpu.VMEM((NX, ROWS, BLOCK), F32),
        [SM] + [VM] * 2 + [HB] * 2,
        VM,
        "second_half",
        pair_shapes + [pltpu.SemaphoreType.DMA((2 * NX,))],
    )(place, low, query_part, wk, wv)
    sent = [(kept[k] + arrived[k].astype(F32)).astype(BF16) for k in range(1, NX)]
    parts = [lax.ppermute(sent[k - 1], "x", shift(NX, k)) for k in range(1, NX)]
    return call(
        finish_kernel, jax.ShapeDtypeStruct((BLOCK, ROWS), BF16), [VM] * (2 + len(parts)), VM, "finish",
    )(kept[0], arrived[0], *parts)


def solution(mesh):
    grid = Mesh(mesh.devices.reshape(NZ, NY, NX, NC), ("z", "y", "x", "c"))
    split = P(("z", "y"), ("x", "c"))
    weight = P(None, ("x", "c"))
    return jax.shard_map(
        shards,
        mesh=grid,
        in_specs=(split, split, split, split, P(), weight, weight, weight),
        out_specs=split,
        check_vma=False,
    )
```

```python
import math

import jax
import jax.numpy as jnp
from jax import lax
from jax.experimental import pallas as pl
from jax.experimental.pallas import tpu as pltpu
from jax.sharding import Mesh, PartitionSpec as P

HEAD = 128
BLOCK = 128
GROUP = 5
ROWS = GROUP * BLOCK
NZ, NY, NX, NC = 8, 4, 4, 2
PAIRS = NZ // 2
ANC = 17
ROPE_BASE = 1000000.0
MASKED = -1e30
FACTOR = HEAD ** -0.5
NT = (((1,), (1,)), ((), ()))
NN = (((1,), (0,)), ((), ()))
F32, BF16, I32 = jnp.float32, jnp.bfloat16, jnp.int32
VMEM_LIMIT = 16 << 20
PLAN_FLOPS = 1_000_000_000
STATS_FLOPS = 2 * 2 * (NY * ROWS) * (NZ * BLOCK) * HEAD
GRADS_FLOPS = 3 * 2 * (NY * ROWS) * (NZ * BLOCK) * HEAD
QUERY_FLOPS = 2 * BLOCK * ROWS * 2 * NX * ROWS

VM = pl.BlockSpec(memory_space=pltpu.VMEM)
SM = pl.BlockSpec(memory_space=pltpu.SMEM)
HB = pl.BlockSpec(memory_space=pltpu.HBM)


def dot_nt(a, b):
    return lax.dot_general(a, b, NT, preferred_element_type=F32)


def dot_nn(a, b):
    return lax.dot_general(a, b, NN, preferred_element_type=F32)


def call(body, out_shape, in_specs, out_specs, name, scratch=(), flops=0):
    return pl.pallas_call(
        body,
        out_shape=out_shape,
        in_specs=in_specs,
        out_specs=out_specs,
        scratch_shapes=list(scratch),
        compiler_params=pltpu.CompilerParams(vmem_limit_bytes=VMEM_LIMIT),
        cost_estimate=pl.CostEstimate(flops=flops, transcendentals=0, bytes_accessed=0) if flops else None,
        name=name,
    )


def in_hbm(*arrays):
    return [pltpu.with_memory_space_constraint(a, pltpu.HBM) for a in arrays]


def run_copies(pairs, sem):
    started = [pltpu.make_async_copy(src, dst, sem.at[i]) for i, (src, dst) in enumerate(pairs)]
    for copy in started:
        copy.start()
    for copy in started:
        copy.wait()


def stack_kernel(q_ref, g_ref, k_ref, v_ref, rows_ref, kv_ref, sem):
    pairs = [(k_ref, kv_ref.at[:, 0:HEAD]), (v_ref, kv_ref.at[:, HEAD:2 * HEAD])]
    for h in range(GROUP):
        cols = slice(h * HEAD, (h + 1) * HEAD)
        pairs.append((q_ref.at[:, cols], rows_ref.at[h * BLOCK:(h + 1) * BLOCK, :]))
        pairs.append((g_ref.at[:, cols], rows_ref.at[ROWS + h * BLOCK:ROWS + (h + 1) * BLOCK, :]))
    run_copies(pairs, sem)


def plan_kernel(place_ref, anc_ref, rows_ref, item_ref, list_ref):
    z = place_ref[0]
    y = place_ref[1]
    for j in range(NY):
        query_block = NY * z + ((y - j) & (NY - 1))
        bits = jnp.int32(0)
        for i in range(ANC):
            key_block = anc_ref[i, query_block]
            bits = bits | jnp.where((key_block & (NY - 1)) == y, jnp.int32(1) << (key_block >> 2), 0)
        count = jnp.int32(0)
        for key_z in range(NZ):
            list_ref[count] = key_z
            count = count + ((bits >> key_z) & 1)
        for p in range(PAIRS):
            row = PAIRS * j + p
            first = jnp.where(2 * p < count, list_ref[2 * p], 0)
            both = 2 * p + 1 < count
            second = jnp.where(both, list_ref[2 * p + 1], first)
            item_ref[row, 0] = first
            item_ref[row, 1] = second
            causal = jnp.int32(0) if j == 0 else jnp.int32(-BLOCK)
            item_ref[row, 2] = jnp.where(first == z, causal, -BLOCK)
            item_ref[row, 3] = jnp.where(both, jnp.where(second == z, causal, -BLOCK), BLOCK)
        item_ref[NY * PAIRS + j, 0] = (count + 1) // 2
        item_ref[NY * PAIRS + j, 1] = z


def stats_kernel(item_ref, k0, k1, k2, k3, k4, k5, k6, k7, g0, g1, g2, g3, stat_ref, score_ref, pgrad_ref, kv_ref):
    z = item_ref[NY * PAIRS, 1]
    for r, part in enumerate((k0, k1, k2, k3, k4, k5, k6, k7)):
        kv_ref[(z - r) & (NZ - 1)] = part[...]
    key_row = lax.broadcasted_iota(I32, (BLOCK, ROWS), 0)
    query_row = lax.broadcasted_iota(I32, (BLOCK, ROWS), 1) % BLOCK
    gap = query_row - key_row
    for j, group in enumerate((g0, g1, g2, g3)):

        def step(p, carry, j=j, group=group):
            old, totals, dots = carry
            row = PAIRS * j + p
            first = item_ref[row, 0]
            second = item_ref[row, 1]
            kv = jnp.concatenate([kv_ref[first], kv_ref[second]], axis=0)
            scores = dot_nt(kv[:, :HEAD], group[:ROWS, :]) * FACTOR
            prob_grads = dot_nt(kv[:, HEAD:], group[ROWS:, :])
            upper = jnp.where(gap >= item_ref[row, 2], scores[:BLOCK], MASKED)
            lower = jnp.where(gap >= item_ref[row, 3], scores[BLOCK:], MASKED)
            scores = jnp.concatenate([upper, lower], axis=0)
            score_ref[row] = scores
            pgrad_ref[row] = prob_grads
            highest = jnp.maximum(old, jnp.max(scores, axis=0, keepdims=True))
            weights = jnp.exp(scores - highest)
            shrink = jnp.exp(old - highest)
            totals = totals * shrink + jnp.sum(weights, axis=0, keepdims=True)
            dots = dots * shrink + jnp.sum(weights * prob_grads, axis=0, keepdims=True)
            return highest, totals, dots

        zero = jnp.zeros((1, ROWS), F32)
        start = (jnp.full((1, ROWS), MASKED, F32), zero, zero)
        highest, totals, dots = lax.fori_loop(0, item_ref[NY * PAIRS + j, 0], step, start)
        stat_ref[j, 0:1, :] = highest
        stat_ref[j, 1:2, :] = totals
        stat_ref[j, 2:3, :] = dots
        stat_ref[j, 3:4, :] = zero


def turn_kernel(item_ref, k0, k1, k2, k3, k4, k5, k6, k7, stat_ref, key_cols):
    z = item_ref[NY * PAIRS, 1]
    for r, part in enumerate((k0, k1, k2, k3, k4, k5, k6, k7)):
        key_cols[(z - r) & (NZ - 1)] = part[:, :HEAD].T


def flush_kernel(low_ref, out_ref, sem):
    run_copies([(low_ref, out_ref)], sem)


def grads_kernel(item_ref, cols_ref, score_ref, pgrad_ref, g0, g1, g2, g3, s0, s1, s2, s3,
                 dkv_ref, dq0, dq1, dq2, dq3, dk_acc, dv_acc):
    stats = (s0, s1, s2, s3)
    dk_acc[...] = jnp.zeros_like(dk_acc)
    dv_acc[...] = jnp.zeros_like(dv_acc)
    for j, (group, out) in enumerate(zip((g0, g1, g2, g3), (dq0, dq1, dq2, dq3))):
        views = [stats[k][(j - k) % NY] for k in range(NY)]
        maxima = views[0][0:1]
        for k in range(1, NY):
            maxima = jnp.maximum(maxima, views[k][0:1])
        totals = jnp.zeros((1, ROWS), F32)
        dots = jnp.zeros((1, ROWS), F32)
        for k in range(NY):
            shrink = jnp.exp(views[k][0:1] - maxima)
            totals = totals + views[k][1:2] * shrink
            dots = dots + views[k][2:3] * shrink
        log_totals = maxima + jnp.log(totals)
        row_dots = dots / totals

        def step(p, query_grad, j=j, group=group, log_totals=log_totals, row_dots=row_dots):
            row = PAIRS * j + p
            first = item_ref[row, 0]
            second = item_ref[row, 1]
            probs = jnp.exp(score_ref[row] - log_totals)
            score_grads = (probs * (pgrad_ref[row] - row_dots)).astype(BF16)
            dk_pair = dot_nn(score_grads, group[:ROWS, :])
            dv_pair = dot_nn(probs.astype(BF16), group[ROWS:, :])
            dk_acc[first] += dk_pair[:BLOCK]
            dk_acc[second] += dk_pair[BLOCK:]
            dv_acc[first] += dv_pair[:BLOCK]
            dv_acc[second] += dv_pair[BLOCK:]
            cols = jnp.concatenate([cols_ref[first], cols_ref[second]], axis=1)
            return query_grad + dot_nn(cols, score_grads)

        query_grad = lax.fori_loop(0, item_ref[NY * PAIRS + j, 0], step, jnp.zeros((HEAD, ROWS), F32))
        out[...] = (query_grad * FACTOR).astype(BF16)
    for a in range(NZ):
        dkv_ref[a, :, :HEAD] = (dk_acc[a] * FACTOR).astype(BF16)
        dkv_ref[a, :, HEAD:] = dv_acc[a].astype(BF16)


def unrotate(x, cosine, sine):
    front = x[:HEAD // 2]
    back = x[HEAD // 2:]
    return jnp.concatenate([front * cosine + back * sine, back * cosine - front * sine], axis=0)


def weight_rows(place_ref, step):
    core = place_ref[3] if step < NX else 1 - place_ref[3]
    return pl.ds(pl.multiple_of((2 * ((place_ref[2] + step) & (NX - 1)) + core) * ROWS, ROWS), ROWS)


def fetch_kernel(place_ref, anc_ref, dq_ref, wq_hbm, cos_ref, sin_ref, *refs):
    blocks, sem = refs[:-1], refs[-1]
    copies = [
        pltpu.make_async_copy(wq_hbm.at[weight_rows(place_ref, i), :], block, sem.at[i])
        for i, block in enumerate(blocks)
    ]
    for copy in copies:
        copy.start()
    own_block = NY * place_ref[0] + place_ref[1]
    depth = jnp.int32(0)
    for i in range(ANC):
        depth = depth + jnp.where(anc_ref[i, own_block] != own_block, 1, 0)
    half = (HEAD // 2, BLOCK)
    pair = lax.broadcasted_iota(I32, half, 0).astype(F32)
    token_place = (lax.broadcasted_iota(I32, half, 1) + BLOCK * depth).astype(F32)
    angles = jnp.exp(pair * (-2.0 * math.log(ROPE_BASE) / HEAD)) * token_place
    cos_ref[...] = jnp.cos(angles)
    sin_ref[...] = jnp.sin(angles)
    for copy in copies:
        copy.wait()


def start_pair(place_ref, first, wk_hbm, wv_hbm, wk, wv, sem):
    copies = []
    for i in range(NX):
        rows = weight_rows(place_ref, first + i)
        copies.append(pltpu.make_async_copy(wk_hbm.at[rows, :], wk.at[i], sem.at[2 * i]))
        copies.append(pltpu.make_async_copy(wv_hbm.at[rows, :], wv.at[i], sem.at[2 * i + 1]))
    for copy in copies:
        copy.start()
    return copies


def query_part_kernel(place_ref, cos_ref, sin_ref, q0, q1, q2, q3, wk_hbm, wv_hbm, *refs):
    blocks, out_ref, wk, wv, sem = refs[:2 * NX], *refs[2 * NX:]
    copies = start_pair(place_ref, 0, wk_hbm, wv_hbm, wk, wv, sem)
    cosine = cos_ref[...]
    sine = sin_ref[...]
    low = []
    for h in range(GROUP):
        cols = slice(h * HEAD, (h + 1) * HEAD)
        total = q0[:, cols].astype(F32)
        for part in (q1, q2, q3):
            total = total + part[:, cols].astype(F32)
        low.append(unrotate(total, cosine, sine).astype(BF16))
    low = jnp.concatenate(low, axis=0)
    for i, block in enumerate(blocks):
        out_ref[i] = dot_nn(block[...], low).astype(BF16)
    for copy in copies:
        copy.wait()


def first_half_kernel(cos_ref, sin_ref, dkv_ref, part_ref, wk, wv, kept_ref, b1, b2, b3, low_ref):
    total = dkv_ref[0].astype(F32)
    for a in range(1, NZ):
        total = total + dkv_ref[a].astype(F32)
    low_ref[:HEAD, :] = unrotate(total[:, :HEAD].T, cos_ref[...], sin_ref[...]).astype(BF16)
    low_ref[HEAD:, :] = total[:, HEAD:].T.astype(BF16)
    for i, out_ref in enumerate((kept_ref, b1, b2, b3)):
        out_ref[...] = (part_ref[i] + key_value_part(low_ref, wk[i], wv[i])).astype(out_ref.dtype)


def second_half_kernel(place_ref, low_ref, part_ref, wk_hbm, wv_hbm, b4, b5, b6, b7, wk, wv, sem):
    copies = start_pair(place_ref, NX, wk_hbm, wv_hbm, wk, wv, sem)
    for i, out_ref in enumerate((b4, b5, b6, b7)):
        for copy in copies[2 * i:2 * i + 2]:
            copy.wait()
        out_ref[...] = (part_ref[NX + i] + key_value_part(low_ref, wk[i], wv[i])).astype(out_ref.dtype)


def key_value_part(low_ref, wk, wv):
    return dot_nn(wk, low_ref[:HEAD, :]) + dot_nn(wv, low_ref[HEAD:, :])


def finish_kernel(kept_ref, p1, p2, p3, p4, p5, p6, p7, out_ref):
    for h in range(GROUP):
        rows = slice(h * HEAD, (h + 1) * HEAD)
        total = kept_ref[rows, :]
        for part in (p1, p2, p3, p4, p5, p6, p7):
            total = total + part[rows, :].astype(F32)
        out_ref[:, rows] = total.T.astype(BF16)


def shift(size, k):
    return [(i, (i + k) % size) for i in range(size)]


def shards(queries, keys, values, out_grad, ancestry, w_query, key_matrix, value_matrix):
    z, y, x, c = (lax.axis_index(name) for name in "zyxc")
    place = jnp.stack([z, y, x, c]).astype(I32)
    group, kv = call(
        stack_kernel,
        [pltpu.VMEM((2 * ROWS, HEAD), BF16), pltpu.VMEM((BLOCK, 2 * HEAD), BF16)],
        [HB] * 4,
        [VM] * 2,
        "stack",
        [pltpu.SemaphoreType.DMA((2 * GROUP + 2,))],
    )(*in_hbm(queries, out_grad, keys, values))
    below, above = [kv], [kv]
    for r in range(1, NZ // 2):
        below.append(lax.ppermute(below[-1], "z", shift(NZ, 1)))
        above.append(lax.ppermute(above[-1], "z", shift(NZ, -1)))
    kvs = below + [lax.ppermute(below[-1], "z", shift(NZ, 1))] + above[:0:-1]

    groups = [group] + [lax.ppermute(group, "y", shift(NY, k)) for k in range(1, NY)]
    items = call(
        plan_kernel,
        jax.ShapeDtypeStruct((NY * PAIRS + NY, 4), I32),
        [SM, SM, VM],
        SM,
        "plan",
        [pltpu.SMEM((NZ + 1,), I32)],
        PLAN_FLOPS,
    )(place, ancestry.T, group)

    tiles = (NY * PAIRS, 2 * BLOCK, ROWS)
    stats, scores, prob_grads = call(
        stats_kernel,
        [jax.ShapeDtypeStruct((NY, 4, ROWS), F32), pltpu.VMEM(tiles, F32), pltpu.VMEM(tiles, F32)],
        [SM] + [VM] * (NZ + NY),
        [VM] * 3,
        "stats",
        [pltpu.VMEM((NZ, BLOCK, 2 * HEAD), BF16)],
        STATS_FLOPS,
    )(items, *kvs, *groups)
    all_stats = [stats] + [lax.ppermute(stats, "y", shift(NY, k)) for k in range(1, NY)]
    key_cols = call(
        turn_kernel, pltpu.VMEM((NZ, HEAD, BLOCK), BF16), [SM] + [VM] * (NZ + 1), VM, "turn",
    )(items, *kvs, stats)
    dkv, *dq_parts = call(
        grads_kernel,
        [pltpu.VMEM((NZ, BLOCK, 2 * HEAD), BF16)] + [pltpu.VMEM((HEAD, ROWS), BF16)] * NY,
        [SM] + [VM] * (3 + 2 * NY),
        [VM] * (1 + NY),
        "grads",
        [pltpu.VMEM((NZ, BLOCK, HEAD), F32), pltpu.VMEM((NZ, BLOCK, HEAD), F32)],
        GRADS_FLOPS,
    )(items, key_cols, scores, prob_grads, *groups, *all_stats)
    dq_own = [dq_parts[0]] + [lax.ppermute(dq_parts[k], "y", shift(NY, -k)) for k in range(1, NY)]
    dkv = call(
        flush_kernel, pltpu.HBM(dkv.shape, BF16), [VM], HB, "flush", [pltpu.SemaphoreType.DMA((1,))],
    )(dkv)
    dkv_own = lax.all_to_all(dkv, "z", 0, 0, tiled=True)

    wq, wk, wv = in_hbm(w_query, key_matrix, value_matrix)
    cosine, sine, *blocks = call(
        fetch_kernel,
        [pltpu.VMEM((HEAD // 2, BLOCK), F32)] * 2 + [pltpu.VMEM((ROWS, ROWS), BF16)] * (2 * NX),
        [SM, SM, VM, HB],
        [VM] * (2 * NX + 2),
        "fetch",
        [pltpu.SemaphoreType.DMA((2 * NX,))],
    )(place, ancestry.T, dq_parts[0], wq)
    pair_shapes = [pltpu.VMEM((NX, ROWS, HEAD), BF16)] * 2
    query_part, wk_first, wv_first = call(
        query_part_kernel,
        [pltpu.VMEM((2 * NX, ROWS, BLOCK), BF16)] + pair_shapes,
        [SM] + [VM] * (2 + NY) + [HB] * 2 + [VM] * (2 * NX),
        [VM] * 3,
        "query_part",
        [pltpu.SemaphoreType.DMA((2 * NX,))],
        QUERY_FLOPS,
    )(place, cosine, sine, *dq_own, wk, wv, *blocks)
    block = pltpu.VMEM((ROWS, BLOCK), BF16)
    kept, b1, b2, b3, low = call(
        first_half_kernel,
        [pltpu.VMEM((ROWS, BLOCK), F32), block, block, block, pltpu.VMEM((2 * HEAD, BLOCK), BF16)],
        [VM] * 6,
        [VM] * 5,
        "first_half",
    )(cosine, sine, dkv_own, query_part, wk_first, wv_first)
    others = call(
        second_half_kernel,
        [block] * NX,
        [SM] + [VM] * 2 + [HB] * 2,
        [VM] * NX,
        "second_half",
        pair_shapes + [pltpu.SemaphoreType.DMA((2 * NX,))],
    )(place, low, query_part, wk, wv)
    parts = []
    for step, sent in enumerate([b1, b2, b3, *others], start=1):
        flip, dx = divmod(step, NX)
        pairs = [(NC * a + core, NC * ((a + dx) % NX) + (core ^ flip)) for a in range(NX) for core in range(NC)]
        parts.append(lax.ppermute(sent, ("x", "c"), pairs))
    return call(
        finish_kernel, jax.ShapeDtypeStruct((BLOCK, ROWS), BF16), [VM] * (1 + len(parts)), VM, "finish",
    )(kept, *parts)


def solution(mesh):
    grid = Mesh(mesh.devices.reshape(NZ, NY, NX, NC), ("z", "y", "x", "c"))
    split = P(("z", "y"), ("x", "c"))
    weight = P(None, ("x", "c"))
    return jax.shard_map(
        shards,
        mesh=grid,
        in_specs=(split, split, split, split, P(), weight, weight, weight),
        out_specs=split,
        check_vma=False,
    )
```

```python
import math

import jax
import jax.numpy as jnp
from jax import lax
from jax.experimental import pallas as pl
from jax.experimental.pallas import tpu as pltpu
from jax.sharding import Mesh, PartitionSpec as P

HEAD = 128
BLOCK = 128
GROUP = 5
ROWS = GROUP * BLOCK
NZ, NY, NX, NC = 8, 4, 4, 2
PAIRS = NZ // 2
ANC = 17
ROPE_BASE = 1000000.0
MASKED = -1e30
FACTOR = HEAD ** -0.5
NT = (((1,), (1,)), ((), ()))
NN = (((1,), (0,)), ((), ()))
F32, BF16, I32 = jnp.float32, jnp.bfloat16, jnp.int32
VMEM_LIMIT = 16 << 20
PLAN_FLOPS = 1_000_000_000
STATS_FLOPS = 2 * 2 * (NY * ROWS) * (NZ * BLOCK) * HEAD
GRADS_FLOPS = 3 * 2 * (NY * ROWS) * (NZ * BLOCK) * HEAD
QUERY_FLOPS = 2 * BLOCK * ROWS * 2 * NX * ROWS

VM = pl.BlockSpec(memory_space=pltpu.VMEM)
SM = pl.BlockSpec(memory_space=pltpu.SMEM)
HB = pl.BlockSpec(memory_space=pltpu.HBM)


def dot_nt(a, b):
    return lax.dot_general(a, b, NT, preferred_element_type=F32)


def dot_nn(a, b):
    return lax.dot_general(a, b, NN, preferred_element_type=F32)


def call(body, out_shape, in_specs, out_specs, name, scratch=(), flops=0):
    return pl.pallas_call(
        body,
        out_shape=out_shape,
        in_specs=in_specs,
        out_specs=out_specs,
        scratch_shapes=list(scratch),
        compiler_params=pltpu.CompilerParams(vmem_limit_bytes=VMEM_LIMIT),
        cost_estimate=pl.CostEstimate(flops=flops, transcendentals=0, bytes_accessed=0) if flops else None,
        name=name,
    )


def in_hbm(*arrays):
    return [pltpu.with_memory_space_constraint(a, pltpu.HBM) for a in arrays]


def run_copies(pairs, sem):
    started = [pltpu.make_async_copy(src, dst, sem.at[i]) for i, (src, dst) in enumerate(pairs)]
    for copy in started:
        copy.start()
    for copy in started:
        copy.wait()


def stack_kernel(q_ref, g_ref, k_ref, v_ref, rows_ref, kv_ref, sem):
    pairs = [(k_ref, kv_ref.at[:, 0:HEAD]), (v_ref, kv_ref.at[:, HEAD:2 * HEAD])]
    for h in range(GROUP):
        cols = slice(h * HEAD, (h + 1) * HEAD)
        pairs.append((q_ref.at[:, cols], rows_ref.at[h * BLOCK:(h + 1) * BLOCK, :]))
        pairs.append((g_ref.at[:, cols], rows_ref.at[ROWS + h * BLOCK:ROWS + (h + 1) * BLOCK, :]))
    run_copies(pairs, sem)


def plan_kernel(place_ref, anc_ref, rows_ref, item_ref, list_ref):
    z = place_ref[0]
    y = place_ref[1]
    for j in range(NY):
        query_block = NY * z + ((y - j) & (NY - 1))
        bits = jnp.int32(0)
        for i in range(ANC):
            key_block = anc_ref[i, query_block]
            bits = bits | jnp.where((key_block & (NY - 1)) == y, jnp.int32(1) << (key_block >> 2), 0)
        count = jnp.int32(0)
        for key_z in range(NZ):
            list_ref[count] = key_z
            count = count + ((bits >> key_z) & 1)
        for p in range(PAIRS):
            row = PAIRS * j + p
            first = jnp.where(2 * p < count, list_ref[2 * p], 0)
            both = 2 * p + 1 < count
            second = jnp.where(both, list_ref[2 * p + 1], first)
            item_ref[row, 0] = first
            item_ref[row, 1] = second
            causal = jnp.int32(0) if j == 0 else jnp.int32(-BLOCK)
            item_ref[row, 2] = jnp.where(first == z, causal, -BLOCK)
            item_ref[row, 3] = jnp.where(both, jnp.where(second == z, causal, -BLOCK), BLOCK)
        item_ref[NY * PAIRS + j, 0] = (count + 1) // 2
        item_ref[NY * PAIRS + j, 1] = z
        item_ref[NY * PAIRS + j, 2] = y


def stats_kernel(item_ref, k0, k1, k2, k3, k4, k5, k6, k7, g0, g1, g2, g3, stat_ref, score_ref, pgrad_ref, kv_ref):
    z = item_ref[NY * PAIRS, 1]
    for r, part in enumerate((k0, k1, k2, k3, k4, k5, k6, k7)):
        kv_ref[(z - r) & (NZ - 1)] = part[...]
    key_row = lax.broadcasted_iota(I32, (BLOCK, ROWS), 0)
    query_row = lax.broadcasted_iota(I32, (BLOCK, ROWS), 1) % BLOCK
    gap = query_row - key_row
    for j, group in enumerate((g0, g1, g2, g3)):

        def step(p, carry, j=j, group=group):
            old, totals, dots = carry
            row = PAIRS * j + p
            first = item_ref[row, 0]
            second = item_ref[row, 1]
            kv = jnp.concatenate([kv_ref[first], kv_ref[second]], axis=0)
            scores = dot_nt(kv[:, :HEAD], group[:ROWS, :]) * FACTOR
            prob_grads = dot_nt(kv[:, HEAD:], group[ROWS:, :])
            upper = jnp.where(gap >= item_ref[row, 2], scores[:BLOCK], MASKED)
            lower = jnp.where(gap >= item_ref[row, 3], scores[BLOCK:], MASKED)
            scores = jnp.concatenate([upper, lower], axis=0)
            score_ref[row] = scores
            pgrad_ref[row] = prob_grads
            highest = jnp.maximum(old, jnp.max(scores, axis=0, keepdims=True))
            weights = jnp.exp(scores - highest)
            shrink = jnp.exp(old - highest)
            totals = totals * shrink + jnp.sum(weights, axis=0, keepdims=True)
            dots = dots * shrink + jnp.sum(weights * prob_grads, axis=0, keepdims=True)
            return highest, totals, dots

        zero = jnp.zeros((1, ROWS), F32)
        start = (jnp.full((1, ROWS), MASKED, F32), zero, zero)
        highest, totals, dots = lax.fori_loop(0, item_ref[NY * PAIRS + j, 0], step, start)
        stat_ref[j, 0:1, :] = highest
        stat_ref[j, 1:2, :] = totals
        stat_ref[j, 2:3, :] = dots
        stat_ref[j, 3:4, :] = zero


def merged(mine, other):
    highest = jnp.maximum(mine[0:1], other[0:1])
    shrink_mine = jnp.exp(mine[0:1] - highest)
    shrink_other = jnp.exp(other[0:1] - highest)
    totals = mine[1:2] * shrink_mine + other[1:2] * shrink_other
    dots = mine[2:3] * shrink_mine + other[2:3] * shrink_other
    return highest, totals, dots


def merge_kernel(item_ref, mine_ref, other_ref, out_ref):
    step = 1 - 2 * (item_ref[NY * PAIRS, 2] & 1)
    for j in range(NY):
        highest, totals, dots = merged(mine_ref[j], other_ref[(j + step) & (NY - 1)])
        out_ref[j, 0:1, :] = highest
        out_ref[j, 1:2, :] = totals
        out_ref[j, 2:3, :] = dots
        out_ref[j, 3:4, :] = dots


def turn_kernel(item_ref, k0, k1, k2, k3, k4, k5, k6, k7, stat_ref, key_cols):
    z = item_ref[NY * PAIRS, 1]
    for r, part in enumerate((k0, k1, k2, k3, k4, k5, k6, k7)):
        key_cols[(z - r) & (NZ - 1)] = part[:, :HEAD].T


def flush_kernel(low_ref, out_ref, sem):
    run_copies([(low_ref, out_ref)], sem)


def grads_kernel(item_ref, cols_ref, score_ref, pgrad_ref, g0, g1, g2, g3, mine_ref, other_ref,
                 dkv_ref, dq0, dq1, dq2, dq3, dk_acc, dv_acc):
    step_to_other = NY - 1 - 2 * item_ref[NY * PAIRS, 2]
    dk_acc[...] = jnp.zeros_like(dk_acc)
    dv_acc[...] = jnp.zeros_like(dv_acc)
    for j, (group, out) in enumerate(zip((g0, g1, g2, g3), (dq0, dq1, dq2, dq3))):
        maxima, totals, dots = merged(mine_ref[j], other_ref[(j + step_to_other) & (NY - 1)])
        log_totals = maxima + jnp.log(totals)
        row_dots = dots / totals

        def step(p, query_grad, j=j, group=group, log_totals=log_totals, row_dots=row_dots):
            row = PAIRS * j + p
            first = item_ref[row, 0]
            second = item_ref[row, 1]
            probs = jnp.exp(score_ref[row] - log_totals)
            score_grads = (probs * (pgrad_ref[row] - row_dots)).astype(BF16)
            dk_pair = dot_nn(score_grads, group[:ROWS, :])
            dv_pair = dot_nn(probs.astype(BF16), group[ROWS:, :])
            dk_acc[first] += dk_pair[:BLOCK]
            dk_acc[second] += dk_pair[BLOCK:]
            dv_acc[first] += dv_pair[:BLOCK]
            dv_acc[second] += dv_pair[BLOCK:]
            cols = jnp.concatenate([cols_ref[first], cols_ref[second]], axis=1)
            return query_grad + dot_nn(cols, score_grads)

        query_grad = lax.fori_loop(0, item_ref[NY * PAIRS + j, 0], step, jnp.zeros((HEAD, ROWS), F32))
        out[...] = (query_grad * FACTOR).astype(BF16)
    for a in range(NZ):
        dkv_ref[a, :, :HEAD] = (dk_acc[a] * FACTOR).astype(BF16)
        dkv_ref[a, :, HEAD:] = dv_acc[a].astype(BF16)


def unrotate(x, cosine, sine):
    front = x[:HEAD // 2]
    back = x[HEAD // 2:]
    return jnp.concatenate([front * cosine + back * sine, back * cosine - front * sine], axis=0)


def weight_rows(place_ref, step):
    core = 1 - place_ref[3] if step < NX else place_ref[3]
    return pl.ds(pl.multiple_of((2 * ((place_ref[2] + step) & (NX - 1)) + core) * ROWS, ROWS), ROWS)


def fetch_kernel(place_ref, anc_ref, dq_ref, wq_hbm, cos_ref, sin_ref, *refs):
    blocks, sem = refs[:-1], refs[-1]
    copies = [
        pltpu.make_async_copy(wq_hbm.at[weight_rows(place_ref, i), :], block, sem.at[i])
        for i, block in enumerate(blocks)
    ]
    for copy in copies:
        copy.start()
    own_block = NY * place_ref[0] + place_ref[1]
    depth = jnp.int32(0)
    for i in range(ANC):
        depth = depth + jnp.where(anc_ref[i, own_block] != own_block, 1, 0)
    half = (HEAD // 2, BLOCK)
    pair = lax.broadcasted_iota(I32, half, 0).astype(F32)
    token_place = (lax.broadcasted_iota(I32, half, 1) + BLOCK * depth).astype(F32)
    angles = jnp.exp(pair * (-2.0 * math.log(ROPE_BASE) / HEAD)) * token_place
    cos_ref[...] = jnp.cos(angles)
    sin_ref[...] = jnp.sin(angles)
    for copy in copies:
        copy.wait()


def start_pair(place_ref, first, wk_hbm, wv_hbm, wk, wv, sem):
    copies = []
    for i in range(NX):
        rows = weight_rows(place_ref, first + i)
        copies.append(pltpu.make_async_copy(wk_hbm.at[rows, :], wk.at[i], sem.at[2 * i]))
        copies.append(pltpu.make_async_copy(wv_hbm.at[rows, :], wv.at[i], sem.at[2 * i + 1]))
    for copy in copies:
        copy.start()
    return copies


def query_part_kernel(place_ref, cos_ref, sin_ref, q0, q1, q2, q3, wk_hbm, wv_hbm, *refs):
    blocks, out_ref, wk, wv, sem = refs[:2 * NX], *refs[2 * NX:]
    copies = start_pair(place_ref, 0, wk_hbm, wv_hbm, wk, wv, sem)
    cosine = cos_ref[...]
    sine = sin_ref[...]
    low = []
    for h in range(GROUP):
        cols = slice(h * HEAD, (h + 1) * HEAD)
        total = q0[:, cols].astype(F32)
        for part in (q1, q2, q3):
            total = total + part[:, cols].astype(F32)
        low.append(unrotate(total, cosine, sine).astype(BF16))
    low = jnp.concatenate(low, axis=0)
    for i, block in enumerate(blocks):
        out_ref[i] = dot_nn(block[...], low).astype(BF16)
    for copy in copies:
        copy.wait()


def first_half_kernel(cos_ref, sin_ref, dkv_ref, part_ref, wk, wv, out_ref, low_ref):
    total = dkv_ref[0].astype(F32)
    for a in range(1, NZ):
        total = total + dkv_ref[a].astype(F32)
    low_ref[:HEAD, :] = unrotate(total[:, :HEAD].T, cos_ref[...], sin_ref[...]).astype(BF16)
    low_ref[HEAD:, :] = total[:, HEAD:].T.astype(BF16)
    for i in range(NX):
        out_ref[i] = (part_ref[i] + key_value_part(low_ref, wk[i], wv[i])).astype(BF16)


def second_half_kernel(place_ref, low_ref, part_ref, wk_hbm, wv_hbm, out_ref, wk, wv, sem):
    copies = start_pair(place_ref, NX, wk_hbm, wv_hbm, wk, wv, sem)
    for i in range(NX):
        for copy in copies[2 * i:2 * i + 2]:
            copy.wait()
        out_ref[i] = part_ref[NX + i] + key_value_part(low_ref, wk[i], wv[i])


def key_value_part(low_ref, wk, wv):
    return dot_nn(wk, low_ref[:HEAD, :]) + dot_nn(wv, low_ref[HEAD:, :])


def finish_kernel(kept_ref, arrived_ref, p0, p1, p2, out_ref):
    for h in range(GROUP):
        rows = slice(h * HEAD, (h + 1) * HEAD)
        total = kept_ref[rows, :]
        for part in (arrived_ref, p0, p1, p2):
            total = total + part[rows, :].astype(F32)
        out_ref[:, rows] = total.T.astype(BF16)


def shift(size, k):
    return [(i, (i + k) % size) for i in range(size)]


def shards(queries, keys, values, out_grad, ancestry, w_query, key_matrix, value_matrix):
    z, y, x, c = (lax.axis_index(name) for name in "zyxc")
    place = jnp.stack([z, y, x, c]).astype(I32)
    group, kv = call(
        stack_kernel,
        [pltpu.VMEM((2 * ROWS, HEAD), BF16), pltpu.VMEM((BLOCK, 2 * HEAD), BF16)],
        [HB] * 4,
        [VM] * 2,
        "stack",
        [pltpu.SemaphoreType.DMA((2 * GROUP + 2,))],
    )(*in_hbm(queries, out_grad, keys, values))
    groups = [group] + [lax.ppermute(group, "y", shift(NY, k)) for k in range(1, NY)]
    below, above = [kv], [kv]
    for r in range(1, NZ // 2):
        below.append(lax.ppermute(below[-1], "z", shift(NZ, 1)))
        above.append(lax.ppermute(above[-1], "z", shift(NZ, -1)))
    kvs = below + [lax.ppermute(below[-1], "z", shift(NZ, 1))] + above[:0:-1]

    items = call(
        plan_kernel,
        jax.ShapeDtypeStruct((NY * PAIRS + NY, 4), I32),
        [SM, SM, VM],
        SM,
        "plan",
        [pltpu.SMEM((NZ + 1,), I32)],
        PLAN_FLOPS,
    )(place, ancestry.T, group)

    tiles = (NY * PAIRS, 2 * BLOCK, ROWS)
    stats, scores, prob_grads = call(
        stats_kernel,
        [jax.ShapeDtypeStruct((NY, 4, ROWS), F32), pltpu.VMEM(tiles, F32), pltpu.VMEM(tiles, F32)],
        [SM] + [VM] * (NZ + NY),
        [VM] * 3,
        "stats",
        [pltpu.VMEM((NZ, BLOCK, 2 * HEAD), BF16)],
        STATS_FLOPS,
    )(items, *kvs, *groups)
    beside = lax.ppermute(stats, "y", [(i, i ^ 1) for i in range(NY)])
    half_stats = call(
        merge_kernel, jax.ShapeDtypeStruct(stats.shape, F32), [SM] + [VM] * 2, VM, "merge",
    )(items, stats, beside)
    other_half = lax.ppermute(half_stats, "y", [(i, NY - 1 - i) for i in range(NY)])
    key_cols = call(
        turn_kernel, pltpu.VMEM((NZ, HEAD, BLOCK), BF16), [SM] + [VM] * (NZ + 1), VM, "turn",
    )(items, *kvs, stats)
    dkv, *dq_parts = call(
        grads_kernel,
        [pltpu.VMEM((NZ, BLOCK, 2 * HEAD), BF16)] + [pltpu.VMEM((HEAD, ROWS), BF16)] * NY,
        [SM] + [VM] * (5 + NY),
        [VM] * (1 + NY),
        "grads",
        [pltpu.VMEM((NZ, BLOCK, HEAD), F32), pltpu.VMEM((NZ, BLOCK, HEAD), F32)],
        GRADS_FLOPS,
    )(items, key_cols, scores, prob_grads, *groups, half_stats, other_half)
    dq_own = [dq_parts[0]] + [lax.ppermute(dq_parts[k], "y", shift(NY, -k)) for k in range(1, NY)]
    dkv = call(
        flush_kernel, pltpu.HBM(dkv.shape, BF16), [VM], HB, "flush", [pltpu.SemaphoreType.DMA((1,))],
    )(dkv)
    dkv_own = lax.all_to_all(dkv, "z", 0, 0, tiled=True)

    wq, wk, wv = in_hbm(w_query, key_matrix, value_matrix)
    cosine, sine, *blocks = call(
        fetch_kernel,
        [pltpu.VMEM((HEAD // 2, BLOCK), F32)] * 2 + [pltpu.VMEM((ROWS, ROWS), BF16)] * (2 * NX),
        [SM, SM, VM, HB],
        [VM] * (2 * NX + 2),
        "fetch",
        [pltpu.SemaphoreType.DMA((2 * NX,))],
    )(place, ancestry.T, dq_parts[0], wq)
    pair_shapes = [pltpu.VMEM((NX, ROWS, HEAD), BF16)] * 2
    query_part, wk_away, wv_away = call(
        query_part_kernel,
        [pltpu.VMEM((2 * NX, ROWS, BLOCK), BF16)] + pair_shapes,
        [SM] + [VM] * (2 + NY) + [HB] * 2 + [VM] * (2 * NX),
        [VM] * 3,
        "query_part",
        [pltpu.SemaphoreType.DMA((2 * NX,))],
        QUERY_FLOPS,
    )(place, cosine, sine, *dq_own, wk, wv, *blocks)
    away, low = call(
        first_half_kernel,
        [pltpu.VMEM((NX, ROWS, BLOCK), BF16), pltpu.VMEM((2 * HEAD, BLOCK), BF16)],
        [VM] * 6,
        [VM] * 2,
        "first_half",
    )(cosine, sine, dkv_own, query_part, wk_away, wv_away)
    arrived = lax.ppermute(away, "c", shift(NC, 1))
    kept = call(
        second_half_kernel,
        pltpu.VMEM((NX, ROWS, BLOCK), F32),
        [SM] + [VM] * 2 + [HB] * 2,
        VM,
        "second_half",
        pair_shapes + [pltpu.SemaphoreType.DMA((2 * NX,))],
    )(place, low, query_part, wk, wv)
    sent = [(kept[k] + arrived[k].astype(F32)).astype(BF16) for k in range(1, NX)]
    parts = [lax.ppermute(sent[k - 1], "x", shift(NX, k)) for k in range(1, NX)]
    return call(
        finish_kernel, jax.ShapeDtypeStruct((BLOCK, ROWS), BF16), [VM] * (2 + len(parts)), VM, "finish",
    )(kept[0], arrived[0], *parts)


def solution(mesh):
    grid = Mesh(mesh.devices.reshape(NZ, NY, NX, NC), ("z", "y", "x", "c"))
    split = P(("z", "y"), ("x", "c"))
    weight = P(None, ("x", "c"))
    return jax.shard_map(
        shards,
        mesh=grid,
        in_specs=(split, split, split, split, P(), weight, weight, weight),
        out_specs=split,
        check_vma=False,
    )
```

```python
import math

import jax
import jax.numpy as jnp
from jax import lax
from jax.experimental import pallas as pl
from jax.experimental.pallas import tpu as pltpu
from jax.sharding import Mesh, PartitionSpec as P

HEAD = 128
BLOCK = 128
GROUP = 5
ROWS = GROUP * BLOCK
NZ, NY, NX, NC = 8, 4, 4, 2
PAIRS = NZ // 2
ANC = 17
ROPE_BASE = 1000000.0
MASKED = -1e30
FACTOR = HEAD ** -0.5
NT = (((1,), (1,)), ((), ()))
NN = (((1,), (0,)), ((), ()))
F32, BF16, I32 = jnp.float32, jnp.bfloat16, jnp.int32
VMEM_LIMIT = 16 << 20
PLAN_FLOPS = 1_000_000_000
STATS_FLOPS = 2 * 2 * (NY * ROWS) * (NZ * BLOCK) * HEAD
GRADS_FLOPS = 3 * 2 * (NY * ROWS) * (NZ * BLOCK) * HEAD
QUERY_FLOPS = 2 * BLOCK * ROWS * 2 * NX * ROWS

VM = pl.BlockSpec(memory_space=pltpu.VMEM)
SM = pl.BlockSpec(memory_space=pltpu.SMEM)
HB = pl.BlockSpec(memory_space=pltpu.HBM)


def dot_nt(a, b):
    return lax.dot_general(a, b, NT, preferred_element_type=F32)


def dot_nn(a, b):
    return lax.dot_general(a, b, NN, preferred_element_type=F32)


def call(body, out_shape, in_specs, out_specs, name, scratch=(), flops=0):
    return pl.pallas_call(
        body,
        out_shape=out_shape,
        in_specs=in_specs,
        out_specs=out_specs,
        scratch_shapes=list(scratch),
        compiler_params=pltpu.CompilerParams(vmem_limit_bytes=VMEM_LIMIT),
        cost_estimate=pl.CostEstimate(flops=flops, transcendentals=0, bytes_accessed=0) if flops else None,
        name=name,
    )


def in_hbm(*arrays):
    return [pltpu.with_memory_space_constraint(a, pltpu.HBM) for a in arrays]


def run_copies(pairs, sem):
    started = [pltpu.make_async_copy(src, dst, sem.at[i]) for i, (src, dst) in enumerate(pairs)]
    for copy in started:
        copy.start()
    for copy in started:
        copy.wait()


def stack_kernel(q_ref, g_ref, k_ref, v_ref, rows_ref, kv_ref, sem):
    pairs = [(k_ref, kv_ref.at[:, 0:HEAD]), (v_ref, kv_ref.at[:, HEAD:2 * HEAD])]
    pairs += [(q_ref, rows_ref.at[:, 0:ROWS]), (g_ref, rows_ref.at[:, ROWS:2 * ROWS])]
    run_copies(pairs, sem)


def head_rows(ref, first):
    return jnp.concatenate([ref[:, first + h * HEAD:first + (h + 1) * HEAD] for h in range(GROUP)], axis=0)


def side_by_side(value):
    return jnp.concatenate([value[h * HEAD:(h + 1) * HEAD, :] for h in range(GROUP)], axis=1)


def plan_kernel(place_ref, anc_ref, rows_ref, item_ref, list_ref):
    z = place_ref[0]
    y = place_ref[1]
    for j in range(NY):
        query_block = NY * z + ((y - j) & (NY - 1))
        bits = jnp.int32(0)
        for i in range(ANC):
            key_block = anc_ref[i, query_block]
            bits = bits | jnp.where((key_block & (NY - 1)) == y, jnp.int32(1) << (key_block >> 2), 0)
        count = jnp.int32(0)
        for key_z in range(NZ):
            list_ref[count] = key_z
            count = count + ((bits >> key_z) & 1)
        for p in range(PAIRS):
            row = PAIRS * j + p
            first = jnp.where(2 * p < count, list_ref[2 * p], 0)
            both = 2 * p + 1 < count
            second = jnp.where(both, list_ref[2 * p + 1], first)
            item_ref[row, 0] = first
            item_ref[row, 1] = second
            causal = jnp.int32(0) if j == 0 else jnp.int32(-BLOCK)
            item_ref[row, 2] = jnp.where(first == z, causal, -BLOCK)
            item_ref[row, 3] = jnp.where(both, jnp.where(second == z, causal, -BLOCK), BLOCK)
        item_ref[NY * PAIRS + j, 0] = (count + 1) // 2
        item_ref[NY * PAIRS + j, 1] = z


def stats_kernel(item_ref, k0, k1, k2, k3, k4, k5, k6, k7, g0, g1, g2, g3, stat_ref, score_ref, pgrad_ref, kv_ref):
    z = item_ref[NY * PAIRS, 1]
    for r, part in enumerate((k0, k1, k2, k3, k4, k5, k6, k7)):
        kv_ref[(z - r) & (NZ - 1)] = part[...]
    key_row = lax.broadcasted_iota(I32, (BLOCK, ROWS), 0)
    query_row = lax.broadcasted_iota(I32, (BLOCK, ROWS), 1) % BLOCK
    gap = query_row - key_row
    for j, group in enumerate((g0, g1, g2, g3)):

        def step(p, carry, j=j, group=group):
            old, totals, dots = carry
            row = PAIRS * j + p
            first = item_ref[row, 0]
            second = item_ref[row, 1]
            kv = jnp.concatenate([kv_ref[first], kv_ref[second]], axis=0)
            scores = dot_nt(kv[:, :HEAD], head_rows(group, 0)) * FACTOR
            prob_grads = dot_nt(kv[:, HEAD:], head_rows(group, ROWS))
            upper = jnp.where(gap >= item_ref[row, 2], scores[:BLOCK], MASKED)
            lower = jnp.where(gap >= item_ref[row, 3], scores[BLOCK:], MASKED)
            scores = jnp.concatenate([upper, lower], axis=0)
            score_ref[row] = scores
            pgrad_ref[row] = prob_grads
            highest = jnp.maximum(old, jnp.max(scores, axis=0, keepdims=True))
            weights = jnp.exp(scores - highest)
            shrink = jnp.exp(old - highest)
            totals = totals * shrink + jnp.sum(weights, axis=0, keepdims=True)
            dots = dots * shrink + jnp.sum(weights * prob_grads, axis=0, keepdims=True)
            return highest, totals, dots

        zero = jnp.zeros((1, ROWS), F32)
        start = (jnp.full((1, ROWS), MASKED, F32), zero, zero)
        highest, totals, dots = lax.fori_loop(0, item_ref[NY * PAIRS + j, 0], step, start)
        stat_ref[j, 0:1, :] = highest
        stat_ref[j, 1:2, :] = totals
        stat_ref[j, 2:3, :] = dots
        stat_ref[j, 3:4, :] = zero


def turn_kernel(item_ref, k0, k1, k2, k3, k4, k5, k6, k7, stat_ref, key_cols):
    z = item_ref[NY * PAIRS, 1]
    for r, part in enumerate((k0, k1, k2, k3, k4, k5, k6, k7)):
        key_cols[(z - r) & (NZ - 1)] = part[:, :HEAD].T


def flush_kernel(low_ref, out_ref, sem):
    run_copies([(low_ref, out_ref)], sem)


def grads_kernel(item_ref, cols_ref, score_ref, pgrad_ref, g0, g1, g2, g3, s0, s1, s2, s3,
                 dkv_ref, dq0, dq1, dq2, dq3, dk_acc, dv_acc):
    stats = (s0, s1, s2, s3)
    dk_acc[...] = jnp.zeros_like(dk_acc)
    dv_acc[...] = jnp.zeros_like(dv_acc)
    for j, (group, out) in enumerate(zip((g0, g1, g2, g3), (dq0, dq1, dq2, dq3))):
        views = [stats[k][(j - k) % NY] for k in range(NY)]
        maxima = views[0][0:1]
        for k in range(1, NY):
            maxima = jnp.maximum(maxima, views[k][0:1])
        totals = jnp.zeros((1, ROWS), F32)
        dots = jnp.zeros((1, ROWS), F32)
        for k in range(NY):
            shrink = jnp.exp(views[k][0:1] - maxima)
            totals = totals + views[k][1:2] * shrink
            dots = dots + views[k][2:3] * shrink
        log_totals = maxima + jnp.log(totals)
        row_dots = dots / totals

        def step(p, query_grad, j=j, group=group, log_totals=log_totals, row_dots=row_dots):
            row = PAIRS * j + p
            first = item_ref[row, 0]
            second = item_ref[row, 1]
            probs = jnp.exp(score_ref[row] - log_totals)
            score_grads = (probs * (pgrad_ref[row] - row_dots)).astype(BF16)
            dk_pair = dot_nn(score_grads, head_rows(group, 0))
            dv_pair = dot_nn(probs.astype(BF16), head_rows(group, ROWS))
            dk_acc[first] += dk_pair[:BLOCK]
            dk_acc[second] += dk_pair[BLOCK:]
            dv_acc[first] += dv_pair[:BLOCK]
            dv_acc[second] += dv_pair[BLOCK:]
            cols = jnp.concatenate([cols_ref[first], cols_ref[second]], axis=1)
            return query_grad + dot_nn(cols, score_grads)

        query_grad = lax.fori_loop(0, item_ref[NY * PAIRS + j, 0], step, jnp.zeros((HEAD, ROWS), F32))
        out[...] = (query_grad * FACTOR).astype(BF16)
    for a in range(NZ):
        dkv_ref[a, :, :HEAD] = (dk_acc[a] * FACTOR).astype(BF16)
        dkv_ref[a, :, HEAD:] = dv_acc[a].astype(BF16)


def unrotate(x, cosine, sine):
    front = x[:HEAD // 2]
    back = x[HEAD // 2:]
    return jnp.concatenate([front * cosine + back * sine, back * cosine - front * sine], axis=0)


def weight_rows(place_ref, step):
    core = 1 - place_ref[3] if step < NX else place_ref[3]
    return pl.ds(pl.multiple_of((2 * ((place_ref[2] + step) & (NX - 1)) + core) * ROWS, ROWS), ROWS)


def fetch_kernel(place_ref, anc_ref, dq_ref, wq_hbm, cos_ref, sin_ref, *refs):
    blocks, sem = refs[:-1], refs[-1]
    copies = [
        pltpu.make_async_copy(wq_hbm.at[weight_rows(place_ref, i), :], block, sem.at[i])
        for i, block in enumerate(blocks)
    ]
    for copy in copies:
        copy.start()
    own_block = NY * place_ref[0] + place_ref[1]
    depth = jnp.int32(0)
    for i in range(ANC):
        depth = depth + jnp.where(anc_ref[i, own_block] != own_block, 1, 0)
    half = (HEAD // 2, BLOCK)
    pair = lax.broadcasted_iota(I32, half, 0).astype(F32)
    token_place = (lax.broadcasted_iota(I32, half, 1) + BLOCK * depth).astype(F32)
    angles = jnp.exp(pair * (-2.0 * math.log(ROPE_BASE) / HEAD)) * token_place
    cos_ref[...] = jnp.cos(angles)
    sin_ref[...] = jnp.sin(angles)
    for copy in copies:
        copy.wait()


def start_pair(place_ref, first, wk_hbm, wv_hbm, wk, wv, sem):
    copies = []
    for i in range(NX):
        rows = weight_rows(place_ref, first + i)
        copies.append(pltpu.make_async_copy(wk_hbm.at[rows, :], wk.at[i], sem.at[2 * i]))
        copies.append(pltpu.make_async_copy(wv_hbm.at[rows, :], wv.at[i], sem.at[2 * i + 1]))
    for copy in copies:
        copy.start()
    return copies


def query_part_kernel(place_ref, cos_ref, sin_ref, q0, q1, q2, q3, wk_hbm, wv_hbm, *refs):
    blocks, out_ref, wk, wv, sem = refs[:2 * NX], *refs[2 * NX:]
    copies = start_pair(place_ref, 0, wk_hbm, wv_hbm, wk, wv, sem)
    cosine = cos_ref[...]
    sine = sin_ref[...]
    low = []
    for h in range(GROUP):
        cols = slice(h * HEAD, (h + 1) * HEAD)
        total = q0[:, cols].astype(F32)
        for part in (q1, q2, q3):
            total = total + part[:, cols].astype(F32)
        low.append(unrotate(total, cosine, sine).astype(BF16))
    low = jnp.concatenate(low, axis=0)
    for i, block in enumerate(blocks):
        out_ref[i] = dot_nn(block[...], low).astype(BF16)
    for copy in copies:
        copy.wait()


def first_half_kernel(cos_ref, sin_ref, dkv_ref, part_ref, wk, wv, out_ref, low_ref):
    total = dkv_ref[0].astype(F32)
    for a in range(1, NZ):
        total = total + dkv_ref[a].astype(F32)
    low_ref[:HEAD, :] = unrotate(total[:, :HEAD].T, cos_ref[...], sin_ref[...]).astype(BF16)
    low_ref[HEAD:, :] = total[:, HEAD:].T.astype(BF16)
    for i in range(NX):
        total = part_ref[i] + key_value_part(low_ref, wk[i], wv[i])
        out_ref[i] = side_by_side(total).astype(BF16)


def second_half_kernel(place_ref, low_ref, part_ref, wk_hbm, wv_hbm, out_ref, wk, wv, sem):
    copies = start_pair(place_ref, NX, wk_hbm, wv_hbm, wk, wv, sem)
    for i in range(NX):
        for copy in copies[2 * i:2 * i + 2]:
            copy.wait()
        out_ref[i] = side_by_side(part_ref[NX + i] + key_value_part(low_ref, wk[i], wv[i]))


def key_value_part(low_ref, wk, wv):
    return dot_nn(wk, low_ref[:HEAD, :]) + dot_nn(wv, low_ref[HEAD:, :])


def finish_kernel(kept_ref, arrived_ref, p0, p1, p2, out_ref):
    for h in range(GROUP):
        cols = slice(h * HEAD, (h + 1) * HEAD)
        total = kept_ref[:, cols]
        for part in (arrived_ref, p0, p1, p2):
            total = total + part[:, cols].astype(F32)
        out_ref[:, cols] = total.T.astype(BF16)


def shift(size, k):
    return [(i, (i + k) % size) for i in range(size)]


def shards(queries, keys, values, out_grad, ancestry, w_query, key_matrix, value_matrix):
    z, y, x, c = (lax.axis_index(name) for name in "zyxc")
    place = jnp.stack([z, y, x, c]).astype(I32)
    group, kv = call(
        stack_kernel,
        [pltpu.VMEM((BLOCK, 2 * ROWS), BF16), pltpu.VMEM((BLOCK, 2 * HEAD), BF16)],
        [HB] * 4,
        [VM] * 2,
        "stack",
        [pltpu.SemaphoreType.DMA((4,))],
    )(*in_hbm(queries, out_grad, keys, values))
    groups = [group] + [lax.ppermute(group, "y", shift(NY, k)) for k in range(1, NY)]
    below, above = [kv], [kv]
    for r in range(1, NZ // 2):
        below.append(lax.ppermute(below[-1], "z", shift(NZ, 1)))
        above.append(lax.ppermute(above[-1], "z", shift(NZ, -1)))
    kvs = below + [lax.ppermute(below[-1], "z", shift(NZ, 1))] + above[:0:-1]

    items = call(
        plan_kernel,
        jax.ShapeDtypeStruct((NY * PAIRS + NY, 4), I32),
        [SM, SM, VM],
        SM,
        "plan",
        [pltpu.SMEM((NZ + 1,), I32)],
        PLAN_FLOPS,
    )(place, ancestry.T, group)

    tiles = (NY * PAIRS, 2 * BLOCK, ROWS)
    stats, scores, prob_grads = call(
        stats_kernel,
        [jax.ShapeDtypeStruct((NY, 4, ROWS), F32), pltpu.VMEM(tiles, F32), pltpu.VMEM(tiles, F32)],
        [SM] + [VM] * (NZ + NY),
        [VM] * 3,
        "stats",
        [pltpu.VMEM((NZ, BLOCK, 2 * HEAD), BF16)],
        STATS_FLOPS,
    )(items, *kvs, *groups)
    all_stats = [stats] + [lax.ppermute(stats, "y", shift(NY, k)) for k in range(1, NY)]
    key_cols = call(
        turn_kernel, pltpu.VMEM((NZ, HEAD, BLOCK), BF16), [SM] + [VM] * (NZ + 1), VM, "turn",
    )(items, *kvs, stats)
    dkv, *dq_parts = call(
        grads_kernel,
        [pltpu.VMEM((NZ, BLOCK, 2 * HEAD), BF16)] + [pltpu.VMEM((HEAD, ROWS), BF16)] * NY,
        [SM] + [VM] * (3 + 2 * NY),
        [VM] * (1 + NY),
        "grads",
        [pltpu.VMEM((NZ, BLOCK, HEAD), F32), pltpu.VMEM((NZ, BLOCK, HEAD), F32)],
        GRADS_FLOPS,
    )(items, key_cols, scores, prob_grads, *groups, *all_stats)
    dq_own = [dq_parts[0]] + [lax.ppermute(dq_parts[k], "y", shift(NY, -k)) for k in range(1, NY)]
    dkv = call(
        flush_kernel, pltpu.HBM(dkv.shape, BF16), [VM], HB, "flush", [pltpu.SemaphoreType.DMA((1,))],
    )(dkv)
    dkv_own = lax.all_to_all(dkv, "z", 0, 0, tiled=True)

    wq, wk, wv = in_hbm(w_query, key_matrix, value_matrix)
    cosine, sine, *blocks = call(
        fetch_kernel,
        [pltpu.VMEM((HEAD // 2, BLOCK), F32)] * 2 + [pltpu.VMEM((ROWS, ROWS), BF16)] * (2 * NX),
        [SM, SM, VM, HB],
        [VM] * (2 * NX + 2),
        "fetch",
        [pltpu.SemaphoreType.DMA((2 * NX,))],
    )(place, ancestry.T, dq_parts[0], wq)
    pair_shapes = [pltpu.VMEM((NX, ROWS, HEAD), BF16)] * 2
    query_part, wk_away, wv_away = call(
        query_part_kernel,
        [pltpu.VMEM((2 * NX, ROWS, BLOCK), BF16)] + pair_shapes,
        [SM] + [VM] * (2 + NY) + [HB] * 2 + [VM] * (2 * NX),
        [VM] * 3,
        "query_part",
        [pltpu.SemaphoreType.DMA((2 * NX,))],
        QUERY_FLOPS,
    )(place, cosine, sine, *dq_own, wk, wv, *blocks)
    away, low = call(
        first_half_kernel,
        [pltpu.VMEM((NX, BLOCK, ROWS), BF16), pltpu.VMEM((2 * HEAD, BLOCK), BF16)],
        [VM] * 6,
        [VM] * 2,
        "first_half",
    )(cosine, sine, dkv_own, query_part, wk_away, wv_away)
    arrived = lax.ppermute(away, "c", shift(NC, 1))
    kept = call(
        second_half_kernel,
        pltpu.VMEM((NX, BLOCK, ROWS), F32),
        [SM] + [VM] * 2 + [HB] * 2,
        VM,
        "second_half",
        pair_shapes + [pltpu.SemaphoreType.DMA((2 * NX,))],
    )(place, low, query_part, wk, wv)
    sent = [(kept[k] + arrived[k].astype(F32)).astype(BF16) for k in range(1, NX)]
    parts = [lax.ppermute(sent[k - 1], "x", shift(NX, k)) for k in range(1, NX)]
    return call(
        finish_kernel, jax.ShapeDtypeStruct((BLOCK, ROWS), BF16), [VM] * (2 + len(parts)), VM, "finish",
    )(kept[0], arrived[0], *parts)


def solution(mesh):
    grid = Mesh(mesh.devices.reshape(NZ, NY, NX, NC), ("z", "y", "x", "c"))
    split = P(("z", "y"), ("x", "c"))
    weight = P(None, ("x", "c"))
    return jax.shard_map(
        shards,
        mesh=grid,
        in_specs=(split, split, split, split, P(), weight, weight, weight),
        out_specs=split,
        check_vma=False,
    )
```

```python
import math

import jax
import jax.numpy as jnp
from jax import lax
from jax.experimental import pallas as pl
from jax.experimental.pallas import tpu as pltpu
from jax.sharding import Mesh, PartitionSpec as P

HEAD = 128
BLOCK = 128
GROUP = 5
ROWS = GROUP * BLOCK
NZ, NY, NX, NC = 8, 4, 4, 2
PAIRS = NZ // 2
ANC = 17
ROPE_BASE = 1000000.0
MASKED = -1e30
FACTOR = HEAD ** -0.5
NT = (((1,), (1,)), ((), ()))
NN = (((1,), (0,)), ((), ()))
F32, BF16, I32 = jnp.float32, jnp.bfloat16, jnp.int32
VMEM_LIMIT = 16 << 20
PLAN_FLOPS = 1_000_000_000
STATS_FLOPS = 2 * 2 * (NY * ROWS) * (NZ * BLOCK) * HEAD
GRADS_FLOPS = 3 * 2 * (NY * ROWS) * (NZ * BLOCK) * HEAD
QUERY_FLOPS = 2 * BLOCK * ROWS * 2 * NX * ROWS

VM = pl.BlockSpec(memory_space=pltpu.VMEM)
SM = pl.BlockSpec(memory_space=pltpu.SMEM)
HB = pl.BlockSpec(memory_space=pltpu.HBM)


def dot_nt(a, b):
    return lax.dot_general(a, b, NT, preferred_element_type=F32)


def dot_nn(a, b):
    return lax.dot_general(a, b, NN, preferred_element_type=F32)


def call(body, out_shape, in_specs, out_specs, name, scratch=(), flops=0):
    return pl.pallas_call(
        body,
        out_shape=out_shape,
        in_specs=in_specs,
        out_specs=out_specs,
        scratch_shapes=list(scratch),
        compiler_params=pltpu.CompilerParams(vmem_limit_bytes=VMEM_LIMIT),
        cost_estimate=pl.CostEstimate(flops=flops, transcendentals=0, bytes_accessed=0) if flops else None,
        name=name,
    )


def in_hbm(*arrays):
    return [pltpu.with_memory_space_constraint(a, pltpu.HBM) for a in arrays]


def run_copies(pairs, sem):
    started = [pltpu.make_async_copy(src, dst, sem.at[i]) for i, (src, dst) in enumerate(pairs)]
    for copy in started:
        copy.start()
    for copy in started:
        copy.wait()


def stack_kernel(q_ref, g_ref, k_ref, v_ref, rows_ref, kv_ref, sem):
    pairs = [(k_ref, kv_ref.at[:, 0:HEAD]), (v_ref, kv_ref.at[:, HEAD:2 * HEAD])]
    pairs += [(q_ref, rows_ref.at[:, 0:ROWS]), (g_ref, rows_ref.at[:, ROWS:2 * ROWS])]
    run_copies(pairs, sem)


def head_rows(ref, first):
    return jnp.concatenate([ref[:, first + h * HEAD:first + (h + 1) * HEAD] for h in range(GROUP)], axis=0)


def side_by_side(value):
    return jnp.concatenate([value[h * HEAD:(h + 1) * HEAD, :] for h in range(GROUP)], axis=1)


def plan_kernel(place_ref, anc_ref, rows_ref, item_ref, list_ref):
    z = place_ref[0]
    y = place_ref[1]
    for j in range(NY):
        query_block = NY * z + ((y - j) & (NY - 1))
        bits = jnp.int32(0)
        for i in range(ANC):
            key_block = anc_ref[i, query_block]
            bits = bits | jnp.where((key_block & (NY - 1)) == y, jnp.int32(1) << (key_block >> 2), 0)
        count = jnp.int32(0)
        for key_z in range(NZ):
            list_ref[count] = key_z
            count = count + ((bits >> key_z) & 1)
        for p in range(PAIRS):
            row = PAIRS * j + p
            first = jnp.where(2 * p < count, list_ref[2 * p], 0)
            both = 2 * p + 1 < count
            second = jnp.where(both, list_ref[2 * p + 1], first)
            item_ref[row, 0] = first
            item_ref[row, 1] = second
            causal = jnp.int32(0) if j == 0 else jnp.int32(-BLOCK)
            item_ref[row, 2] = jnp.where(first == z, causal, -BLOCK)
            item_ref[row, 3] = jnp.where(both, jnp.where(second == z, causal, -BLOCK), BLOCK)
        item_ref[NY * PAIRS + j, 0] = (count + 1) // 2
        item_ref[NY * PAIRS + j, 1] = z


def stats_kernel(item_ref, k0, k1, k2, k3, k4, k5, k6, k7, g0, g3, g2, g1, stat_ref, score_ref, pgrad_ref, kv_ref):
    z = item_ref[NY * PAIRS, 1]
    for r, part in enumerate((k0, k1, k2, k3, k4, k5, k6, k7)):
        kv_ref[(z - r) & (NZ - 1)] = part[...]
    key_row = lax.broadcasted_iota(I32, (BLOCK, ROWS), 0)
    query_row = lax.broadcasted_iota(I32, (BLOCK, ROWS), 1) % BLOCK
    gap = query_row - key_row
    for j, group in enumerate((g0, g1, g2, g3)):

        def step(p, carry, j=j, group=group):
            old, totals, dots = carry
            row = PAIRS * j + p
            first = item_ref[row, 0]
            second = item_ref[row, 1]
            kv = jnp.concatenate([kv_ref[first], kv_ref[second]], axis=0)
            scores = dot_nt(kv[:, :HEAD], head_rows(group, 0)) * FACTOR
            prob_grads = dot_nt(kv[:, HEAD:], head_rows(group, ROWS))
            upper = jnp.where(gap >= item_ref[row, 2], scores[:BLOCK], MASKED)
            lower = jnp.where(gap >= item_ref[row, 3], scores[BLOCK:], MASKED)
            scores = jnp.concatenate([upper, lower], axis=0)
            score_ref[row] = scores
            pgrad_ref[row] = prob_grads
            highest = jnp.maximum(old, jnp.max(scores, axis=0, keepdims=True))
            weights = jnp.exp(scores - highest)
            shrink = jnp.exp(old - highest)
            totals = totals * shrink + jnp.sum(weights, axis=0, keepdims=True)
            dots = dots * shrink + jnp.sum(weights * prob_grads, axis=0, keepdims=True)
            return highest, totals, dots

        zero = jnp.zeros((1, ROWS), F32)
        start = (jnp.full((1, ROWS), MASKED, F32), zero, zero)
        highest, totals, dots = lax.fori_loop(0, item_ref[NY * PAIRS + j, 0], step, start)
        stat_ref[j, 0:1, :] = highest
        stat_ref[j, 1:2, :] = totals
        stat_ref[j, 2:3, :] = dots
        stat_ref[j, 3:4, :] = zero


def turn_kernel(item_ref, k0, k1, k2, k3, k4, k5, k6, k7, stat_ref, key_cols):
    z = item_ref[NY * PAIRS, 1]
    for r, part in enumerate((k0, k1, k2, k3, k4, k5, k6, k7)):
        key_cols[(z - r) & (NZ - 1)] = part[:, :HEAD].T


def flush_kernel(low_ref, out_ref, sem):
    run_copies([(low_ref, out_ref)], sem)


def grads_kernel(item_ref, cols_ref, score_ref, pgrad_ref, g0, g1, g2, g3, s0, s3, s2, s1,
                 dkv_ref, dq0, dq1, dq2, dq3, dk_acc, dv_acc):
    stats = (s0, s1, s2, s3)
    dk_acc[...] = jnp.zeros_like(dk_acc)
    dv_acc[...] = jnp.zeros_like(dv_acc)
    for j, (group, out) in enumerate(zip((g0, g1, g2, g3), (dq0, dq1, dq2, dq3))):
        views = [stats[k][(j - k) % NY] for k in range(NY)]
        maxima = views[0][0:1]
        for k in range(1, NY):
            maxima = jnp.maximum(maxima, views[k][0:1])
        totals = jnp.zeros((1, ROWS), F32)
        dots = jnp.zeros((1, ROWS), F32)
        for k in range(NY):
            shrink = jnp.exp(views[k][0:1] - maxima)
            totals = totals + views[k][1:2] * shrink
            dots = dots + views[k][2:3] * shrink
        log_totals = maxima + jnp.log(totals)
        row_dots = dots / totals

        def step(p, query_grad, j=j, group=group, log_totals=log_totals, row_dots=row_dots):
            row = PAIRS * j + p
            first = item_ref[row, 0]
            second = item_ref[row, 1]
            probs = jnp.exp(score_ref[row] - log_totals)
            score_grads = (probs * (pgrad_ref[row] - row_dots)).astype(BF16)
            dk_pair = dot_nn(score_grads, head_rows(group, 0))
            dv_pair = dot_nn(probs.astype(BF16), head_rows(group, ROWS))
            dk_acc[first] += dk_pair[:BLOCK]
            dk_acc[second] += dk_pair[BLOCK:]
            dv_acc[first] += dv_pair[:BLOCK]
            dv_acc[second] += dv_pair[BLOCK:]
            cols = jnp.concatenate([cols_ref[first], cols_ref[second]], axis=1)
            return query_grad + dot_nn(cols, score_grads)

        query_grad = lax.fori_loop(0, item_ref[NY * PAIRS + j, 0], step, jnp.zeros((HEAD, ROWS), F32))
        out[...] = (query_grad * FACTOR).astype(BF16)
    for a in range(NZ):
        dkv_ref[a, :, :HEAD] = (dk_acc[a] * FACTOR).astype(BF16)
        dkv_ref[a, :, HEAD:] = dv_acc[a].astype(BF16)


def unrotate(x, cosine, sine):
    front = x[:HEAD // 2]
    back = x[HEAD // 2:]
    return jnp.concatenate([front * cosine + back * sine, back * cosine - front * sine], axis=0)


def weight_rows(place_ref, step):
    core = 1 - place_ref[3] if step < NX else place_ref[3]
    return pl.ds(pl.multiple_of((2 * ((place_ref[2] + step) & (NX - 1)) + core) * ROWS, ROWS), ROWS)


def fetch_kernel(place_ref, anc_ref, dq_ref, wq_hbm, cos_ref, sin_ref, *refs):
    blocks, sem = refs[:-1], refs[-1]
    copies = [
        pltpu.make_async_copy(wq_hbm.at[weight_rows(place_ref, i), :], block, sem.at[i])
        for i, block in enumerate(blocks)
    ]
    for copy in copies:
        copy.start()
    own_block = NY * place_ref[0] + place_ref[1]
    depth = jnp.int32(0)
    for i in range(ANC):
        depth = depth + jnp.where(anc_ref[i, own_block] != own_block, 1, 0)
    half = (HEAD // 2, BLOCK)
    pair = lax.broadcasted_iota(I32, half, 0).astype(F32)
    token_place = (lax.broadcasted_iota(I32, half, 1) + BLOCK * depth).astype(F32)
    angles = jnp.exp(pair * (-2.0 * math.log(ROPE_BASE) / HEAD)) * token_place
    cos_ref[...] = jnp.cos(angles)
    sin_ref[...] = jnp.sin(angles)
    for copy in copies:
        copy.wait()


def start_pair(place_ref, first, wk_hbm, wv_hbm, wk, wv, sem):
    copies = []
    for i in range(NX):
        rows = weight_rows(place_ref, first + i)
        copies.append(pltpu.make_async_copy(wk_hbm.at[rows, :], wk.at[i], sem.at[2 * i]))
        copies.append(pltpu.make_async_copy(wv_hbm.at[rows, :], wv.at[i], sem.at[2 * i + 1]))
    for copy in copies:
        copy.start()
    return copies


def query_part_kernel(place_ref, cos_ref, sin_ref, q0, q1, q2, q3, wk_hbm, wv_hbm, *refs):
    blocks, out_ref, wk, wv, sem = refs[:2 * NX], *refs[2 * NX:]
    copies = start_pair(place_ref, 0, wk_hbm, wv_hbm, wk, wv, sem)
    cosine = cos_ref[...]
    sine = sin_ref[...]
    low = []
    for h in range(GROUP):
        cols = slice(h * HEAD, (h + 1) * HEAD)
        total = q0[:, cols].astype(F32)
        for part in (q1, q2, q3):
            total = total + part[:, cols].astype(F32)
        low.append(unrotate(total, cosine, sine).astype(BF16))
    low = jnp.concatenate(low, axis=0)
    for i, block in enumerate(blocks):
        out_ref[i] = dot_nn(block[...], low).astype(BF16)
    for copy in copies:
        copy.wait()


def first_half_kernel(cos_ref, sin_ref, dkv_ref, part_ref, wk, wv, out_ref, low_ref):
    total = dkv_ref[0].astype(F32)
    for a in range(1, NZ):
        total = total + dkv_ref[a].astype(F32)
    low_ref[:HEAD, :] = unrotate(total[:, :HEAD].T, cos_ref[...], sin_ref[...]).astype(BF16)
    low_ref[HEAD:, :] = total[:, HEAD:].T.astype(BF16)
    for i in range(NX):
        total = part_ref[i] + key_value_part(low_ref, wk[i], wv[i])
        out_ref[i] = side_by_side(total).astype(BF16)


def second_half_kernel(place_ref, low_ref, part_ref, wk_hbm, wv_hbm, out_ref, wk, wv, sem):
    copies = start_pair(place_ref, NX, wk_hbm, wv_hbm, wk, wv, sem)
    for i in range(NX):
        for copy in copies[2 * i:2 * i + 2]:
            copy.wait()
        out_ref[i] = side_by_side(part_ref[NX + i] + key_value_part(low_ref, wk[i], wv[i]))


def key_value_part(low_ref, wk, wv):
    return dot_nn(wk, low_ref[:HEAD, :]) + dot_nn(wv, low_ref[HEAD:, :])


def finish_kernel(kept_ref, p2, p1, p0, arrived_ref, out_ref):
    for h in range(GROUP):
        cols = slice(h * HEAD, (h + 1) * HEAD)
        total = kept_ref[:, cols]
        for part in (arrived_ref, p0, p1, p2):
            total = total + part[:, cols].astype(F32)
        out_ref[:, cols] = total.T.astype(BF16)


def shift(size, k):
    return [(i, (i + k) % size) for i in range(size)]


def shards(queries, keys, values, out_grad, ancestry, w_query, key_matrix, value_matrix):
    z, y, x, c = (lax.axis_index(name) for name in "zyxc")
    place = jnp.stack([z, y, x, c]).astype(I32)
    group, kv = call(
        stack_kernel,
        [pltpu.VMEM((BLOCK, 2 * ROWS), BF16), pltpu.VMEM((BLOCK, 2 * HEAD), BF16)],
        [HB] * 4,
        [VM] * 2,
        "stack",
        [pltpu.SemaphoreType.DMA((4,))],
    )(*in_hbm(queries, out_grad, keys, values))
    groups = [group] + [lax.ppermute(group, "y", shift(NY, k)) for k in range(1, NY)]
    below, above = [kv], [kv]
    for r in range(1, NZ // 2):
        below.append(lax.ppermute(below[-1], "z", shift(NZ, 1)))
        above.append(lax.ppermute(above[-1], "z", shift(NZ, -1)))
    kvs = below + [lax.ppermute(below[-1], "z", shift(NZ, 1))] + above[:0:-1]

    items = call(
        plan_kernel,
        jax.ShapeDtypeStruct((NY * PAIRS + NY, 4), I32),
        [SM, SM, VM],
        SM,
        "plan",
        [pltpu.SMEM((NZ + 1,), I32)],
        PLAN_FLOPS,
    )(place, ancestry.T, group)

    tiles = (NY * PAIRS, 2 * BLOCK, ROWS)
    stats, scores, prob_grads = call(
        stats_kernel,
        [jax.ShapeDtypeStruct((NY, 4, ROWS), F32), pltpu.VMEM(tiles, F32), pltpu.VMEM(tiles, F32)],
        [SM] + [VM] * (NZ + NY),
        [VM] * 3,
        "stats",
        [pltpu.VMEM((NZ, BLOCK, 2 * HEAD), BF16)],
        STATS_FLOPS,
    )(items, *kvs, group, *groups[:0:-1])
    all_stats = [stats] + [lax.ppermute(stats, "y", shift(NY, k)) for k in range(1, NY)]
    key_cols = call(
        turn_kernel, pltpu.VMEM((NZ, HEAD, BLOCK), BF16), [SM] + [VM] * (NZ + 1), VM, "turn",
    )(items, *kvs, stats)
    dkv, *dq_parts = call(
        grads_kernel,
        [pltpu.VMEM((NZ, BLOCK, 2 * HEAD), BF16)] + [pltpu.VMEM((HEAD, ROWS), BF16)] * NY,
        [SM] + [VM] * (3 + 2 * NY),
        [VM] * (1 + NY),
        "grads",
        [pltpu.VMEM((NZ, BLOCK, HEAD), F32), pltpu.VMEM((NZ, BLOCK, HEAD), F32)],
        GRADS_FLOPS,
    )(items, key_cols, scores, prob_grads, *groups, all_stats[0], *all_stats[:0:-1])
    dq_own = [dq_parts[0]] + [lax.ppermute(dq_parts[k], "y", shift(NY, -k)) for k in range(1, NY)]
    dkv = call(
        flush_kernel, pltpu.HBM(dkv.shape, BF16), [VM], HB, "flush", [pltpu.SemaphoreType.DMA((1,))],
    )(dkv)
    dkv_own = lax.all_to_all(dkv, "z", 0, 0, tiled=True)

    wq, wk, wv = in_hbm(w_query, key_matrix, value_matrix)
    cosine, sine, *blocks = call(
        fetch_kernel,
        [pltpu.VMEM((HEAD // 2, BLOCK), F32)] * 2 + [pltpu.VMEM((ROWS, ROWS), BF16)] * (2 * NX),
        [SM, SM, VM, HB],
        [VM] * (2 * NX + 2),
        "fetch",
        [pltpu.SemaphoreType.DMA((2 * NX,))],
    )(place, ancestry.T, dq_parts[0], wq)
    pair_shapes = [pltpu.VMEM((NX, ROWS, HEAD), BF16)] * 2
    query_part, wk_away, wv_away = call(
        query_part_kernel,
        [pltpu.VMEM((2 * NX, ROWS, BLOCK), BF16)] + pair_shapes,
        [SM] + [VM] * (2 + NY) + [HB] * 2 + [VM] * (2 * NX),
        [VM] * 3,
        "query_part",
        [pltpu.SemaphoreType.DMA((2 * NX,))],
        QUERY_FLOPS,
    )(place, cosine, sine, *dq_own, wk, wv, *blocks)
    away, low = call(
        first_half_kernel,
        [pltpu.VMEM((NX, BLOCK, ROWS), BF16), pltpu.VMEM((2 * HEAD, BLOCK), BF16)],
        [VM] * 6,
        [VM] * 2,
        "first_half",
    )(cosine, sine, dkv_own, query_part, wk_away, wv_away)
    arrived = lax.ppermute(away, "c", shift(NC, 1))
    kept = call(
        second_half_kernel,
        pltpu.VMEM((NX, BLOCK, ROWS), F32),
        [SM] + [VM] * 2 + [HB] * 2,
        VM,
        "second_half",
        pair_shapes + [pltpu.SemaphoreType.DMA((2 * NX,))],
    )(place, low, query_part, wk, wv)
    sent = [(kept[k] + arrived[k].astype(F32)).astype(BF16) for k in range(1, NX)]
    parts = [lax.ppermute(sent[k - 1], "x", shift(NX, k)) for k in range(1, NX)]
    return call(
        finish_kernel, jax.ShapeDtypeStruct((BLOCK, ROWS), BF16), [VM] * (2 + len(parts)), VM, "finish",
    )(kept[0], *parts[::-1], arrived[0])


def solution(mesh):
    grid = Mesh(mesh.devices.reshape(NZ, NY, NX, NC), ("z", "y", "x", "c"))
    split = P(("z", "y"), ("x", "c"))
    weight = P(None, ("x", "c"))
    return jax.shard_map(
        shards,
        mesh=grid,
        in_specs=(split, split, split, split, P(), weight, weight, weight),
        out_specs=split,
        check_vma=False,
    )
```

```python
import math

import jax
import jax.numpy as jnp
from jax import lax
from jax.experimental import pallas as pl
from jax.experimental.pallas import tpu as pltpu
from jax.sharding import Mesh, PartitionSpec as P

HEAD = 128
BLOCK = 128
GROUP = 5
ROWS = GROUP * BLOCK
NZ, NY, NX, NC = 8, 4, 4, 2
PAIRS = NZ // 2
ANC = 17
ROPE_BASE = 1000000.0
MASKED = -1e30
FACTOR = HEAD ** -0.5
NT = (((1,), (1,)), ((), ()))
NN = (((1,), (0,)), ((), ()))
F32, BF16, I32 = jnp.float32, jnp.bfloat16, jnp.int32
VMEM_LIMIT = 16 << 20
PLAN_FLOPS = 1_000_000_000
STATS_FLOPS = 2 * 2 * (NY * ROWS) * (NZ * BLOCK) * HEAD
GRADS_FLOPS = 3 * 2 * (NY * ROWS) * (NZ * BLOCK) * HEAD
QUERY_FLOPS = 2 * BLOCK * ROWS * 2 * NX * ROWS

VM = pl.BlockSpec(memory_space=pltpu.VMEM)
SM = pl.BlockSpec(memory_space=pltpu.SMEM)
HB = pl.BlockSpec(memory_space=pltpu.HBM)


def dot_nt(a, b):
    return lax.dot_general(a, b, NT, preferred_element_type=F32)


def dot_nn(a, b):
    return lax.dot_general(a, b, NN, preferred_element_type=F32)


def call(body, out_shape, in_specs, out_specs, name, scratch=(), flops=0):
    return pl.pallas_call(
        body,
        out_shape=out_shape,
        in_specs=in_specs,
        out_specs=out_specs,
        scratch_shapes=list(scratch),
        compiler_params=pltpu.CompilerParams(vmem_limit_bytes=VMEM_LIMIT),
        cost_estimate=pl.CostEstimate(flops=flops, transcendentals=0, bytes_accessed=0) if flops else None,
        name=name,
    )


def in_hbm(*arrays):
    return [pltpu.with_memory_space_constraint(a, pltpu.HBM) for a in arrays]


def run_copies(pairs, sem):
    started = [pltpu.make_async_copy(src, dst, sem.at[i]) for i, (src, dst) in enumerate(pairs)]
    for copy in started:
        copy.start()
    for copy in started:
        copy.wait()


def stack_kernel(q_ref, g_ref, k_ref, v_ref, rows_ref, kv_ref, sem):
    pairs = [(k_ref, kv_ref.at[:, 0:HEAD]), (v_ref, kv_ref.at[:, HEAD:2 * HEAD])]
    pairs += [(q_ref, rows_ref.at[:, 0:ROWS]), (g_ref, rows_ref.at[:, ROWS:2 * ROWS])]
    run_copies(pairs, sem)


def head_rows(ref, first):
    return jnp.concatenate([ref[:, first + h * HEAD:first + (h + 1) * HEAD] for h in range(GROUP)], axis=0)


def side_by_side(value):
    return jnp.concatenate([value[h * HEAD:(h + 1) * HEAD, :] for h in range(GROUP)], axis=1)


def plan_kernel(place_ref, anc_ref, rows_ref, item_ref, list_ref):
    z = place_ref[0]
    y = place_ref[1]
    for j in range(NY):
        query_block = NY * z + ((y - j) & (NY - 1))
        bits = jnp.int32(0)
        for i in range(ANC):
            key_block = anc_ref[i, query_block]
            bits = bits | jnp.where((key_block & (NY - 1)) == y, jnp.int32(1) << (key_block >> 2), 0)
        count = jnp.int32(0)
        for key_z in range(NZ):
            list_ref[count] = key_z
            count = count + ((bits >> key_z) & 1)
        for p in range(PAIRS):
            row = PAIRS * j + p
            first = jnp.where(2 * p < count, list_ref[2 * p], 0)
            both = 2 * p + 1 < count
            second = jnp.where(both, list_ref[2 * p + 1], first)
            item_ref[row, 0] = first
            item_ref[row, 1] = second
            causal = jnp.int32(0) if j == 0 else jnp.int32(-BLOCK)
            item_ref[row, 2] = jnp.where(first == z, causal, -BLOCK)
            item_ref[row, 3] = jnp.where(both, jnp.where(second == z, causal, -BLOCK), BLOCK)
        item_ref[NY * PAIRS + j, 0] = (count + 1) // 2
        item_ref[NY * PAIRS + j, 1] = z


def stats_kernel(item_ref, k0, k1, k2, k3, k4, k5, k6, k7, g0, g3, g2, g1, stat_ref, score_ref, pgrad_ref, kv_ref):
    z = item_ref[NY * PAIRS, 1]
    for r, part in enumerate((k0, k1, k2, k3, k4, k5, k6, k7)):
        kv_ref[(z - r) & (NZ - 1)] = part[...]
    key_row = lax.broadcasted_iota(I32, (BLOCK, ROWS), 0)
    query_row = lax.broadcasted_iota(I32, (BLOCK, ROWS), 1) % BLOCK
    gap = query_row - key_row
    for j, group in enumerate((g0, g1, g2, g3)):

        def step(p, carry, j=j, group=group):
            old, totals, dots = carry
            row = PAIRS * j + p
            first = item_ref[row, 0]
            second = item_ref[row, 1]
            kv = jnp.concatenate([kv_ref[first], kv_ref[second]], axis=0)
            scores = dot_nt(kv[:, :HEAD], head_rows(group, 0)) * FACTOR
            prob_grads = dot_nt(kv[:, HEAD:], head_rows(group, ROWS))
            upper = jnp.where(gap >= item_ref[row, 2], scores[:BLOCK], MASKED)
            lower = jnp.where(gap >= item_ref[row, 3], scores[BLOCK:], MASKED)
            scores = jnp.concatenate([upper, lower], axis=0)
            score_ref[row] = scores
            pgrad_ref[row] = prob_grads
            highest = jnp.maximum(old, jnp.max(scores, axis=0, keepdims=True))
            weights = jnp.exp(scores - highest)
            shrink = jnp.exp(old - highest)
            totals = totals * shrink + jnp.sum(weights, axis=0, keepdims=True)
            dots = dots * shrink + jnp.sum(weights * prob_grads, axis=0, keepdims=True)
            return highest, totals, dots

        zero = jnp.zeros((1, ROWS), F32)
        start = (jnp.full((1, ROWS), MASKED, F32), zero, zero)
        highest, totals, dots = lax.fori_loop(0, item_ref[NY * PAIRS + j, 0], step, start)
        stat_ref[j, 0:1, :] = highest
        stat_ref[j, 1:2, :] = totals
        stat_ref[j, 2:3, :] = dots
        stat_ref[j, 3:4, :] = zero


def turn_kernel(item_ref, k0, k1, k2, k3, k4, k5, k6, k7, stat_ref, key_cols):
    z = item_ref[NY * PAIRS, 1]
    for r, part in enumerate((k0, k1, k2, k3, k4, k5, k6, k7)):
        key_cols[(z - r) & (NZ - 1)] = part[:, :HEAD].T


def flush_kernel(low_ref, out_ref, sem):
    run_copies([(low_ref, out_ref)], sem)


def grads_kernel(item_ref, cols_ref, score_ref, pgrad_ref, g0, g1, g2, g3, s0, s3, s2, s1,
                 dkv_ref, dq0, dq1, dq2, dq3, dk_acc, dv_acc):
    stats = (s0, s1, s2, s3)
    dk_acc[...] = jnp.zeros_like(dk_acc)
    dv_acc[...] = jnp.zeros_like(dv_acc)
    for j, (group, out) in enumerate(zip((g0, g1, g2, g3), (dq0, dq1, dq2, dq3))):
        views = [stats[k][(j - k) % NY] for k in range(NY)]
        maxima = views[0][0:1]
        for k in range(1, NY):
            maxima = jnp.maximum(maxima, views[k][0:1])
        totals = jnp.zeros((1, ROWS), F32)
        dots = jnp.zeros((1, ROWS), F32)
        for k in range(NY):
            shrink = jnp.exp(views[k][0:1] - maxima)
            totals = totals + views[k][1:2] * shrink
            dots = dots + views[k][2:3] * shrink
        log_totals = maxima + jnp.log(totals)
        row_dots = dots / totals

        def step(p, query_grad, j=j, group=group, log_totals=log_totals, row_dots=row_dots):
            row = PAIRS * j + p
            first = item_ref[row, 0]
            second = item_ref[row, 1]
            probs = jnp.exp(score_ref[row] - log_totals)
            score_grads = (probs * (pgrad_ref[row] - row_dots)).astype(BF16)
            dk_pair = dot_nn(score_grads, head_rows(group, 0))
            dv_pair = dot_nn(probs.astype(BF16), head_rows(group, ROWS))
            dk_acc[first] += dk_pair[:BLOCK]
            dk_acc[second] += dk_pair[BLOCK:]
            dv_acc[first] += dv_pair[:BLOCK]
            dv_acc[second] += dv_pair[BLOCK:]
            cols = jnp.concatenate([cols_ref[first], cols_ref[second]], axis=1)
            return query_grad + dot_nn(cols, score_grads)

        query_grad = lax.fori_loop(0, item_ref[NY * PAIRS + j, 0], step, jnp.zeros((HEAD, ROWS), F32))
        out[...] = (query_grad * FACTOR).astype(BF16)
    for a in range(NZ):
        dkv_ref[a, :, :HEAD] = (dk_acc[a] * FACTOR).astype(BF16)
        dkv_ref[a, :, HEAD:] = dv_acc[a].astype(BF16)


def unrotate(x, cosine, sine):
    front = x[:HEAD // 2]
    back = x[HEAD // 2:]
    return jnp.concatenate([front * cosine + back * sine, back * cosine - front * sine], axis=0)


def weight_rows(place_ref, step):
    core = 1 - place_ref[3] if step < NX else place_ref[3]
    return pl.ds(pl.multiple_of((2 * ((place_ref[2] + step) & (NX - 1)) + core) * ROWS, ROWS), ROWS)


def fetch_kernel(place_ref, anc_ref, dq_ref, wq_hbm, cos_ref, sin_ref, *refs):
    blocks, sem = refs[:-1], refs[-1]
    copies = [
        pltpu.make_async_copy(wq_hbm.at[weight_rows(place_ref, i), :], block, sem.at[i])
        for i, block in enumerate(blocks)
    ]
    for copy in copies:
        copy.start()
    own_block = NY * place_ref[0] + place_ref[1]
    depth = jnp.int32(0)
    for i in range(ANC):
        depth = depth + jnp.where(anc_ref[i, own_block] != own_block, 1, 0)
    half = (HEAD // 2, BLOCK)
    pair = lax.broadcasted_iota(I32, half, 0).astype(F32)
    token_place = (lax.broadcasted_iota(I32, half, 1) + BLOCK * depth).astype(F32)
    angles = jnp.exp(pair * (-2.0 * math.log(ROPE_BASE) / HEAD)) * token_place
    cos_ref[...] = jnp.cos(angles)
    sin_ref[...] = jnp.sin(angles)
    for copy in copies:
        copy.wait()


def start_pair(place_ref, first, wk_hbm, wv_hbm, wk, wv, sem):
    copies = []
    for i in range(NX):
        rows = weight_rows(place_ref, first + i)
        copies.append(pltpu.make_async_copy(wk_hbm.at[rows, :], wk.at[i], sem.at[2 * i]))
        copies.append(pltpu.make_async_copy(wv_hbm.at[rows, :], wv.at[i], sem.at[2 * i + 1]))
    for copy in copies:
        copy.start()
    return copies


def query_part_kernel(place_ref, cos_ref, sin_ref, q0, q3, q2, q1, wk_hbm, wv_hbm, *refs):
    blocks, out_ref, wk, wv, sem = refs[:2 * NX], *refs[2 * NX:]
    copies = start_pair(place_ref, 0, wk_hbm, wv_hbm, wk, wv, sem)
    cosine = cos_ref[...]
    sine = sin_ref[...]
    low = []
    for h in range(GROUP):
        cols = slice(h * HEAD, (h + 1) * HEAD)
        total = q0[:, cols].astype(F32)
        for part in (q1, q2, q3):
            total = total + part[:, cols].astype(F32)
        low.append(unrotate(total, cosine, sine).astype(BF16))
    low = jnp.concatenate(low, axis=0)
    for i, block in enumerate(blocks):
        out_ref[i] = dot_nn(block[...], low).astype(BF16)
    for copy in copies:
        copy.wait()


def first_half_kernel(cos_ref, sin_ref, dkv_ref, part_ref, wk, wv, out_ref, low_ref):
    total = dkv_ref[0].astype(F32)
    for a in range(1, NZ):
        total = total + dkv_ref[a].astype(F32)
    low_ref[:HEAD, :] = unrotate(total[:, :HEAD].T, cos_ref[...], sin_ref[...]).astype(BF16)
    low_ref[HEAD:, :] = total[:, HEAD:].T.astype(BF16)
    for i in range(NX):
        total = part_ref[i] + key_value_part(low_ref, wk[i], wv[i])
        out_ref[i] = side_by_side(total).astype(BF16)


def second_half_kernel(place_ref, low_ref, part_ref, wk_hbm, wv_hbm, out_ref, wk, wv, sem):
    copies = start_pair(place_ref, NX, wk_hbm, wv_hbm, wk, wv, sem)
    for i in range(NX):
        for copy in copies[2 * i:2 * i + 2]:
            copy.wait()
        out_ref[i] = side_by_side(part_ref[NX + i] + key_value_part(low_ref, wk[i], wv[i]))


def key_value_part(low_ref, wk, wv):
    return dot_nn(wk, low_ref[:HEAD, :]) + dot_nn(wv, low_ref[HEAD:, :])


def finish_kernel(kept_ref, p2, p0, p1, arrived_ref, out_ref):
    for h in range(GROUP):
        cols = slice(h * HEAD, (h + 1) * HEAD)
        total = kept_ref[:, cols]
        for part in (arrived_ref, p0, p1, p2):
            total = total + part[:, cols].astype(F32)
        out_ref[:, cols] = total.T.astype(BF16)


def shift(size, k):
    return [(i, (i + k) % size) for i in range(size)]


def shards(queries, keys, values, out_grad, ancestry, w_query, key_matrix, value_matrix):
    z, y, x, c = (lax.axis_index(name) for name in "zyxc")
    place = jnp.stack([z, y, x, c]).astype(I32)
    group, kv = call(
        stack_kernel,
        [pltpu.VMEM((BLOCK, 2 * ROWS), BF16), pltpu.VMEM((BLOCK, 2 * HEAD), BF16)],
        [HB] * 4,
        [VM] * 2,
        "stack",
        [pltpu.SemaphoreType.DMA((4,))],
    )(*in_hbm(queries, out_grad, keys, values))
    groups = [group] + [lax.ppermute(group, "y", shift(NY, k)) for k in range(1, NY)]
    below, above = [kv], [kv]
    for r in range(1, NZ // 2):
        below.append(lax.ppermute(below[-1], "z", shift(NZ, 1)))
        above.append(lax.ppermute(above[-1], "z", shift(NZ, -1)))
    kvs = below + [lax.ppermute(below[-1], "z", shift(NZ, 1))] + above[:0:-1]

    items = call(
        plan_kernel,
        jax.ShapeDtypeStruct((NY * PAIRS + NY, 4), I32),
        [SM, SM, VM],
        SM,
        "plan",
        [pltpu.SMEM((NZ + 1,), I32)],
        PLAN_FLOPS,
    )(place, ancestry.T, group)

    tiles = (NY * PAIRS, 2 * BLOCK, ROWS)
    stats, scores, prob_grads = call(
        stats_kernel,
        [jax.ShapeDtypeStruct((NY, 4, ROWS), F32), pltpu.VMEM(tiles, F32), pltpu.VMEM(tiles, F32)],
        [SM] + [VM] * (NZ + NY),
        [VM] * 3,
        "stats",
        [pltpu.VMEM((NZ, BLOCK, 2 * HEAD), BF16)],
        STATS_FLOPS,
    )(items, *kvs, group, *groups[:0:-1])
    all_stats = [stats] + [lax.ppermute(stats, "y", shift(NY, k)) for k in range(1, NY)]
    key_cols = call(
        turn_kernel, pltpu.VMEM((NZ, HEAD, BLOCK), BF16), [SM] + [VM] * (NZ + 1), VM, "turn",
    )(items, *kvs, stats)
    dkv, *dq_parts = call(
        grads_kernel,
        [pltpu.VMEM((NZ, BLOCK, 2 * HEAD), BF16)] + [pltpu.VMEM((HEAD, ROWS), BF16)] * NY,
        [SM] + [VM] * (3 + 2 * NY),
        [VM] * (1 + NY),
        "grads",
        [pltpu.VMEM((NZ, BLOCK, HEAD), F32), pltpu.VMEM((NZ, BLOCK, HEAD), F32)],
        GRADS_FLOPS,
    )(items, key_cols, scores, prob_grads, *groups, all_stats[0], *all_stats[:0:-1])
    dq_own = [dq_parts[0]] + [lax.ppermute(dq_parts[k], "y", shift(NY, -k)) for k in range(1, NY)]
    dkv = call(
        flush_kernel, pltpu.HBM(dkv.shape, BF16), [VM], HB, "flush", [pltpu.SemaphoreType.DMA((1,))],
    )(dkv)
    dkv_own = lax.all_to_all(dkv, "z", 0, 0, tiled=True)

    wq, wk, wv = in_hbm(w_query, key_matrix, value_matrix)
    cosine, sine, *blocks = call(
        fetch_kernel,
        [pltpu.VMEM((HEAD // 2, BLOCK), F32)] * 2 + [pltpu.VMEM((ROWS, ROWS), BF16)] * (2 * NX),
        [SM, SM, VM, HB],
        [VM] * (2 * NX + 2),
        "fetch",
        [pltpu.SemaphoreType.DMA((2 * NX,))],
    )(place, ancestry.T, dq_parts[0], wq)
    pair_shapes = [pltpu.VMEM((NX, ROWS, HEAD), BF16)] * 2
    query_part, wk_away, wv_away = call(
        query_part_kernel,
        [pltpu.VMEM((2 * NX, ROWS, BLOCK), BF16)] + pair_shapes,
        [SM] + [VM] * (2 + NY) + [HB] * 2 + [VM] * (2 * NX),
        [VM] * 3,
        "query_part",
        [pltpu.SemaphoreType.DMA((2 * NX,))],
        QUERY_FLOPS,
    )(place, cosine, sine, dq_own[0], *dq_own[:0:-1], wk, wv, *blocks)
    away, low = call(
        first_half_kernel,
        [pltpu.VMEM((NX, BLOCK, ROWS), BF16), pltpu.VMEM((2 * HEAD, BLOCK), BF16)],
        [VM] * 6,
        [VM] * 2,
        "first_half",
    )(cosine, sine, dkv_own, query_part, wk_away, wv_away)
    arrived = lax.ppermute(away, "c", shift(NC, 1))
    kept = call(
        second_half_kernel,
        pltpu.VMEM((NX, BLOCK, ROWS), F32),
        [SM] + [VM] * 2 + [HB] * 2,
        VM,
        "second_half",
        pair_shapes + [pltpu.SemaphoreType.DMA((2 * NX,))],
    )(place, low, query_part, wk, wv)
    sent = [(kept[k] + arrived[k].astype(F32)).astype(BF16) for k in range(1, NX)]
    parts = [lax.ppermute(sent[k - 1], "x", shift(NX, k)) for k in range(1, NX)]
    return call(
        finish_kernel, jax.ShapeDtypeStruct((BLOCK, ROWS), BF16), [VM] * (2 + len(parts)), VM, "finish",
    )(kept[0], parts[2], parts[0], parts[1], arrived[0])


def solution(mesh):
    grid = Mesh(mesh.devices.reshape(NZ, NY, NX, NC), ("z", "y", "x", "c"))
    split = P(("z", "y"), ("x", "c"))
    weight = P(None, ("x", "c"))
    return jax.shard_map(
        shards,
        mesh=grid,
        in_specs=(split, split, split, split, P(), weight, weight, weight),
        out_specs=split,
        check_vma=False,
    )
```

```python
import math

import jax
import jax.numpy as jnp
from jax import lax
from jax.experimental import pallas as pl
from jax.experimental.pallas import tpu as pltpu
from jax.sharding import Mesh, PartitionSpec as P

HEAD = 128
BLOCK = 128
GROUP = 5
ROWS = GROUP * BLOCK
NZ, NY, NX, NC = 8, 4, 4, 2
PAIRS = NZ // 2
ANC = 17
ROPE_BASE = 1000000.0
MASKED = -1e30
FACTOR = HEAD ** -0.5
NT = (((1,), (1,)), ((), ()))
NN = (((1,), (0,)), ((), ()))
F32, BF16, I32 = jnp.float32, jnp.bfloat16, jnp.int32
VMEM_LIMIT = 16 << 20
PLAN_FLOPS = 1_000_000_000
STATS_FLOPS = 2 * 2 * (NY * ROWS) * (NZ * BLOCK) * HEAD
GRADS_FLOPS = 3 * 2 * (NY * ROWS) * (NZ * BLOCK) * HEAD
QUERY_FLOPS = 2 * BLOCK * ROWS * 2 * NX * ROWS

VM = pl.BlockSpec(memory_space=pltpu.VMEM)
SM = pl.BlockSpec(memory_space=pltpu.SMEM)
HB = pl.BlockSpec(memory_space=pltpu.HBM)


def dot_nt(a, b):
    return lax.dot_general(a, b, NT, preferred_element_type=F32)


def dot_nn(a, b):
    return lax.dot_general(a, b, NN, preferred_element_type=F32)


def call(body, out_shape, in_specs, out_specs, name, scratch=(), flops=0):
    return pl.pallas_call(
        body,
        out_shape=out_shape,
        in_specs=in_specs,
        out_specs=out_specs,
        scratch_shapes=list(scratch),
        compiler_params=pltpu.CompilerParams(vmem_limit_bytes=VMEM_LIMIT),
        cost_estimate=pl.CostEstimate(flops=flops, transcendentals=0, bytes_accessed=0) if flops else None,
        name=name,
    )


def in_hbm(*arrays):
    return [pltpu.with_memory_space_constraint(a, pltpu.HBM) for a in arrays]


def run_copies(pairs, sem):
    started = [pltpu.make_async_copy(src, dst, sem.at[i]) for i, (src, dst) in enumerate(pairs)]
    for copy in started:
        copy.start()
    for copy in started:
        copy.wait()


def stack_kernel(q_ref, g_ref, k_ref, v_ref, rows_ref, kv_ref, sem):
    pairs = [(k_ref, kv_ref.at[:, 0:HEAD]), (v_ref, kv_ref.at[:, HEAD:2 * HEAD])]
    pairs += [(q_ref, rows_ref.at[:, 0:ROWS]), (g_ref, rows_ref.at[:, ROWS:2 * ROWS])]
    run_copies(pairs, sem)


def head_rows(ref, first):
    return jnp.concatenate([ref[:, first + h * HEAD:first + (h + 1) * HEAD] for h in range(GROUP)], axis=0)


def side_by_side(value):
    return jnp.concatenate([value[h * HEAD:(h + 1) * HEAD, :] for h in range(GROUP)], axis=1)


def plan_kernel(place_ref, anc_ref, rows_ref, item_ref, list_ref):
    z = place_ref[0]
    y = place_ref[1]
    for j in range(NY):
        query_block = NY * z + ((y - j) & (NY - 1))
        bits = jnp.int32(0)
        for i in range(ANC):
            key_block = anc_ref[i, query_block]
            bits = bits | jnp.where((key_block & (NY - 1)) == y, jnp.int32(1) << (key_block >> 2), 0)
        count = jnp.int32(0)
        for key_z in range(NZ):
            list_ref[count] = key_z
            count = count + ((bits >> key_z) & 1)
        for p in range(PAIRS):
            row = PAIRS * j + p
            first = jnp.where(2 * p < count, list_ref[2 * p], 0)
            both = 2 * p + 1 < count
            second = jnp.where(both, list_ref[2 * p + 1], first)
            item_ref[row, 0] = first
            item_ref[row, 1] = second
            causal = jnp.int32(0) if j == 0 else jnp.int32(-BLOCK)
            item_ref[row, 2] = jnp.where(first == z, causal, -BLOCK)
            item_ref[row, 3] = jnp.where(both, jnp.where(second == z, causal, -BLOCK), BLOCK)
        item_ref[NY * PAIRS + j, 0] = (count + 1) // 2
        item_ref[NY * PAIRS + j, 1] = z


def stats_kernel(item_ref, k0, k1, k2, k3, k4, k5, k6, k7, g0, g1, g2, g3, stat_ref, score_ref, pgrad_ref, kv_ref):
    z = item_ref[NY * PAIRS, 1]
    for r, part in enumerate((k0, k1, k2, k3, k4, k5, k6, k7)):
        kv_ref[(z - r) & (NZ - 1)] = part[...]
    key_row = lax.broadcasted_iota(I32, (BLOCK, ROWS), 0)
    query_row = lax.broadcasted_iota(I32, (BLOCK, ROWS), 1) % BLOCK
    gap = query_row - key_row
    for j, group in enumerate((g0, g1, g2, g3)):

        def step(p, carry, j=j, group=group):
            old, totals, dots = carry
            row = PAIRS * j + p
            first = item_ref[row, 0]
            second = item_ref[row, 1]
            kv = jnp.concatenate([kv_ref[first], kv_ref[second]], axis=0)
            scores = dot_nt(kv[:, :HEAD], head_rows(group, 0)) * FACTOR
            prob_grads = dot_nt(kv[:, HEAD:], head_rows(group, ROWS))
            upper = jnp.where(gap >= item_ref[row, 2], scores[:BLOCK], MASKED)
            lower = jnp.where(gap >= item_ref[row, 3], scores[BLOCK:], MASKED)
            scores = jnp.concatenate([upper, lower], axis=0)
            score_ref[row] = scores
            pgrad_ref[row] = prob_grads
            highest = jnp.maximum(old, jnp.max(scores, axis=0, keepdims=True))
            weights = jnp.exp(scores - highest)
            shrink = jnp.exp(old - highest)
            totals = totals * shrink + jnp.sum(weights, axis=0, keepdims=True)
            dots = dots * shrink + jnp.sum(weights * prob_grads, axis=0, keepdims=True)
            return highest, totals, dots

        zero = jnp.zeros((1, ROWS), F32)
        start = (jnp.full((1, ROWS), MASKED, F32), zero, zero)
        highest, totals, dots = lax.fori_loop(0, item_ref[NY * PAIRS + j, 0], step, start)
        stat_ref[j, 0:1, :] = highest
        stat_ref[j, 1:2, :] = totals
        stat_ref[j, 2:3, :] = dots
        stat_ref[j, 3:4, :] = zero


def turn_kernel(item_ref, k0, k1, k2, k3, k4, k5, k6, k7, stat_ref, key_cols):
    z = item_ref[NY * PAIRS, 1]
    for r, part in enumerate((k0, k1, k2, k3, k4, k5, k6, k7)):
        key_cols[(z - r) & (NZ - 1)] = part[:, :HEAD].T


def flush_kernel(low_ref, out_ref, sem):
    run_copies([(low_ref, out_ref)], sem)


def grads_kernel(item_ref, cols_ref, score_ref, pgrad_ref, g0, g1, g2, g3, s0, s3, s2, s1,
                 dkv_ref, dq0, dq1, dq2, dq3, dk_acc, dv_acc):
    stats = (s0, s1, s2, s3)
    dk_acc[...] = jnp.zeros_like(dk_acc)
    dv_acc[...] = jnp.zeros_like(dv_acc)
    for j, (group, out) in enumerate(zip((g0, g1, g2, g3), (dq0, dq1, dq2, dq3))):
        views = [stats[k][(j - k) % NY] for k in range(NY)]
        maxima = views[0][0:1]
        for k in range(1, NY):
            maxima = jnp.maximum(maxima, views[k][0:1])
        totals = jnp.zeros((1, ROWS), F32)
        dots = jnp.zeros((1, ROWS), F32)
        for k in range(NY):
            shrink = jnp.exp(views[k][0:1] - maxima)
            totals = totals + views[k][1:2] * shrink
            dots = dots + views[k][2:3] * shrink
        log_totals = maxima + jnp.log(totals)
        row_dots = dots / totals

        def step(p, query_grad, j=j, group=group, log_totals=log_totals, row_dots=row_dots):
            row = PAIRS * j + p
            first = item_ref[row, 0]
            second = item_ref[row, 1]
            probs = jnp.exp(score_ref[row] - log_totals)
            score_grads = (probs * (pgrad_ref[row] - row_dots)).astype(BF16)
            dk_pair = dot_nn(score_grads, head_rows(group, 0))
            dv_pair = dot_nn(probs.astype(BF16), head_rows(group, ROWS))
            dk_acc[first] += dk_pair[:BLOCK]
            dk_acc[second] += dk_pair[BLOCK:]
            dv_acc[first] += dv_pair[:BLOCK]
            dv_acc[second] += dv_pair[BLOCK:]
            cols = jnp.concatenate([cols_ref[first], cols_ref[second]], axis=1)
            return query_grad + dot_nn(cols, score_grads)

        query_grad = lax.fori_loop(0, item_ref[NY * PAIRS + j, 0], step, jnp.zeros((HEAD, ROWS), F32))
        out[...] = (query_grad * FACTOR).astype(BF16)
    for a in range(NZ):
        dkv_ref[a, :, :HEAD] = (dk_acc[a] * FACTOR).astype(BF16)
        dkv_ref[a, :, HEAD:] = dv_acc[a].astype(BF16)


def unrotate(x, cosine, sine):
    front = x[:HEAD // 2]
    back = x[HEAD // 2:]
    return jnp.concatenate([front * cosine + back * sine, back * cosine - front * sine], axis=0)


def weight_rows(place_ref, step):
    core = 1 - place_ref[3] if step < NX else place_ref[3]
    return pl.ds(pl.multiple_of((2 * ((place_ref[2] + step) & (NX - 1)) + core) * ROWS, ROWS), ROWS)


def fetch_kernel(place_ref, anc_ref, dq_ref, wq_hbm, cos_ref, sin_ref, *refs):
    blocks, sem = refs[:-1], refs[-1]
    copies = [
        pltpu.make_async_copy(wq_hbm.at[weight_rows(place_ref, i), :], block, sem.at[i])
        for i, block in enumerate(blocks)
    ]
    for copy in copies:
        copy.start()
    own_block = NY * place_ref[0] + place_ref[1]
    depth = jnp.int32(0)
    for i in range(ANC):
        depth = depth + jnp.where(anc_ref[i, own_block] != own_block, 1, 0)
    half = (HEAD // 2, BLOCK)
    pair = lax.broadcasted_iota(I32, half, 0).astype(F32)
    token_place = (lax.broadcasted_iota(I32, half, 1) + BLOCK * depth).astype(F32)
    angles = jnp.exp(pair * (-2.0 * math.log(ROPE_BASE) / HEAD)) * token_place
    cos_ref[...] = jnp.cos(angles)
    sin_ref[...] = jnp.sin(angles)
    for copy in copies:
        copy.wait()


def start_pair(place_ref, first, wk_hbm, wv_hbm, wk, wv, sem):
    copies = []
    for i in range(NX):
        rows = weight_rows(place_ref, first + i)
        copies.append(pltpu.make_async_copy(wk_hbm.at[rows, :], wk.at[i], sem.at[2 * i]))
        copies.append(pltpu.make_async_copy(wv_hbm.at[rows, :], wv.at[i], sem.at[2 * i + 1]))
    for copy in copies:
        copy.start()
    return copies


def query_part_kernel(place_ref, cos_ref, sin_ref, q0, q3, q2, q1, wk_hbm, wv_hbm, *refs):
    blocks, out_ref, wk, wv, sem = refs[:2 * NX], *refs[2 * NX:]
    copies = start_pair(place_ref, 0, wk_hbm, wv_hbm, wk, wv, sem)
    cosine = cos_ref[...]
    sine = sin_ref[...]
    low = []
    for h in range(GROUP):
        cols = slice(h * HEAD, (h + 1) * HEAD)
        total = q0[:, cols].astype(F32)
        for part in (q1, q2, q3):
            total = total + part[:, cols].astype(F32)
        low.append(unrotate(total, cosine, sine).astype(BF16))
    low = jnp.concatenate(low, axis=0)
    for i, block in enumerate(blocks):
        out_ref[i] = dot_nn(block[...], low).astype(BF16)
    for copy in copies:
        copy.wait()


def first_half_kernel(cos_ref, sin_ref, dkv_ref, part_ref, wk, wv, out_ref, low_ref):
    total = dkv_ref[0].astype(F32)
    for a in range(1, NZ):
        total = total + dkv_ref[a].astype(F32)
    low_ref[:HEAD, :] = unrotate(total[:, :HEAD].T, cos_ref[...], sin_ref[...]).astype(BF16)
    low_ref[HEAD:, :] = total[:, HEAD:].T.astype(BF16)
    for i in range(NX):
        total = part_ref[i] + key_value_part(low_ref, wk[i], wv[i])
        out_ref[i] = side_by_side(total).astype(BF16)


def second_half_kernel(place_ref, low_ref, part_ref, wk_hbm, wv_hbm, out_ref, wk, wv, sem):
    copies = start_pair(place_ref, NX, wk_hbm, wv_hbm, wk, wv, sem)
    for i in range(NX):
        for copy in copies[2 * i:2 * i + 2]:
            copy.wait()
        out_ref[i] = side_by_side(part_ref[NX + i] + key_value_part(low_ref, wk[i], wv[i]))


def key_value_part(low_ref, wk, wv):
    return dot_nn(wk, low_ref[:HEAD, :]) + dot_nn(wv, low_ref[HEAD:, :])


def finish_kernel(kept_ref, p2, p0, p1, arrived_ref, out_ref):
    for h in range(GROUP):
        cols = slice(h * HEAD, (h + 1) * HEAD)
        total = kept_ref[:, cols]
        for part in (arrived_ref, p0, p1, p2):
            total = total + part[:, cols].astype(F32)
        out_ref[:, cols] = total.T.astype(BF16)


def shift(size, k):
    return [(i, (i + k) % size) for i in range(size)]


def shards(queries, keys, values, out_grad, ancestry, w_query, key_matrix, value_matrix):
    z, y, x, c = (lax.axis_index(name) for name in "zyxc")
    place = jnp.stack([z, y, x, c]).astype(I32)
    group, kv = call(
        stack_kernel,
        [pltpu.VMEM((BLOCK, 2 * ROWS), BF16), pltpu.VMEM((BLOCK, 2 * HEAD), BF16)],
        [HB] * 4,
        [VM] * 2,
        "stack",
        [pltpu.SemaphoreType.DMA((4,))],
    )(*in_hbm(queries, out_grad, keys, values))
    groups = [group] + [lax.ppermute(group, "y", shift(NY, k)) for k in range(1, NY)]
    below, above = [kv], [kv]
    for r in range(1, NZ // 2):
        below.append(lax.ppermute(below[-1], "z", shift(NZ, 1)))
        above.append(lax.ppermute(above[-1], "z", shift(NZ, -1)))
    kvs = below + [lax.ppermute(below[-1], "z", shift(NZ, 1))] + above[:0:-1]

    items = call(
        plan_kernel,
        jax.ShapeDtypeStruct((NY * PAIRS + NY, 4), I32),
        [SM, SM, VM],
        SM,
        "plan",
        [pltpu.SMEM((NZ + 1,), I32)],
        PLAN_FLOPS,
    )(place, ancestry.T, group)

    tiles = (NY * PAIRS, 2 * BLOCK, ROWS)
    stats, scores, prob_grads = call(
        stats_kernel,
        [jax.ShapeDtypeStruct((NY, 4, ROWS), F32), pltpu.VMEM(tiles, F32), pltpu.VMEM(tiles, F32)],
        [SM] + [VM] * (NZ + NY),
        [VM] * 3,
        "stats",
        [pltpu.VMEM((NZ, BLOCK, 2 * HEAD), BF16)],
        STATS_FLOPS,
    )(items, *kvs, *groups)
    all_stats = [stats] + [lax.ppermute(stats, "y", shift(NY, k)) for k in range(1, NY)]
    key_cols = call(
        turn_kernel, pltpu.VMEM((NZ, HEAD, BLOCK), BF16), [SM] + [VM] * (NZ + 1), VM, "turn",
    )(items, *kvs, stats)
    dkv, *dq_parts = call(
        grads_kernel,
        [pltpu.VMEM((NZ, BLOCK, 2 * HEAD), BF16)] + [pltpu.VMEM((HEAD, ROWS), BF16)] * NY,
        [SM] + [VM] * (3 + 2 * NY),
        [VM] * (1 + NY),
        "grads",
        [pltpu.VMEM((NZ, BLOCK, HEAD), F32), pltpu.VMEM((NZ, BLOCK, HEAD), F32)],
        GRADS_FLOPS,
    )(items, key_cols, scores, prob_grads, *groups, all_stats[0], *all_stats[:0:-1])
    dq_own = [dq_parts[0]] + [lax.ppermute(dq_parts[k], "y", shift(NY, -k)) for k in range(1, NY)]
    dkv = call(
        flush_kernel, pltpu.HBM(dkv.shape, BF16), [VM], HB, "flush", [pltpu.SemaphoreType.DMA((1,))],
    )(dkv)
    dkv_own = lax.all_to_all(dkv, "z", 0, 0, tiled=True)

    wq, wk, wv = in_hbm(w_query, key_matrix, value_matrix)
    cosine, sine, *blocks = call(
        fetch_kernel,
        [pltpu.VMEM((HEAD // 2, BLOCK), F32)] * 2 + [pltpu.VMEM((ROWS, ROWS), BF16)] * (2 * NX),
        [SM, SM, VM, HB],
        [VM] * (2 * NX + 2),
        "fetch",
        [pltpu.SemaphoreType.DMA((2 * NX,))],
    )(place, ancestry.T, dq_parts[0], wq)
    pair_shapes = [pltpu.VMEM((NX, ROWS, HEAD), BF16)] * 2
    query_part, wk_away, wv_away = call(
        query_part_kernel,
        [pltpu.VMEM((2 * NX, ROWS, BLOCK), BF16)] + pair_shapes,
        [SM] + [VM] * (2 + NY) + [HB] * 2 + [VM] * (2 * NX),
        [VM] * 3,
        "query_part",
        [pltpu.SemaphoreType.DMA((2 * NX,))],
        QUERY_FLOPS,
    )(place, cosine, sine, dq_own[0], *dq_own[:0:-1], wk, wv, *blocks)
    away, low = call(
        first_half_kernel,
        [pltpu.VMEM((NX, BLOCK, ROWS), BF16), pltpu.VMEM((2 * HEAD, BLOCK), BF16)],
        [VM] * 6,
        [VM] * 2,
        "first_half",
    )(cosine, sine, dkv_own, query_part, wk_away, wv_away)
    arrived = lax.ppermute(away, "c", shift(NC, 1))
    kept = call(
        second_half_kernel,
        pltpu.VMEM((NX, BLOCK, ROWS), F32),
        [SM] + [VM] * 2 + [HB] * 2,
        VM,
        "second_half",
        pair_shapes + [pltpu.SemaphoreType.DMA((2 * NX,))],
    )(place, low, query_part, wk, wv)
    sent = [(kept[k] + arrived[k].astype(F32)).astype(BF16) for k in range(1, NX)]
    parts = [lax.ppermute(sent[k - 1], "x", shift(NX, k)) for k in range(1, NX)]
    return call(
        finish_kernel, jax.ShapeDtypeStruct((BLOCK, ROWS), BF16), [VM] * (2 + len(parts)), VM, "finish",
    )(kept[0], parts[2], parts[0], parts[1], arrived[0])


def solution(mesh):
    grid = Mesh(mesh.devices.reshape(NZ, NY, NX, NC), ("z", "y", "x", "c"))
    split = P(("z", "y"), ("x", "c"))
    weight = P(None, ("x", "c"))
    return jax.shard_map(
        shards,
        mesh=grid,
        in_specs=(split, split, split, split, P(), weight, weight, weight),
        out_specs=split,
        check_vma=False,
    )
```
